32 devices in a mesh: groups: 2 (over x), frame: 16 (over z, y, core).
Axes of the slice: x: 2, y: 2, z: 4, core: 2. Of those that a mesh axis runs over, the one named last changes fastest.
Arguments:
- latent: bfloat16 [2048, 1536], P(('groups', 'frame')), parts along dimension 0, may hold values from -6 to 6
- norm_gain: float32 [1536], replicated, may hold values from 0.25 to 1.75
- w_query: bfloat16 [1536, 1536], P('frame'), may hold values from -0.3125 to 0.3125
- w_key: bfloat16 [1536, 1536], P('frame'), may hold values from -0.15625 to 0.15625
- w_value: bfloat16 [1536, 1536], P('frame'), may hold values from -0.625 to 0.625
- mem_cache: bfloat16 [256, 16, 2, 1536], P('groups', 'frame'), parts along dimension 0, may hold values from -60 to 60
- intersection: int32 [8, 8], P('groups'), parts along dimension 0, may hold values from 0 to 127, as said below
- counts: int32 [8], P('groups'), parts along dimension 0, may hold values from 1 to 8, as said below
- slot_of: int32 [256], P('groups'), parts along dimension 0, may hold values from 0 to 127, each once
- step_scale: float32 [2], replicated, may hold values from 0.5 to 1.5
Outputs:
- denoised: bfloat16 [2048, 1536], P(('groups', 'frame')), parts along dimension 0
The draws below stay inside these ranges and needn't reach their ends.
There are 2 independent parts, one for each index of `groups`. The reference program is written for one: setup_inputs(seed, part) draws one part's arguments, and reference() takes and returns one part's arrays. A program takes and returns all parts, laid end to end along the dimension named above; an argument that names none is the same for every part. Nothing has to cross between parts.
Inputs may be any that keep to these rules, and one draw needn't show every extreme that they name: `intersection`: each row names 8 different memory frames. `counts`: some frame has all 8 entries live.
All inputs are finite; a program needn't handle non-finite values.
Results may differ from the reference program's by a relative error of at most 0.025.
The reference program's roundings to bfloat16 on the way count: a program that leaves them out, or rounds other values in their place, can miss the bound.
Values may be sent and summed in bfloat16 or wider, within the bound.
No kernel may reach another device: no remote copies, remote signals or barrier semaphores. Data moves between devices by JAX's collectives and lax.ppermute only.
A program may use at most 128 MiB of HBM per device.

```python
import math
import jax
import jax.numpy as jnp
from jax import lax

D = 1536
HEADS = 12
HS = 128
MEM = 128
LIST = 8
STEPS = 2
FRAMES = 4
TPF = 256
TOKENS = 1024
MT = 16


def draw_mem_cache(key, part):
    first_key = jax.random.fold_in(key, 0)
    return jnp.clip(jax.random.normal(first_key, (MEM, MT, 2, D), jnp.float32), -6.0, 6.0).astype(jnp.bfloat16)


def draw_intersection(key, part):
    frame_keys = jax.random.split(key, FRAMES)
    picked = jax.vmap(lambda frame_key: jax.random.permutation(frame_key, MEM)[:LIST])(frame_keys)
    return picked.astype(jnp.int32)


def draw_counts(key, part):
    first_key, second_key = jax.random.split(key)
    base = jax.random.randint(first_key, (FRAMES,), 1, LIST + 1)
    filled = jax.random.randint(second_key, (), 0, FRAMES)
    return jnp.where(jnp.arange(FRAMES) == filled, LIST, base).astype(jnp.int32)


def block_scale(stream_key, shape, cuts, least, high):
    gain = 1.0
    for dim, parts in cuts:
        draws = jax.random.uniform(jax.random.fold_in(jax.random.fold_in(stream_key, 6), dim), (parts,), jnp.float32, least / len(cuts), high / len(cuts))
        gain = gain * jnp.repeat(jnp.exp(draws), shape[dim] // parts).reshape((-1,) + (1,) * (len(shape) - 1 - dim))
    return gain


def normal_values(key, dims, scale, reach, cuts=(), kind=jnp.bfloat16):
    factor_of = block_scale(key, dims, cuts, -0.22, 0.18) if cuts else 1.0
    array = jax.random.normal(key, dims, jnp.float32) * scale * factor_of
    return jnp.minimum(jnp.maximum(array, -reach), reach).astype(kind)


def setup_inputs(seed: int = 0, part: int = 0) -> dict:
    streams_of = jax.random.split(jax.random.key(seed), 11)
    part_splits = jax.random.split(jax.random.fold_in(streams_of[10], part), 11)
    latent = normal_values(part_splits[0], (TOKENS, D), 1.0, 6.0, ((0, 16),))
    norm_gain = jnp.clip(1.0 + 0.15 * jax.random.normal(streams_of[1], (D,), jnp.float32), 0.25, 1.75)
    w_query = normal_values(streams_of[2], (D, D), (D // 4) ** -0.5, 0.3125, ((0, 16),))
    w_key = normal_values(streams_of[3], (D, D), D ** -0.5, 0.15625, ((0, 16),))
    w_value = normal_values(streams_of[4], (D, D), (D // 16) ** -0.5, 0.625, ((0, 16),))
    mem_cache = draw_mem_cache(jax.random.fold_in(jax.random.fold_in(streams_of[10], part), 71), part)
    intersection = draw_intersection(jax.random.fold_in(jax.random.fold_in(streams_of[10], part), 71), part)
    counts = draw_counts(jax.random.fold_in(jax.random.fold_in(streams_of[10], part), 71), part)
    slot_of = jax.random.permutation(part_splits[8], MEM).astype(jnp.int32)
    step_scale = jnp.clip(jnp.exp(jax.random.uniform(streams_of[9], (STEPS,), jnp.float32, math.log(0.5), math.log(1.5))), 0.5, 1.5)
    return dict(latent=latent, norm_gain=norm_gain, w_query=w_query, w_key=w_key, w_value=w_value, mem_cache=mem_cache, intersection=intersection, counts=counts, slot_of=slot_of, step_scale=step_scale)


def project(normed, weight):
    return jnp.dot(normed, weight, preferred_element_type=jnp.float32).astype(jnp.bfloat16)

def reference(latent, norm_gain, w_query, w_key, w_value, mem_cache, intersection, counts, slot_of, step_scale):
    current = latent
    scale_dot = 1.0 / math.sqrt(HS)
    for step_index in range(STEPS):
        widened = current.astype(jnp.float32)
        inverse = lax.rsqrt(lax.optimization_barrier(jnp.mean(widened * widened, axis=-1, keepdims=True)) + 1e-06)
        normed = (widened * inverse * norm_gain).astype(jnp.bfloat16)
        queries = project(normed, w_query)
        keys_all = project(normed, w_key)
        values_all = project(normed, w_value)

        def one_frame(frame_index):
            start = (frame_index * TPF).astype(jnp.int32)
            q_rows = lax.dynamic_slice_in_dim(queries, start, TPF, 0).reshape(TPF, HEADS, HS).astype(jnp.float32)
            k_rows = lax.dynamic_slice_in_dim(keys_all, start, TPF, 0).reshape(TPF, HEADS, HS)
            v_rows = lax.dynamic_slice_in_dim(values_all, start, TPF, 0).reshape(TPF, HEADS, HS)
            memory = mem_cache[slot_of[intersection[frame_index]]]
            mem_keys = memory[:, :, 0, :].reshape(LIST * MT, HEADS, HS)
            mem_values = memory[:, :, 1, :].reshape(LIST * MT, HEADS, HS)
            joined_keys = jnp.concatenate([k_rows, mem_keys], axis=0).astype(jnp.float32)
            joined_values = jnp.concatenate([v_rows, mem_values], axis=0).astype(jnp.float32)
            live_keys = jnp.concatenate([jnp.ones((TPF,), dtype=bool), jnp.arange(LIST * MT, dtype=jnp.int32) // MT < counts[frame_index]])
            scores = jnp.einsum('thd,khd->htk', q_rows, joined_keys) * scale_dot
            scores = jnp.where(live_keys[None, None, :], scores, -1e+30)
            largest = lax.optimization_barrier(jnp.max(scores, axis=-1, keepdims=True))
            weights = jnp.exp(scores - largest)
            denominator = lax.optimization_barrier(jnp.sum(weights, axis=-1))
            rounded = lax.optimization_barrier(weights.astype(jnp.bfloat16)).astype(jnp.float32)
            blended = jnp.einsum('htk,khd->thd', rounded, joined_values)
            blended = blended / jnp.transpose(denominator)[:, :, None]
            return blended.reshape(TPF, D).astype(jnp.bfloat16)
        attended = lax.map(one_frame, jnp.arange(FRAMES, dtype=jnp.int32)).reshape(FRAMES * TPF, D)
        current = (widened + step_scale[step_index] * attended.astype(jnp.float32)).astype(jnp.bfloat16)
    return current
```

```python
import functools
import math

import jax
import jax.numpy as jnp
from jax import lax
from jax.experimental import pallas as pl
from jax.experimental.pallas import tpu as pltpu
from jax.sharding import PartitionSpec as P

HEADS = 12
HS = 128
SPATIAL = 4
STEPS = 2
AXES = ("groups", "frame")
VMEM_LIMIT = 48 * 1024 * 1024


def coords(index):
    return index // 4, (index // 2) % 2, index % 2


def quarter_of(plane, y):
    return (plane % 2) * 2 + y


def moved(array, target):
    devices = lax.axis_size("frame")
    pairs = []
    for x in range(lax.axis_size("groups")):
        for index in range(devices):
            place = target(x, *coords(index))
            if place is not None:
                to_x, to_plane, to_y, to_c = place
                pairs.append((x * devices + index, to_x * devices + to_plane * 4 + to_y * 2 + to_c))
    return lax.ppermute(array, AXES, pairs)


def here():
    x = lax.axis_index("groups")
    index = lax.axis_index("frame")
    plane = index // 4
    rest = index - plane * 4
    y = rest // 2
    return x, index, plane, y, rest - y * 2


def flipped(value, bits):
    out = value
    bit = 1
    while bit <= bits:
        if bits & bit:
            out = out + bit - 2 * bit * ((value // bit) % 2)
        bit *= 2
    return out


def columns(quarter, width):
    return pl.ds(pl.multiple_of(quarter * width, 128), width)


def pack_kernel(
    list_ref, slot_ref, w_query, w_key, w_value, mem_ref,
    own_ref, beside_ref, even_ref, odd_ref, kept_ref, sent_ref,
    rows, stored, row_sem, mem_sem, out_sem, give_sem,
):
    x, index, plane, y, c = here()
    devices = lax.axis_size("frame")
    frames, entries = list_ref.shape
    width = own_ref.shape[2]
    reads = []
    for number, weight in enumerate((w_query, w_key, w_value)):
        reads.append(pltpu.make_async_copy(weight, rows.at[number], row_sem.at[number]))
        reads[-1].start()
    picks = []
    for frame in range(frames):
        for entry in range(entries):
            number = frame * entries + entry
            row = slot_ref[list_ref[frame, entry]]
            picks.append(pltpu.make_async_copy(mem_ref.at[row, 0], stored.at[number], mem_sem.at[number]))
            picks[-1].start()
    across = y + x - 2 * x * y
    low = plane % 2
    quarters = (quarter_of(plane, y), low * 2 + 1 - y, low * 2 + across, (1 - low) * 2 + across)
    for read in reads:
        read.wait()
    gives = []
    for number, (quarter, out) in enumerate(zip(quarters, (own_ref, beside_ref, even_ref, odd_ref))):
        gives.append(pltpu.make_async_copy(rows.at[:, :, columns(quarter, width)], out, out_sem.at[number]))
        gives[-1].start()
    for pick in picks:
        pick.wait()
    bits = devices.bit_length() - 1
    for away in range(devices):
        target = flipped(index, away)
        to_plane = target // 4
        to_y = (target - to_plane * 4) // 2
        to_frame = (to_plane // 2) * 2 + target % 2
        place = 0
        for bit in range(1, bits):
            place = place * 2 + (away >> bit & 1)
        out = sent_ref if away & 1 else kept_ref
        gives.append(
            pltpu.make_async_copy(
                stored.at[pl.ds(to_frame * entries, entries), :, columns(quarter_of(to_plane, to_y), width)],
                out.at[place],
                give_sem.at[away],
            )
        )
        gives[-1].start()
    for give in gives:
        give.wait()


def pack(w_query, w_key, w_value, mem_cache, intersection, slot_of):
    devices = lax.axis_size("frame")
    shard_rows, features = w_query.shape
    width = features // SPATIAL
    frames, entries = intersection.shape
    piece = jax.ShapeDtypeStruct((3, shard_rows, width), w_query.dtype)
    half = jax.ShapeDtypeStruct((devices // 2, entries, 2, width), mem_cache.dtype)
    anywhere = pl.BlockSpec(memory_space=pl.ANY)
    scalars = pl.BlockSpec(memory_space=pltpu.SMEM)
    return pl.pallas_call(
        pack_kernel,
        out_shape=(piece,) * 4 + (half,) * 2,
        in_specs=[scalars, scalars] + [anywhere] * 4,
        out_specs=(anywhere,) * 6,
        scratch_shapes=[
            pltpu.VMEM((3, shard_rows, features), w_query.dtype),
            pltpu.VMEM((frames * entries, 2, features), mem_cache.dtype),
            pltpu.SemaphoreType.DMA((3,)),
            pltpu.SemaphoreType.DMA((frames * entries,)),
            pltpu.SemaphoreType.DMA((4,)),
            pltpu.SemaphoreType.DMA((devices,)),
        ],
        compiler_params=pltpu.CompilerParams(vmem_limit_bytes=VMEM_LIMIT),
        name="pack",
    )(intersection, slot_of, w_query, w_key, w_value, mem_cache)


def all_pieces(own, beside, even, odd):
    planes = lax.axis_size("frame") // 4
    found = []
    for bits in sorted(range(1, planes), key=lambda value: (-value.bit_length(), value)):
        direct = moved(even if bits % 2 == 0 else odd, lambda x, p, y, c, bits=bits: (x, p ^ bits, y ^ x, c))
        found.append((direct, (bits, 0, True)))
    near = moved(beside, lambda x, p, y, c: (x, p, 1 - y, c))
    pieces = [(own, (0, 0, False)), (near, (0, 1, False))]
    for direct, (bits, _, _) in found:
        pieces.append((direct, (bits, 0, True)))
        pieces.append((moved(direct, lambda x, p, y, c: (1 - x, p, y, c)), (bits, 1, True)))
    places = [(array, place + (0,)) for array, place in pieces]
    places += [(moved(array, lambda x, p, y, c: (x, p, y, 1 - c)), place + (1,)) for array, place in pieces]
    return places


def all_memory(kept, sent):
    devices = lax.axis_size("frame")
    held = jnp.stack([kept, hop(sent, 0)])
    for bit in range(1, devices.bit_length() - 1):
        half = held.shape[1] // 2
        held = jnp.concatenate([held[:, :half], hop(held[:, half:], bit)])
    keys, values = held[:, 0, :, 0, :], held[:, 0, :, 1, :]
    return keys.reshape(-1, keys.shape[-1]), values.reshape(-1, values.shape[-1])


def hop(array, bit):
    return lax.ppermute(array, "frame", [(i, i ^ 1 << bit) for i in range(lax.axis_size("frame"))])


def all_tokens(latent):
    other = moved(latent, lambda x, p, y, c: (x, p, y, 1 - c) if c != p % 2 else None)
    block = jnp.concatenate([latent, other])
    near = moved(block, lambda x, p, y, c: (x, p, 1 - y, c) if c == p % 2 else None)
    far = moved(block, lambda x, p, y, c: (x, p ^ 1, y, c) if c == p % 2 else None)
    far_near = moved(far, lambda x, p, y, c: (x, p, 1 - y, c) if c != p % 2 else None)
    return block, near, far, far_near


def step_kernel(places, updates, last, head_count, *refs):
    refs = list(refs)
    count_ref, scale_ref, gain_ref, key_ref, value_ref = refs[:5]
    token_refs = refs[5:9]
    piece_refs = refs[9 : 9 + len(places)]
    update_refs = refs[9 + len(places) : 9 + len(places) + len(updates)]
    outs = refs[9 + len(places) + len(updates) : -8]
    current, normed, weights, parts, attended, token_sem, piece_sem, update_sem = refs[-8:]
    x, _, plane, y, c = here()
    low = plane % 2
    chip_rows = token_refs[0].shape[0]
    width = parts.shape[2]
    at_home = low == c

    def token_copies(first, second):
        return (
            pltpu.make_async_copy(first, current.at[pl.ds(y * chip_rows, chip_rows)], token_sem.at[0]),
            pltpu.make_async_copy(second, current.at[pl.ds((1 - y) * chip_rows, chip_rows)], token_sem.at[1]),
        )

    @pl.when(at_home)
    def _():
        for copy in token_copies(token_refs[0], token_refs[1]):
            copy.start()

    @pl.when(jnp.logical_not(at_home))
    def _():
        for copy in token_copies(token_refs[2], token_refs[3]):
            copy.start()

    update_copies = []
    for number, (ref, _) in enumerate(zip(update_refs, updates)):
        update_copies.append(pltpu.make_async_copy(ref, parts.at[number], update_sem.at[number]))
        update_copies[-1].start()
    piece_copies = []
    shard_rows = piece_refs[0].shape[1]
    for number, (ref, (plane_bits, y_bits, with_x, c_bits)) in enumerate(zip(piece_refs, places)):
        from_y = flipped(y, y_bits)
        if with_x:
            from_y = from_y + x - 2 * x * from_y
        shard = flipped(plane, plane_bits) * 4 + from_y * 2 + flipped(c, c_bits)
        start = pl.multiple_of(shard * shard_rows, 16)
        piece_copies.append(
            pltpu.make_async_copy(ref, weights.at[:, pl.ds(start, shard_rows), :], piece_sem.at[number])
        )
        piece_copies[-1].start()
    for copy in token_copies(token_refs[0], token_refs[1]):
        copy.wait()
    for copy in update_copies:
        copy.wait()
    for number, (plane_bits, y_bits) in enumerate(updates):
        quarter = quarter_of(flipped(plane, plane_bits), flipped(y, y_bits))
        spot = columns(quarter, width)
        current[:, spot] = (
            current[:, spot].astype(jnp.float32) + scale_ref[0] * parts[number].astype(jnp.float32)
        ).astype(current.dtype)
    widened = current[...].astype(jnp.float32)
    inverse = lax.rsqrt(jnp.mean(widened * widened, axis=-1, keepdims=True) + 1e-06)
    normed[...] = (widened * inverse * gain_ref[...]).astype(normed.dtype)
    for copy in piece_copies:
        copy.wait()
    queries, keys, values = (
        jnp.dot(normed[...], weights[number], preferred_element_type=jnp.float32).astype(jnp.bfloat16)
        for number in range(3)
    )
    frame = (plane // 2) * 2 + c
    entries = key_ref.shape[0] // lax.axis_size("frame")
    head_size = width // head_count
    scale_dot = 1.0 / math.sqrt(head_size)
    entry = lax.broadcasted_iota(jnp.int32, (1, key_ref.shape[0]), 1) % entries
    live = entry < count_ref[frame]
    contract_last = (((1,), (1,)), ((), ()))
    for head in range(head_count):
        span = slice(head * head_size, (head + 1) * head_size)
        frame_scores = (
            lax.dot_general(queries[:, span], keys[:, span], contract_last, preferred_element_type=jnp.float32)
            * scale_dot
        )
        mem_scores = (
            lax.dot_general(queries[:, span], key_ref[:, span], contract_last, preferred_element_type=jnp.float32)
            * scale_dot
        )
        mem_scores = jnp.where(live, mem_scores, -1e30)
        largest = jnp.maximum(
            jnp.max(frame_scores, axis=-1, keepdims=True), jnp.max(mem_scores, axis=-1, keepdims=True)
        )
        frame_weights = jnp.exp(frame_scores - largest)
        mem_weights = jnp.exp(mem_scores - largest)
        denominator = jnp.sum(frame_weights, axis=-1, keepdims=True) + jnp.sum(mem_weights, axis=-1, keepdims=True)
        blended = jnp.dot(
            frame_weights.astype(jnp.bfloat16), values[:, span], preferred_element_type=jnp.float32
        ) + jnp.dot(mem_weights.astype(jnp.bfloat16), value_ref[:, span], preferred_element_type=jnp.float32)
        attended[:, span] = (blended / denominator).astype(attended.dtype)
    if not last:
        outs[0][...] = attended[...]
        return
    spot = columns(quarter_of(plane, y), width)
    attended[...] = (
        current[:, spot].astype(jnp.float32) + scale_ref[1] * attended[...].astype(jnp.float32)
    ).astype(attended.dtype)
    rows = chip_rows // 2
    here_rows, there_rows = y * chip_rows, (1 - y) * chip_rows

    def part(start):
        return attended[pl.ds(pl.multiple_of(start, rows), rows), :]

    keep, first, second, third, fourth = outs
    keep[...] = part(here_rows)
    fourth[...] = part(there_rows + rows)

    @pl.when(at_home)
    def _():
        first[...] = part(there_rows)
        second[...] = part(there_rows + rows)
        third[...] = part(here_rows + rows)

    @pl.when(jnp.logical_not(at_home))
    def _():
        first[...] = part(here_rows + rows)
        second[...] = part(here_rows)
        third[...] = part(there_rows)


def step(pieces, updates, last, counts, scales, norm_gain, keys, values, tokens):
    shard_rows, width = pieces[0][0].shape[1:]
    features = norm_gain.shape[0]
    chip_rows = tokens[0].shape[0]
    frame_rows = 2 * chip_rows
    dtype = tokens[0].dtype
    head_count = HEADS // SPATIAL
    kernel = functools.partial(
        step_kernel, tuple(place for _, place in pieces), tuple(bits for _, bits in updates), last, head_count
    )
    if last:
        out_shape = tuple(jax.ShapeDtypeStruct((chip_rows // 2, width), dtype) for _ in range(5))
    else:
        out_shape = (jax.ShapeDtypeStruct((frame_rows, width), dtype),)
    anywhere = pl.BlockSpec(memory_space=pl.ANY)
    scalars = pl.BlockSpec(memory_space=pltpu.SMEM)
    vectors = pl.BlockSpec(memory_space=pltpu.VMEM)
    flops = 2 * frame_rows * width * (3 * features + 2 * (frame_rows + keys.shape[0]))
    return pl.pallas_call(
        kernel,
        out_shape=out_shape,
        in_specs=[scalars, scalars, vectors, vectors, vectors] + [anywhere] * (4 + len(pieces) + len(updates)),
        out_specs=tuple(vectors for _ in out_shape),
        scratch_shapes=[
            pltpu.VMEM((frame_rows, features), dtype),
            pltpu.VMEM((frame_rows, features), jnp.bfloat16),
            pltpu.VMEM((3, features, width), jnp.bfloat16),
            pltpu.VMEM((max(len(updates), 1), frame_rows, width), dtype),
            pltpu.VMEM((frame_rows, width), dtype),
            pltpu.SemaphoreType.DMA((2,)),
            pltpu.SemaphoreType.DMA((len(pieces),)),
            pltpu.SemaphoreType.DMA((max(len(updates), 1),)),
        ],
        compiler_params=pltpu.CompilerParams(vmem_limit_bytes=VMEM_LIMIT),
        cost_estimate=pl.CostEstimate(
            flops=flops, transcendentals=frame_rows * head_count * (frame_rows + keys.shape[0]), bytes_accessed=6 << 20
        ),
        name="last_step" if last else "step",
    )(
        counts,
        scales,
        norm_gain.reshape(1, -1),
        keys,
        values,
        *tokens,
        *[array for array, _ in pieces],
        *[array for array, _ in updates],
    )


def join_kernel(keep, first, second, third, fourth, out):
    _, _, plane, y, c = here()
    low = plane % 2
    width = keep.shape[1]

    def put(ref, plane_low, at_y):
        out[:, columns(plane_low * 2 + at_y, width)] = ref[...]

    @pl.when(low == c)
    def _():
        put(keep, low, y)
        put(first, low, 1 - y)
        put(second, 1 - low, y)
        put(third, 1 - low, 1 - y)

    @pl.when(low != c)
    def _():
        put(first, 1 - low, y)
        put(second, low, 1 - y)
        put(third, low, y)
        put(fourth, 1 - low, 1 - y)


def joined(keep, first, second, third, fourth):
    at_home = lambda p, c: c == p % 2
    first = moved(
        first, lambda x, p, y, c: (x, p, 1 - y, c) if at_home(p, c) else (x, p ^ 1, y, 1 - c)
    )
    second = moved(
        second, lambda x, p, y, c: (x, p, 1 - y, 1 - c) if at_home(p, c) else (x, p ^ 1, y, c)
    )
    third = moved(
        third, lambda x, p, y, c: (x, p, y, 1 - c) if at_home(p, c) else (x, p ^ 1, 1 - y, c)
    )
    fourth = moved(
        fourth, lambda x, p, y, c: None if at_home(p, c) else (x, p ^ 1, 1 - y, 1 - c)
    )
    rows, width = keep.shape
    return pl.pallas_call(
        join_kernel,
        out_shape=jax.ShapeDtypeStruct((rows, width * SPATIAL), keep.dtype),
        name="join",
    )(keep, first, second, third, fourth)


def paired_planes(
    latent, norm_gain, w_query, w_key, w_value, mem_cache, intersection, counts, slot_of, step_scale
):
    own, beside, even, odd, kept, sent = pack(w_query, w_key, w_value, mem_cache, intersection, slot_of)
    pieces = all_pieces(own, beside, even, odd)
    tokens = all_tokens(latent)
    keys, values = all_memory(kept, sent)
    (attended,) = step(pieces, [], False, counts, step_scale, norm_gain, keys, values, tokens)
    updates = [
        (attended, (0, 0)),
        (moved(attended, lambda x, p, y, c: (x, p ^ 1, 1 - y, c)), (1, 1)),
        (moved(attended, lambda x, p, y, c: (x, p ^ 1, y, c)), (1, 0)),
        (moved(attended, lambda x, p, y, c: (x, p, 1 - y, c)), (0, 1)),
    ]
    shares = step(pieces, updates, True, counts, step_scale, norm_gain, keys, values, tokens)
    return joined(*shares)


def fits_paired_planes(latent, norm_gain, w_query, w_key, w_value, mem_cache, *_):
    devices = lax.axis_size("frame")
    planes = devices // SPATIAL
    return (
        lax.axis_size("groups") == 2
        and devices == planes * SPATIAL
        and planes >= 2
        and planes & (planes - 1) == 0
        and w_query.shape[0] % 16 == 0
        and mem_cache.shape[1] == 1
    )


def from_partner(array, axis, bit):
    return lax.ppermute(array, axis, [(i, i ^ 1 << bit) for i in range(lax.axis_size(axis))])


def in_order(mine, theirs, upper, axis_dim):
    low_first = jnp.concatenate([mine, theirs], axis=axis_dim)
    high_first = jnp.concatenate([theirs, mine], axis=axis_dim)
    return jnp.where(upper, high_first, low_first)


def attend(queries, frame_pair, mem_keys, mem_values, live_keys, head_count):
    tok_rows, feature_width = queries.shape
    head_size = feature_width // head_count
    scale_dot = 1.0 / math.sqrt(head_size)
    q_heads = queries.reshape(tok_rows, head_count, head_size)
    k_heads = frame_pair[0].reshape(-1, head_count, head_size)
    v_heads = frame_pair[1].reshape(-1, head_count, head_size)
    frame_scores = (
        jnp.einsum("thd,khd->htk", q_heads, k_heads, preferred_element_type=jnp.float32) * scale_dot
    )
    remote_scores = (
        jnp.einsum("thd,khd->htk", q_heads, mem_keys, preferred_element_type=jnp.float32)
        * scale_dot
    )
    remote_scores = jnp.where(live_keys[None, None, :], remote_scores, -1e30)
    largest = jnp.maximum(
        jnp.max(frame_scores, axis=-1, keepdims=True),
        jnp.max(remote_scores, axis=-1, keepdims=True),
    )
    frame_weights = jnp.exp(frame_scores - largest)
    remote_weights = jnp.exp(remote_scores - largest)
    denominator = jnp.sum(frame_weights, axis=-1) + jnp.sum(remote_weights, axis=-1)
    blended = jnp.einsum(
        "htk,khd->thd",
        frame_weights.astype(jnp.bfloat16),
        v_heads,
        preferred_element_type=jnp.float32,
    )
    blended = blended + jnp.einsum(
        "htk,khd->thd",
        remote_weights.astype(jnp.bfloat16),
        mem_values,
        preferred_element_type=jnp.float32,
    )
    blended = blended / jnp.transpose(denominator)[:, :, None]
    return blended.reshape(tok_rows, feature_width).astype(jnp.bfloat16)


def rms_normed(current, norm_gain):
    widened = current.astype(jnp.float32)
    inverse = lax.rsqrt(jnp.mean(widened * widened, axis=-1, keepdims=True) + 1e-06)
    return (widened, (widened * inverse * norm_gain).astype(jnp.bfloat16))


def separate_frames(
    latent, norm_gain, w_query, w_key, w_value, mem_cache, intersection, counts, slot_of, step_scale
):
    devices = lax.axis_size("frame")
    position = lax.axis_index("frame")
    frame_index = position // SPATIAL
    doublings = SPATIAL.bit_length() - 1
    target_frame = jnp.arange(devices, dtype=jnp.int32) // SPATIAL
    current = latent
    feature_width = latent.shape[1]
    share_width = feature_width // SPATIAL
    head_share = HEADS // SPATIAL

    def column_pieces(weight):
        row_count = weight.shape[0]
        split_cols = jnp.transpose(weight.reshape(row_count, SPATIAL, share_width), (1, 0, 2))
        return jnp.tile(split_cols, (devices // SPATIAL, 1, 1))

    own_query, own_key, own_value = (
        lax.all_to_all(column_pieces(w_query), "frame", split_axis=0, concat_axis=1, tiled=True),
        lax.all_to_all(column_pieces(w_key), "frame", split_axis=0, concat_axis=1, tiled=True),
        lax.all_to_all(column_pieces(w_value), "frame", split_axis=0, concat_axis=1, tiled=True),
    )
    own_query, own_key, own_value = (own_query[0], own_key[0], own_value[0])
    listed = mem_cache[slot_of[intersection[target_frame]]]
    list_len = listed.shape[1]
    local_mem = listed.shape[2]
    grouped = listed.reshape(
        devices // SPATIAL, SPATIAL, list_len, local_mem, 2, SPATIAL, share_width
    )
    diagonal_part = jnp.diagonal(grouped, axis1=1, axis2=5)
    outgoing = jnp.moveaxis(diagonal_part, -1, 1).reshape(
        devices, list_len, local_mem, 2, share_width
    )
    fetched = lax.all_to_all(outgoing, "frame", split_axis=0, concat_axis=2, tiled=True)[0]
    mem_len = fetched.shape[1]
    mem_keys = fetched[:, :, 0, :].reshape(list_len * mem_len, head_share, HS)
    mem_values = fetched[:, :, 1, :].reshape(list_len * mem_len, head_share, HS)
    live_keys = jnp.arange(list_len * mem_len, dtype=jnp.int32) // mem_len < counts[frame_index]
    tok_rows = latent.shape[0]
    for step_index in range(STEPS):
        widened, normed = rms_normed(current, norm_gain)
        gathered = normed
        for bit_index in range(doublings):
            partner = from_partner(gathered, "frame", bit_index)
            gathered = in_order(gathered, partner, position >> bit_index & 1 == 1, 0)
        queries = jnp.dot(gathered, own_query, preferred_element_type=jnp.float32).astype(
            jnp.bfloat16
        )
        keys_frame = jnp.dot(gathered, own_key, preferred_element_type=jnp.float32).astype(
            jnp.bfloat16
        )
        values_frame = jnp.dot(gathered, own_value, preferred_element_type=jnp.float32).astype(
            jnp.bfloat16
        )
        frame_pair = jnp.stack([keys_frame, values_frame])
        attended = attend(queries, frame_pair, mem_keys, mem_values, live_keys, head_share)
        blocks = attended.reshape(SPATIAL, tok_rows, share_width)[:, None]
        for bit_index in range(doublings):
            upper = position >> bit_index & 1 == 1
            dest_count = blocks.shape[0]
            paired = blocks.reshape((dest_count // 2, 2) + blocks.shape[1:])
            kept = jnp.where(upper, paired[:, 1], paired[:, 0])
            sent = jnp.where(upper, paired[:, 0], paired[:, 1])
            arrived = from_partner(sent, "frame", bit_index)
            blocks = in_order(kept, arrived, upper, 1)
        joined = jnp.transpose(blocks[0], (1, 0, 2)).reshape(tok_rows, feature_width)
        current = (widened + step_scale[step_index] * joined.astype(jnp.float32)).astype(
            jnp.bfloat16
        )
    return current


def per_device(*arguments):
    return (paired_planes if fits_paired_planes(*arguments) else separate_frames)(*arguments)


def solution(mesh):
    placed = (
        P(("groups", "frame"), None),
        P(),
        P("frame", None),
        P("frame", None),
        P("frame", None),
        P("groups", "frame", None, None),
        P("groups", None),
        P("groups"),
        P("groups"),
        P(),
    )
    return jax.shard_map(
        per_device,
        mesh=mesh,
        in_specs=placed,
        out_specs=P(("groups", "frame"), None),
        check_vma=False,
    )
```

```python
import functools
import math

import jax
import jax.numpy as jnp
from jax import lax
from jax.experimental import pallas as pl
from jax.experimental.pallas import tpu as pltpu
from jax.sharding import PartitionSpec as P


HEADS = 12
HS = 128
SPATIAL = 4
STEPS = 2
AXES = ("groups", "frame")
VMEM_LIMIT = 48 * 1024 * 1024


def coords(index):
    return index // 4, (index // 2) % 2, index % 2


def quarter_of(plane, y):
    return (plane % 2) * 2 + y


def moved(array, target):
    devices = lax.axis_size("frame")
    pairs = []
    for x in range(lax.axis_size("groups")):
        for index in range(devices):
            place = target(x, *coords(index))
            if place is not None:
                to_x, to_plane, to_y, to_c = place
                pairs.append((x * devices + index, to_x * devices + to_plane * 4 + to_y * 2 + to_c))
    return lax.ppermute(array, AXES, pairs)


def here():
    x = lax.axis_index("groups")
    index = lax.axis_index("frame")
    plane = index // 4
    rest = index - plane * 4
    y = rest // 2
    return x, index, plane, y, rest - y * 2


def flipped(value, bits):
    out = value
    bit = 1
    while bit <= bits:
        if bits & bit:
            out = out + bit - 2 * bit * ((value // bit) % 2)
        bit *= 2
    return out


def joined_bits(one, other):
    return one + other - 2 * one * other


def columns(quarter, width):
    return pl.ds(pl.multiple_of(quarter * width, 128), width)


def pack_weights_kernel(
    w_query, w_key, w_value, own_ref, beside_ref, even_ref, odd_ref, rows, row_sem, out_sem
):
    x, _, plane, y, c = here()
    width = own_ref.shape[2]
    reads = []
    for number, weight in enumerate((w_query, w_key, w_value)):
        reads.append(pltpu.make_async_copy(weight, rows.at[number], row_sem.at[number]))
        reads[-1].start()
    across = joined_bits(joined_bits(x, y), c)
    low = plane % 2
    quarters = (low * 2 + across, (1 - low) * 2 + across, low * 2 + 1 - y, quarter_of(plane, y))
    for read in reads:
        read.wait()
    gives = []
    for number, (quarter, out) in enumerate(zip(quarters, (even_ref, odd_ref, beside_ref, own_ref))):
        gives.append(pltpu.make_async_copy(rows.at[:, :, columns(quarter, width)], out, out_sem.at[number]))
        gives[-1].start()
    for give in gives:
        give.wait()


def pack_weights(w_query, w_key, w_value):
    shard_rows, features = w_query.shape
    piece = jax.ShapeDtypeStruct((3, shard_rows, features // SPATIAL), w_query.dtype)
    anywhere = pl.BlockSpec(memory_space=pl.ANY)
    held = pl.BlockSpec(memory_space=pltpu.HBM)
    return pl.pallas_call(
        pack_weights_kernel,
        out_shape=(piece,) * 4,
        in_specs=[held] * 3,
        out_specs=(anywhere,) * 4,
        scratch_shapes=[
            pltpu.VMEM((3, shard_rows, features), w_query.dtype),
            pltpu.SemaphoreType.DMA((3,)),
            pltpu.SemaphoreType.DMA((4,)),
        ],
        name="pack_weights",
    )(w_query, w_key, w_value)


def pack_memory_kernel(
    list_hbm, slot_hbm, mem_ref, kept_ref, sent_ref, list_ref, slot_ref, stored, scalar_sem, mem_sem, give_sem
):
    _, index, _, _, _ = here()
    devices = lax.axis_size("frame")
    frames, entries = list_ref.shape
    width = kept_ref.shape[-1]
    scalars = [
        pltpu.make_async_copy(list_hbm, list_ref, scalar_sem.at[0]),
        pltpu.make_async_copy(slot_hbm, slot_ref, scalar_sem.at[1]),
    ]
    for copy in scalars:
        copy.start()
    for copy in scalars:
        copy.wait()
    picks = []
    for frame in range(frames):
        for entry in range(entries):
            number = frame * entries + entry
            row = slot_ref[list_ref[frame, entry]]
            picks.append(pltpu.make_async_copy(mem_ref.at[row, 0], stored.at[number], mem_sem.at[number]))
            picks[-1].start()
    for pick in picks:
        pick.wait()
    gives = []
    bits = devices.bit_length() - 1
    for away in range(devices):
        target = flipped(index, away)
        to_plane, to_y, to_c = coords(target)
        to_frame = (to_plane // 2) * 2 + to_c
        place = 0
        for bit in range(1, bits):
            place = place * 2 + (away >> bit & 1)
        out = sent_ref if away & 1 else kept_ref
        gives.append(
            pltpu.make_async_copy(
                stored.at[pl.ds(to_frame * entries, entries), :, columns(quarter_of(to_plane, to_y), width)],
                out.at[place],
                give_sem.at[away],
            )
        )
        gives[-1].start()
    for give in gives:
        give.wait()


def pack_memory(mem_cache, intersection, slot_of):
    devices = lax.axis_size("frame")
    features = mem_cache.shape[-1]
    frames, entries = intersection.shape
    half = jax.ShapeDtypeStruct((devices // 2, entries, 2, features // SPATIAL), mem_cache.dtype)
    anywhere = pl.BlockSpec(memory_space=pl.ANY)
    held = pl.BlockSpec(memory_space=pltpu.HBM)
    return pl.pallas_call(
        pack_memory_kernel,
        out_shape=(half,) * 2,
        in_specs=[held] * 3,
        out_specs=(anywhere,) * 2,
        scratch_shapes=[
            pltpu.SMEM(intersection.shape, intersection.dtype),
            pltpu.SMEM(slot_of.shape, slot_of.dtype),
            pltpu.VMEM((frames * entries, 2, features), mem_cache.dtype),
            pltpu.SemaphoreType.DMA((2,)),
            pltpu.SemaphoreType.DMA((frames * entries,)),
            pltpu.SemaphoreType.DMA((devices,)),
        ],
        name="pack_memory",
    )(intersection, slot_of, mem_cache)


def all_pieces(own, beside, even, odd):
    planes = lax.axis_size("frame") // 4
    pieces = [("own", own, (0, 0, False))]
    pieces.append(("near", moved(beside, lambda x, p, y, c: (x, p, 1 - y, c)), (0, 1, False)))
    for bits in range(1, planes):
        name = f"plane{bits}"
        sent = even if bits % 2 == 0 else odd
        direct = moved(sent, lambda x, p, y, c, bits=bits: (x, p ^ bits, y ^ x ^ c, c))
        pieces.append((name, direct, (bits, 0, True)))
        name = f"cross{bits}"
        pieces.append((name, moved(direct, lambda x, p, y, c: (1 - x, p, y, c)), (bits, 1, True)))
    places = [(array, place + (0,)) for _, array, place in pieces]
    for name, array, place in pieces:
        places.append((moved(array, lambda x, p, y, c: (x, p, y, 1 - c)), place + (1,)))
    return places


def all_memory(kept, sent):
    devices = lax.axis_size("frame")
    held = jnp.stack([kept, hop(sent, 0)])
    for bit in range(1, devices.bit_length() - 1):
        half = held.shape[1] // 2
        held = jnp.concatenate([held[:, :half], hop(held[:, half:], bit)])
    keys, values = held[:, 0, :, 0, :], held[:, 0, :, 1, :]
    return keys.reshape(-1, keys.shape[-1]), values.reshape(-1, values.shape[-1])


def hop(array, bit):
    return lax.ppermute(array, "frame", [(i, i ^ 1 << bit) for i in range(lax.axis_size("frame"))])


def all_tokens(latent):
    other = moved(latent, lambda x, p, y, c: (x, p, y, 1 - c) if c != p % 2 else None)
    block = jnp.concatenate([latent, other])
    near = moved(block, lambda x, p, y, c: (x, p, 1 - y, c) if c == p % 2 else None)
    far = moved(block, lambda x, p, y, c: (x, p ^ 1, y, c) if c == p % 2 else None)
    far_near = moved(far, lambda x, p, y, c: (x, p, 1 - y, c) if c != p % 2 else None)
    return block, near, far, far_near


def step_kernel(places, updates, last, head_count, *refs):
    refs = list(refs)
    count_hbm, scale_hbm, gain_ref, key_ref, value_ref = refs[:5]
    token_refs = refs[5:9]
    piece_refs = refs[9 : 9 + len(places)]
    update_refs = refs[9 + len(places) : 9 + len(places) + len(updates)]
    outs = refs[9 + len(places) + len(updates) : -11]
    current, normed, weights, parts, attended, count_ref, scale_ref, token_sem, piece_sem, update_sem, scalar_sem = (
        refs[-11:]
    )
    x, _, plane, y, c = here()
    low = plane % 2
    chip_rows = token_refs[0].shape[0]
    width = parts.shape[2]
    at_home = low == c

    scalar_copies = (
        pltpu.make_async_copy(count_hbm, count_ref, scalar_sem.at[0]),
        pltpu.make_async_copy(scale_hbm, scale_ref, scalar_sem.at[1]),
    )
    for copy in scalar_copies:
        copy.start()

    def token_copies(first, second):
        return (
            pltpu.make_async_copy(first, current.at[pl.ds(y * chip_rows, chip_rows)], token_sem.at[0]),
            pltpu.make_async_copy(second, current.at[pl.ds((1 - y) * chip_rows, chip_rows)], token_sem.at[1]),
        )

    @pl.when(at_home)
    def _():
        for copy in token_copies(token_refs[0], token_refs[1]):
            copy.start()

    @pl.when(jnp.logical_not(at_home))
    def _():
        for copy in token_copies(token_refs[2], token_refs[3]):
            copy.start()

    update_copies = []
    for number, (ref, _) in enumerate(zip(update_refs, updates)):
        update_copies.append(pltpu.make_async_copy(ref, parts.at[number], update_sem.at[number]))
        update_copies[-1].start()
    piece_copies = []
    shard_rows = piece_refs[0].shape[1]
    for number, (ref, (plane_bits, y_bits, with_x, c_bits)) in enumerate(zip(piece_refs, places)):
        from_y, from_c = flipped(y, y_bits), flipped(c, c_bits)
        if with_x:
            from_y = joined_bits(joined_bits(from_y, x), from_c)
        shard = flipped(plane, plane_bits) * 4 + from_y * 2 + from_c
        start = pl.multiple_of(shard * shard_rows, 16)
        piece_copies.append(
            pltpu.make_async_copy(ref, weights.at[:, pl.ds(start, shard_rows), :], piece_sem.at[number])
        )
        piece_copies[-1].start()
    for copy in token_copies(token_refs[0], token_refs[1]):
        copy.wait()
    for copy in update_copies:
        copy.wait()
    for copy in scalar_copies:
        copy.wait()
    for number, (plane_bits, y_bits) in enumerate(updates):
        quarter = quarter_of(flipped(plane, plane_bits), flipped(y, y_bits))
        spot = columns(quarter, width)
        current[:, spot] = (
            current[:, spot].astype(jnp.float32) + scale_ref[0] * parts[number].astype(jnp.float32)
        ).astype(current.dtype)
    widened = current[...].astype(jnp.float32)
    inverse = lax.rsqrt(jnp.mean(widened * widened, axis=-1, keepdims=True) + 1e-06)
    normed[...] = (widened * inverse * gain_ref[...]).astype(normed.dtype)
    for copy in piece_copies:
        copy.wait()
    queries, keys, values = (
        jnp.dot(normed[...], weights[number], preferred_element_type=jnp.float32).astype(jnp.bfloat16)
        for number in range(3)
    )
    frame = (plane // 2) * 2 + c
    entries = key_ref.shape[0] // lax.axis_size("frame")
    head_size = width // head_count
    scale_dot = 1.0 / math.sqrt(head_size)
    entry = lax.broadcasted_iota(jnp.int32, (1, key_ref.shape[0]), 1) % entries
    live = entry < count_ref[frame]
    contract_last = (((1,), (1,)), ((), ()))
    for head in range(head_count):
        span = slice(head * head_size, (head + 1) * head_size)
        frame_scores = (
            lax.dot_general(queries[:, span], keys[:, span], contract_last, preferred_element_type=jnp.float32)
            * scale_dot
        )
        mem_scores = (
            lax.dot_general(queries[:, span], key_ref[:, span], contract_last, preferred_element_type=jnp.float32)
            * scale_dot
        )
        mem_scores = jnp.where(live, mem_scores, -1e30)
        largest = jnp.maximum(
            jnp.max(frame_scores, axis=-1, keepdims=True), jnp.max(mem_scores, axis=-1, keepdims=True)
        )
        frame_weights = jnp.exp(frame_scores - largest)
        mem_weights = jnp.exp(mem_scores - largest)
        denominator = jnp.sum(frame_weights, axis=-1, keepdims=True) + jnp.sum(mem_weights, axis=-1, keepdims=True)
        blended = jnp.dot(
            frame_weights.astype(jnp.bfloat16), values[:, span], preferred_element_type=jnp.float32
        ) + jnp.dot(mem_weights.astype(jnp.bfloat16), value_ref[:, span], preferred_element_type=jnp.float32)
        attended[:, span] = (blended / denominator).astype(attended.dtype)
    if not last:
        outs[0][...] = attended[...]
        return
    spot = columns(quarter_of(plane, y), width)
    attended[...] = (
        current[:, spot].astype(jnp.float32) + scale_ref[1] * attended[...].astype(jnp.float32)
    ).astype(attended.dtype)
    rows = chip_rows // 2
    here_rows, there_rows = y * chip_rows, (1 - y) * chip_rows

    def part(start):
        return attended[pl.ds(pl.multiple_of(start, rows), rows), :]

    keep, first, second, third, fourth = outs
    keep[...] = part(here_rows)
    fourth[...] = part(there_rows + rows)

    @pl.when(at_home)
    def _():
        first[...] = part(there_rows)
        second[...] = part(there_rows + rows)
        third[...] = part(here_rows + rows)

    @pl.when(jnp.logical_not(at_home))
    def _():
        first[...] = part(here_rows + rows)
        second[...] = part(here_rows)
        third[...] = part(there_rows)


def step(pieces, updates, last, counts, scales, norm_gain, keys, values, tokens):
    _, width = pieces[0][0].shape[1:]
    features = norm_gain.shape[0]
    chip_rows = tokens[0].shape[0]
    frame_rows = 2 * chip_rows
    dtype = tokens[0].dtype
    head_count = HEADS // SPATIAL
    kernel = functools.partial(
        step_kernel, tuple(place for _, place in pieces), tuple(bits for _, bits in updates), last, head_count
    )
    if last:
        out_shape = tuple(jax.ShapeDtypeStruct((chip_rows // 2, width), dtype) for _ in range(5))
    else:
        out_shape = (jax.ShapeDtypeStruct((frame_rows, width), dtype),)
    anywhere = pl.BlockSpec(memory_space=pl.ANY)
    held = pl.BlockSpec(memory_space=pltpu.HBM)
    vectors = pl.BlockSpec(memory_space=pltpu.VMEM)
    flops = 2 * frame_rows * width * (3 * features + 2 * (frame_rows + keys.shape[0]))
    return pl.pallas_call(
        kernel,
        out_shape=out_shape,
        in_specs=[held, held, vectors, vectors, vectors] + [anywhere] * (4 + len(pieces) + len(updates)),
        out_specs=tuple(vectors for _ in out_shape),
        scratch_shapes=[
            pltpu.VMEM((frame_rows, features), dtype),
            pltpu.VMEM((frame_rows, features), jnp.bfloat16),
            pltpu.VMEM((3, features, width), jnp.bfloat16),
            pltpu.VMEM((max(len(updates), 1), frame_rows, width), dtype),
            pltpu.VMEM((frame_rows, width), dtype),
            pltpu.SMEM(counts.shape, counts.dtype),
            pltpu.SMEM(scales.shape, scales.dtype),
            pltpu.SemaphoreType.DMA((2,)),
            pltpu.SemaphoreType.DMA((len(pieces),)),
            pltpu.SemaphoreType.DMA((max(len(updates), 1),)),
            pltpu.SemaphoreType.DMA((2,)),
        ],
        compiler_params=pltpu.CompilerParams(vmem_limit_bytes=VMEM_LIMIT),
        cost_estimate=pl.CostEstimate(
            flops=flops, transcendentals=frame_rows * head_count * (frame_rows + keys.shape[0]), bytes_accessed=6 << 20
        ),
        name="last_step" if last else "step",
    )(
        counts,
        scales,
        norm_gain.reshape(1, -1),
        keys,
        values,
        *tokens,
        *[array for array, _ in pieces],
        *[array for array, _ in updates],
    )


def join_kernel(keep, first, second, third, fourth, out, sem):
    _, _, plane, y, c = here()
    low = plane % 2
    width = keep.shape[1]

    def put(number, ref, plane_low, at_y):
        return pltpu.make_async_copy(ref, out.at[:, columns(plane_low * 2 + at_y, width)], sem.at[number])

    @pl.when(low == c)
    def _():
        put(0, keep, low, y).start()
        put(1, first, low, 1 - y).start()
        put(2, second, 1 - low, y).start()
        put(3, third, 1 - low, 1 - y).start()

    @pl.when(low != c)
    def _():
        put(0, first, 1 - low, y).start()
        put(1, second, low, 1 - y).start()
        put(2, third, low, y).start()
        put(3, fourth, 1 - low, 1 - y).start()

    for number in range(4):
        put(number, first, number // 2, number % 2).wait()


def joined(keep, first, second, third, fourth):
    def at_home(p, c):
        return c == p % 2

    first = moved(first, lambda x, p, y, c: (x, p, 1 - y, c) if at_home(p, c) else (x, p ^ 1, y, 1 - c))
    second = moved(second, lambda x, p, y, c: (x, p, 1 - y, 1 - c) if at_home(p, c) else (x, p ^ 1, y, c))
    third = moved(third, lambda x, p, y, c: (x, p, y, 1 - c) if at_home(p, c) else (x, p ^ 1, 1 - y, c))
    fourth = moved(fourth, lambda x, p, y, c: None if at_home(p, c) else (x, p ^ 1, 1 - y, 1 - c))
    rows, width = keep.shape
    anywhere = pl.BlockSpec(memory_space=pl.ANY)
    return pl.pallas_call(
        join_kernel,
        out_shape=jax.ShapeDtypeStruct((rows, width * SPATIAL), keep.dtype),
        in_specs=[anywhere] * 5,
        out_specs=anywhere,
        scratch_shapes=[pltpu.SemaphoreType.DMA((4,))],
        name="join",
    )(keep, first, second, third, fourth)


def paired_planes(
    latent, norm_gain, w_query, w_key, w_value, mem_cache, intersection, counts, slot_of, step_scale
):
    pieces = all_pieces(*pack_weights(w_query, w_key, w_value))
    tokens = all_tokens(latent)
    keys, values = all_memory(*pack_memory(mem_cache, intersection, slot_of))
    (attended,) = step(pieces, [], False, counts, step_scale, norm_gain, keys, values, tokens)
    updates = [
        (attended, (0, 0)),
        (moved(attended, lambda x, p, y, c: (x, p ^ 1, 1 - y, c)), (1, 1)),
        (moved(attended, lambda x, p, y, c: (x, p ^ 1, y, c)), (1, 0)),
        (moved(attended, lambda x, p, y, c: (x, p, 1 - y, c)), (0, 1)),
    ]
    shares = step(pieces, updates, True, counts, step_scale, norm_gain, keys, values, tokens)
    return joined(*shares)


def fits_paired_planes(latent, norm_gain, w_query, w_key, w_value, mem_cache, *_):
    devices = lax.axis_size("frame")
    planes = devices // SPATIAL
    return (
        lax.axis_size("groups") == 2
        and devices == planes * SPATIAL
        and planes >= 2
        and planes & (planes - 1) == 0
        and w_query.shape[0] % 16 == 0
        and mem_cache.shape[1] == 1
    )


def from_partner(array, axis, bit):
    return lax.ppermute(array, axis, [(i, i ^ 1 << bit) for i in range(lax.axis_size(axis))])


def in_order(mine, theirs, upper, axis_dim):
    low_first = jnp.concatenate([mine, theirs], axis=axis_dim)
    high_first = jnp.concatenate([theirs, mine], axis=axis_dim)
    return jnp.where(upper, high_first, low_first)


def attend(queries, frame_pair, mem_keys, mem_values, live_keys, head_count):
    tok_rows, feature_width = queries.shape
    head_size = feature_width // head_count
    scale_dot = 1.0 / math.sqrt(head_size)
    q_heads = queries.reshape(tok_rows, head_count, head_size)
    k_heads = frame_pair[0].reshape(-1, head_count, head_size)
    v_heads = frame_pair[1].reshape(-1, head_count, head_size)
    frame_scores = (
        jnp.einsum("thd,khd->htk", q_heads, k_heads, preferred_element_type=jnp.float32) * scale_dot
    )
    remote_scores = (
        jnp.einsum("thd,khd->htk", q_heads, mem_keys, preferred_element_type=jnp.float32)
        * scale_dot
    )
    remote_scores = jnp.where(live_keys[None, None, :], remote_scores, -1e30)
    largest = jnp.maximum(
        jnp.max(frame_scores, axis=-1, keepdims=True),
        jnp.max(remote_scores, axis=-1, keepdims=True),
    )
    frame_weights = jnp.exp(frame_scores - largest)
    remote_weights = jnp.exp(remote_scores - largest)
    denominator = jnp.sum(frame_weights, axis=-1) + jnp.sum(remote_weights, axis=-1)
    blended = jnp.einsum(
        "htk,khd->thd",
        frame_weights.astype(jnp.bfloat16),
        v_heads,
        preferred_element_type=jnp.float32,
    )
    blended = blended + jnp.einsum(
        "htk,khd->thd",
        remote_weights.astype(jnp.bfloat16),
        mem_values,
        preferred_element_type=jnp.float32,
    )
    blended = blended / jnp.transpose(denominator)[:, :, None]
    return blended.reshape(tok_rows, feature_width).astype(jnp.bfloat16)


def rms_normed(current, norm_gain):
    widened = current.astype(jnp.float32)
    inverse = lax.rsqrt(jnp.mean(widened * widened, axis=-1, keepdims=True) + 1e-06)
    return (widened, (widened * inverse * norm_gain).astype(jnp.bfloat16))


def separate_frames(
    latent, norm_gain, w_query, w_key, w_value, mem_cache, intersection, counts, slot_of, step_scale
):
    devices = lax.axis_size("frame")
    position = lax.axis_index("frame")
    frame_index = position // SPATIAL
    doublings = SPATIAL.bit_length() - 1
    target_frame = jnp.arange(devices, dtype=jnp.int32) // SPATIAL
    current = latent
    feature_width = latent.shape[1]
    share_width = feature_width // SPATIAL
    head_share = HEADS // SPATIAL

    def column_pieces(weight):
        row_count = weight.shape[0]
        split_cols = jnp.transpose(weight.reshape(row_count, SPATIAL, share_width), (1, 0, 2))
        return jnp.tile(split_cols, (devices // SPATIAL, 1, 1))

    own_query, own_key, own_value = (
        lax.all_to_all(column_pieces(w_query), "frame", split_axis=0, concat_axis=1, tiled=True),
        lax.all_to_all(column_pieces(w_key), "frame", split_axis=0, concat_axis=1, tiled=True),
        lax.all_to_all(column_pieces(w_value), "frame", split_axis=0, concat_axis=1, tiled=True),
    )
    own_query, own_key, own_value = (own_query[0], own_key[0], own_value[0])
    listed = mem_cache[slot_of[intersection[target_frame]]]
    list_len = listed.shape[1]
    local_mem = listed.shape[2]
    grouped = listed.reshape(
        devices // SPATIAL, SPATIAL, list_len, local_mem, 2, SPATIAL, share_width
    )
    diagonal_part = jnp.diagonal(grouped, axis1=1, axis2=5)
    outgoing = jnp.moveaxis(diagonal_part, -1, 1).reshape(
        devices, list_len, local_mem, 2, share_width
    )
    fetched = lax.all_to_all(outgoing, "frame", split_axis=0, concat_axis=2, tiled=True)[0]
    mem_len = fetched.shape[1]
    mem_keys = fetched[:, :, 0, :].reshape(list_len * mem_len, head_share, HS)
    mem_values = fetched[:, :, 1, :].reshape(list_len * mem_len, head_share, HS)
    live_keys = jnp.arange(list_len * mem_len, dtype=jnp.int32) // mem_len < counts[frame_index]
    tok_rows = latent.shape[0]
    for step_index in range(STEPS):
        widened, normed = rms_normed(current, norm_gain)
        gathered = normed
        for bit_index in range(doublings):
            partner = from_partner(gathered, "frame", bit_index)
            gathered = in_order(gathered, partner, position >> bit_index & 1 == 1, 0)
        queries = jnp.dot(gathered, own_query, preferred_element_type=jnp.float32).astype(
            jnp.bfloat16
        )
        keys_frame = jnp.dot(gathered, own_key, preferred_element_type=jnp.float32).astype(
            jnp.bfloat16
        )
        values_frame = jnp.dot(gathered, own_value, preferred_element_type=jnp.float32).astype(
            jnp.bfloat16
        )
        frame_pair = jnp.stack([keys_frame, values_frame])
        attended = attend(queries, frame_pair, mem_keys, mem_values, live_keys, head_share)
        blocks = attended.reshape(SPATIAL, tok_rows, share_width)[:, None]
        for bit_index in range(doublings):
            upper = position >> bit_index & 1 == 1
            dest_count = blocks.shape[0]
            paired = blocks.reshape((dest_count // 2, 2) + blocks.shape[1:])
            kept = jnp.where(upper, paired[:, 1], paired[:, 0])
            sent = jnp.where(upper, paired[:, 0], paired[:, 1])
            arrived = from_partner(sent, "frame", bit_index)
            blocks = in_order(kept, arrived, upper, 1)
        joined = jnp.transpose(blocks[0], (1, 0, 2)).reshape(tok_rows, feature_width)
        current = (widened + step_scale[step_index] * joined.astype(jnp.float32)).astype(
            jnp.bfloat16
        )
    return current


def per_device(*arguments):
    return (paired_planes if fits_paired_planes(*arguments) else separate_frames)(*arguments)


def solution(mesh):
    placed = (
        P(("groups", "frame"), None),
        P(),
        P("frame", None),
        P("frame", None),
        P("frame", None),
        P("groups", "frame", None, None),
        P("groups", None),
        P("groups"),
        P("groups"),
        P(),
    )
    return jax.shard_map(
        per_device,
        mesh=mesh,
        in_specs=placed,
        out_specs=P(("groups", "frame"), None),
        check_vma=False,
    )
```

```python
import functools
import math

import jax
import jax.numpy as jnp
from jax import lax
from jax.experimental import pallas as pl
from jax.experimental.pallas import tpu as pltpu
from jax.sharding import PartitionSpec as P


HEADS = 12
HS = 128
SPATIAL = 4
STEPS = 2
AXES = ("groups", "frame")


def coords(index):
    return index // 4, (index // 2) % 2, index % 2


def quarter_of(plane, y):
    return (plane % 2) * 2 + y


def moved(array, target):
    devices = lax.axis_size("frame")
    pairs = []
    for x in range(lax.axis_size("groups")):
        for index in range(devices):
            place = target(x, *coords(index))
            if place is not None:
                to_x, to_plane, to_y, to_c = place
                pairs.append((x * devices + index, to_x * devices + to_plane * 4 + to_y * 2 + to_c))
    return lax.ppermute(array, AXES, pairs)


def here():
    x = lax.axis_index("groups")
    index = lax.axis_index("frame")
    plane = index // 4
    rest = index - plane * 4
    y = rest // 2
    return x, index, plane, y, rest - y * 2


def flipped(value, bits):
    out = value
    bit = 1
    while bit <= bits:
        if bits & bit:
            out = out + bit - 2 * bit * ((value // bit) % 2)
        bit *= 2
    return out


def joined_bits(one, other):
    return one + other - 2 * one * other


def columns(quarter, width):
    return pl.ds(pl.multiple_of(quarter * width, 128), width)


def pack_weights_kernel(
    w_query, w_key, w_value, own_ref, beside_ref, even_ref, odd_ref, rows, row_sem, out_sem
):
    x, _, plane, y, c = here()
    width = own_ref.shape[1] // 3
    reads = []
    for number, weight in enumerate((w_query, w_key, w_value)):
        reads.append(pltpu.make_async_copy(weight, rows.at[number], row_sem.at[number]))
        reads[-1].start()
    across = joined_bits(joined_bits(x, y), c)
    low = plane % 2
    quarters = (low * 2 + across, (1 - low) * 2 + across, low * 2 + 1 - y, quarter_of(plane, y))
    gives = []
    for number, read in enumerate(reads):
        read.wait()
        for place, (quarter, out) in enumerate(zip(quarters, (even_ref, odd_ref, beside_ref, own_ref))):
            gives.append(
                pltpu.make_async_copy(
                    rows.at[number, :, columns(quarter, width)],
                    out.at[:, pl.ds(number * width, width)],
                    out_sem.at[number, place],
                )
            )
            gives[-1].start()
    for give in gives:
        give.wait()


def pack_weights(w_query, w_key, w_value):
    shard_rows, features = w_query.shape
    piece = jax.ShapeDtypeStruct((shard_rows, 3 * (features // SPATIAL)), w_query.dtype)
    anywhere = pl.BlockSpec(memory_space=pl.ANY)
    held = pl.BlockSpec(memory_space=pltpu.HBM)
    return pl.pallas_call(
        pack_weights_kernel,
        out_shape=(piece,) * 4,
        in_specs=[held] * 3,
        out_specs=(anywhere,) * 4,
        scratch_shapes=[
            pltpu.VMEM((3, shard_rows, features), w_query.dtype),
            pltpu.SemaphoreType.DMA((3,)),
            pltpu.SemaphoreType.DMA((3, 4)),
        ],
        name="pack_weights",
    )(w_query, w_key, w_value)


def pack_memory_kernel(
    list_hbm, slot_hbm, mem_ref, kept_ref, sent_ref, list_ref, slot_ref, stored, scalar_sem, mem_sem, give_sem
):
    _, index, _, _, _ = here()
    devices = lax.axis_size("frame")
    frames, entries = list_ref.shape
    width = kept_ref.shape[-1]
    scalars = [
        pltpu.make_async_copy(list_hbm, list_ref, scalar_sem.at[0]),
        pltpu.make_async_copy(slot_hbm, slot_ref, scalar_sem.at[1]),
    ]
    for copy in scalars:
        copy.start()
    for copy in scalars:
        copy.wait()
    picks = []
    for frame in range(frames):
        for entry in range(entries):
            number = frame * entries + entry
            row = slot_ref[list_ref[frame, entry]]
            picks.append(pltpu.make_async_copy(mem_ref.at[row, 0], stored.at[number], mem_sem.at[number]))
            picks[-1].start()
    for pick in picks:
        pick.wait()
    gives = []
    bits = devices.bit_length() - 1
    for away in range(devices):
        target = flipped(index, away)
        to_plane, to_y, to_c = coords(target)
        to_frame = (to_plane // 2) * 2 + to_c
        place = 0
        for bit in range(1, bits):
            place = place * 2 + (away >> bit & 1)
        out = sent_ref if away & 1 else kept_ref
        gives.append(
            pltpu.make_async_copy(
                stored.at[pl.ds(to_frame * entries, entries), :, columns(quarter_of(to_plane, to_y), width)],
                out.at[place],
                give_sem.at[away],
            )
        )
        gives[-1].start()
    for give in gives:
        give.wait()


def pack_memory(mem_cache, intersection, slot_of):
    devices = lax.axis_size("frame")
    features = mem_cache.shape[-1]
    frames, entries = intersection.shape
    half = jax.ShapeDtypeStruct((devices // 2, entries, 2, features // SPATIAL), mem_cache.dtype)
    anywhere = pl.BlockSpec(memory_space=pl.ANY)
    held = pl.BlockSpec(memory_space=pltpu.HBM)
    return pl.pallas_call(
        pack_memory_kernel,
        out_shape=(half,) * 2,
        in_specs=[held] * 3,
        out_specs=(anywhere,) * 2,
        scratch_shapes=[
            pltpu.SMEM(intersection.shape, intersection.dtype),
            pltpu.SMEM(slot_of.shape, slot_of.dtype),
            pltpu.VMEM((frames * entries, 2, features), mem_cache.dtype),
            pltpu.SemaphoreType.DMA((2,)),
            pltpu.SemaphoreType.DMA((frames * entries,)),
            pltpu.SemaphoreType.DMA((devices,)),
        ],
        name="pack_memory",
    )(intersection, slot_of, mem_cache)


def all_pieces(own, beside, even, odd):
    planes = lax.axis_size("frame") // 4
    pieces = [("own", own, (0, 0, False))]
    pieces.append(("near", moved(beside, lambda x, p, y, c: (x, p, 1 - y, c)), (0, 1, False)))
    for bits in range(1, planes):
        name = f"plane{bits}"
        sent = even if bits % 2 == 0 else odd
        direct = moved(sent, lambda x, p, y, c, bits=bits: (x, p ^ bits, y ^ x ^ c, c))
        pieces.append((name, direct, (bits, 0, True)))
        name = f"cross{bits}"
        pieces.append((name, moved(direct, lambda x, p, y, c: (1 - x, p, y, c)), (bits, 1, True)))
    places = [(array, place + (0,)) for _, array, place in pieces]
    for name, array, place in pieces:
        places.append((moved(array, lambda x, p, y, c: (x, p, y, 1 - c)), place + (1,)))
    return places


def all_memory(kept, sent):
    devices = lax.axis_size("frame")
    held = jnp.stack([kept, hop(sent, 0)])
    for bit in range(1, devices.bit_length() - 1):
        half = held.shape[1] // 2
        held = jnp.concatenate([held[:, :half], hop(held[:, half:], bit)])
    keys, values = held[:, 0, :, 0, :], held[:, 0, :, 1, :]
    return keys.reshape(-1, keys.shape[-1]), values.reshape(-1, values.shape[-1])


def hop(array, bit):
    return lax.ppermute(array, "frame", [(i, i ^ 1 << bit) for i in range(lax.axis_size("frame"))])


def all_tokens(latent):
    other = moved(latent, lambda x, p, y, c: (x, p, y, 1 - c) if c != p % 2 else None)
    block = jnp.concatenate([latent, other])
    near = moved(block, lambda x, p, y, c: (x, p, 1 - y, c) if c == p % 2 else None)
    far = moved(block, lambda x, p, y, c: (x, p ^ 1, y, c) if c == p % 2 else None)
    far_near = moved(far, lambda x, p, y, c: (x, p, 1 - y, c) if c != p % 2 else None)
    return block, near, far, far_near


def late_plane(devices):
    return devices // 4 - 1


def piece_start(place, shard_rows, plane_number):
    x, _, _, y, c = here()
    _, y_bits, with_x, c_bits = place
    from_y, from_c = flipped(y, y_bits), flipped(c, c_bits)
    if with_x:
        from_y = joined_bits(joined_bits(from_y, x), from_c)
    return pl.multiple_of((plane_number * 4 + from_y * 2 + from_c) * shard_rows, 16)


def gather_pieces(piece_refs, places, first_plane, weights, sem):
    copies = []
    for number, (ref, place) in enumerate(zip(piece_refs, places)):
        start = piece_start(place, ref.shape[0], place[0] - first_plane)
        copies.append(pltpu.make_async_copy(ref, weights.at[pl.ds(start, ref.shape[0])], sem.at[number]))
        copies[-1].start()
    return copies


def store_normed(current, rows, inverse, gain_ref, normed):
    _, _, plane, _, _ = here()
    planes = lax.axis_size("frame") // 4
    span = current.shape[1] // planes
    for bits in range(planes):
        spot = columns(flipped(plane, bits), span)
        widened = current[rows, spot].astype(jnp.float32)
        normed[rows, bits * span : (bits + 1) * span] = (widened * inverse * gain_ref[0:1, spot]).astype(normed.dtype)


BLOCK = 32


def prepare_kernel(extra_ref, block, near, far, far_near, current, normed, token_sem):
    _, _, plane, y, c = here()
    chip_rows = block.shape[0]
    at_home = plane % 2 == c

    def token_copies(first, second):
        return (
            pltpu.make_async_copy(first, current.at[pl.ds(y * chip_rows, chip_rows)], token_sem.at[0]),
            pltpu.make_async_copy(second, current.at[pl.ds((1 - y) * chip_rows, chip_rows)], token_sem.at[1]),
        )

    @pl.when(at_home)
    def _():
        for copy in token_copies(block, near):
            copy.start()

    @pl.when(jnp.logical_not(at_home))
    def _():
        for copy in token_copies(far, far_near):
            copy.start()

    for copy in token_copies(block, near):
        copy.wait()

    @pl.loop(0, current.shape[0] // BLOCK)
    def _(number):
        rows = pl.ds(pl.multiple_of(number * BLOCK, BLOCK), BLOCK)
        widened = current[rows, :].astype(jnp.float32)
        inverse = lax.rsqrt(jnp.mean(widened * widened, axis=-1, keepdims=True) + 1e-06)
        store_normed(current, rows, inverse, extra_ref, normed)


def project_kernel(places, *refs):
    normed = refs[0]
    piece_refs = refs[1 : 1 + len(places)]
    out, weights, sem = refs[1 + len(places) :]
    for copy in gather_pieces(piece_refs, places, 0, weights, sem):
        copy.wait()
    out[...] = jnp.dot(normed[:, : weights.shape[0]], weights[...], preferred_element_type=jnp.float32)


def assemble_kernel(places, *refs):
    for copy in gather_pieces(refs[:-2], places, 0, refs[-2], refs[-1]):
        copy.wait()


def attend_heads(projected, key_ref, value_ref, extra_ref, attended, head_count):
    width = projected.shape[1] // 3
    head_size = width // head_count
    scale_dot = 1.0 / math.sqrt(head_size)
    mem_rows = key_ref.shape[0]
    live = extra_ref[3:4, :mem_rows] > 0.5
    contract_last = (((1,), (1,)), ((), ()))
    frame_rows = projected.shape[0]
    half = frame_rows // 2
    for head in range(head_count):
        span = slice(head * head_size, (head + 1) * head_size)
        keys = projected[:, width + head * head_size : width + (head + 1) * head_size]
        values = projected[:, 2 * width + head * head_size : 2 * width + (head + 1) * head_size]
        for start in range(0, frame_rows, half):
            queries = projected[start : start + half, span]
            frame_scores = (
                lax.dot_general(queries, keys, contract_last, preferred_element_type=jnp.float32) * scale_dot
            )
            mem_scores = (
                lax.dot_general(queries, key_ref[:, span], contract_last, preferred_element_type=jnp.float32)
                * scale_dot
            )
            mem_scores = jnp.where(live, mem_scores, -1e30)
            largest = jnp.maximum(
                jnp.max(frame_scores, axis=-1, keepdims=True), jnp.max(mem_scores, axis=-1, keepdims=True)
            )
            frame_weights = jnp.exp(frame_scores - largest)
            mem_weights = jnp.exp(mem_scores - largest)
            denominator = jnp.sum(frame_weights, axis=-1, keepdims=True) + jnp.sum(
                mem_weights, axis=-1, keepdims=True
            )
            blended = jnp.dot(
                frame_weights.astype(jnp.bfloat16), values, preferred_element_type=jnp.float32
            ) + jnp.dot(mem_weights.astype(jnp.bfloat16), value_ref[:, span], preferred_element_type=jnp.float32)
            attended[start : start + half, span] = (blended / denominator).astype(attended.dtype)


def step_kernel(places, first_plane, head_count, extra_ref, key_ref, value_ref, normed, part_ref, *refs):
    piece_refs = refs[: len(places)]
    attended, weights, projected, sem = refs[len(places) :]
    for copy in gather_pieces(piece_refs, places, first_plane, weights, sem):
        copy.wait()
    early = normed.shape[1] - weights.shape[0]
    projected[...] = (
        part_ref[...] + jnp.dot(normed[:, early:], weights[...], preferred_element_type=jnp.float32)
    ).astype(projected.dtype)
    attend_heads(projected, key_ref, value_ref, extra_ref, attended, head_count)


def last_step_kernel(
    update_places, head_count, extra_ref, key_ref, value_ref, current_ref, weights, first_part, second_part, third_part,
    fourth_part, keep, first, second, third, fourth, current, normed, projected, attended,
):
    _, _, plane, y, c = here()
    width = first_part.shape[1]
    at_home = plane % 2 == c

    @pl.loop(0, current.shape[0] // BLOCK)
    def _(number):
        rows = pl.ds(pl.multiple_of(number * BLOCK, BLOCK), BLOCK)
        total = jnp.zeros((BLOCK, 1), jnp.float32)
        for part, (plane_bits, y_bits) in zip((first_part, second_part, third_part, fourth_part), update_places):
            spot = columns(quarter_of(flipped(plane, plane_bits), flipped(y, y_bits)), width)
            updated = (
                current_ref[rows, spot].astype(jnp.float32)
                + extra_ref[1:2, :width] * part[rows, :].astype(jnp.float32)
            ).astype(current.dtype)
            current[rows, spot] = updated
            widened = updated.astype(jnp.float32)
            total = total + jnp.sum(widened * widened, axis=-1, keepdims=True)
        inverse = lax.rsqrt(total / current.shape[1] + 1e-06)
        store_normed(current, rows, inverse, extra_ref, normed)

    projected[...] = jnp.dot(normed[...], weights[...], preferred_element_type=jnp.float32).astype(projected.dtype)
    attend_heads(projected, key_ref, value_ref, extra_ref, attended, head_count)
    spot = columns(quarter_of(plane, y), width)
    attended[...] = (
        current[:, spot].astype(jnp.float32) + extra_ref[2:3, :width] * attended[...].astype(jnp.float32)
    ).astype(attended.dtype)
    chip_rows = attended.shape[0] // 2
    rows = chip_rows // 2
    here_rows, there_rows = y * chip_rows, (1 - y) * chip_rows

    def part(start):
        return attended[pl.ds(pl.multiple_of(start, rows), rows), :]

    keep[...] = part(here_rows)
    fourth[...] = part(there_rows + rows)

    @pl.when(at_home)
    def _():
        first[...] = part(there_rows)
        second[...] = part(there_rows + rows)
        third[...] = part(here_rows + rows)

    @pl.when(jnp.logical_not(at_home))
    def _():
        first[...] = part(here_rows + rows)
        second[...] = part(here_rows)
        third[...] = part(there_rows)


MIB = 1024 * 1024


def kernel_call(kernel, out_shape, operands, anywhere, scratch_shapes, limit, flops):
    vectors = pl.BlockSpec(memory_space=pltpu.VMEM)
    free = pl.BlockSpec(memory_space=pl.ANY)
    moved_bytes = sum(operand.size * operand.dtype.itemsize for operand in operands)
    return pl.pallas_call(
        kernel,
        out_shape=out_shape,
        in_specs=[free if number in anywhere else vectors for number in range(len(operands))],
        out_specs=jax.tree.map(lambda _: vectors, out_shape),
        scratch_shapes=scratch_shapes,
        compiler_params=pltpu.CompilerParams(vmem_limit_bytes=limit),
        cost_estimate=pl.CostEstimate(flops=flops, transcendentals=0, bytes_accessed=moved_bytes),
    )(*operands)


def prepare(extra, tokens):
    frame = jax.ShapeDtypeStruct((2 * tokens[0].shape[0], tokens[0].shape[1]), tokens[0].dtype)
    return kernel_call(
        prepare_kernel, (frame, frame), (extra, *tokens), range(1, 5), [pltpu.SemaphoreType.DMA((2,))],
        8 * MIB, 0,
    )


def project(normed, pieces):
    rows, width = pieces[0][0].shape
    depth = rows * len(pieces)
    return kernel_call(
        functools.partial(project_kernel, tuple(place for _, place in pieces)),
        jax.ShapeDtypeStruct((normed.shape[0], width), jnp.float32),
        (normed, *[array for array, _ in pieces]),
        range(1, 1 + len(pieces)),
        [pltpu.VMEM((depth, width), normed.dtype), pltpu.SemaphoreType.DMA((len(pieces),))],
        16 * MIB,
        2 * normed.shape[0] * depth * width,
    )


def assemble(pieces):
    rows, width = pieces[0][0].shape
    return kernel_call(
        functools.partial(assemble_kernel, tuple(place for _, place in pieces)),
        jax.ShapeDtypeStruct((rows * len(pieces), width), pieces[0][0].dtype),
        [array for array, _ in pieces],
        range(len(pieces)),
        [pltpu.SemaphoreType.DMA((len(pieces),))],
        8 * MIB,
        0,
    )


def step(extra, keys, values, normed, part, pieces):
    rows, width = pieces[0][0].shape
    depth = rows * len(pieces)
    frame_rows = normed.shape[0]
    return kernel_call(
        functools.partial(step_kernel, tuple(place for _, place in pieces), pieces[0][1][0], HEADS // SPATIAL),
        jax.ShapeDtypeStruct((frame_rows, width // 3), normed.dtype),
        (extra, keys, values, normed, part, *[array for array, _ in pieces]),
        range(5, 5 + len(pieces)),
        [
            pltpu.VMEM((depth, width), normed.dtype),
            pltpu.VMEM((frame_rows, width), normed.dtype),
            pltpu.SemaphoreType.DMA((len(pieces),)),
        ],
        16 * MIB,
        2 * frame_rows * width * (depth + frame_rows),
    )


def last_step(extra, keys, values, current, weights, updates):
    frame_rows, features = current.shape
    width = weights.shape[1] // 3
    share = jax.ShapeDtypeStruct((frame_rows // 4, width), current.dtype)
    return kernel_call(
        functools.partial(last_step_kernel, tuple(place for _, place in updates), HEADS // SPATIAL),
        (share,) * 5,
        (extra, keys, values, current, weights, *[array for array, _ in updates]),
        (),
        [
            pltpu.VMEM((frame_rows, features), current.dtype),
            pltpu.VMEM((frame_rows, features), current.dtype),
            pltpu.VMEM((frame_rows, 3 * width), current.dtype),
            pltpu.VMEM((frame_rows, width), current.dtype),
        ],
        16 * MIB,
        2 * frame_rows * 3 * width * (features + frame_rows),
    )


def join_kernel(keep, first, second, third, fourth, out):
    _, _, plane, y, c = here()
    low = plane % 2
    width = keep.shape[1]

    def put(ref, plane_low, at_y):
        out[:, columns(plane_low * 2 + at_y, width)] = ref[...]

    @pl.when(low == c)
    def _():
        put(keep, low, y)
        put(first, low, 1 - y)
        put(second, 1 - low, y)
        put(third, 1 - low, 1 - y)

    @pl.when(low != c)
    def _():
        put(first, 1 - low, y)
        put(second, low, 1 - y)
        put(third, low, y)
        put(fourth, 1 - low, 1 - y)


def joined(keep, first, second, third, fourth):
    def at_home(p, c):
        return c == p % 2

    first = moved(first, lambda x, p, y, c: (x, p, 1 - y, c) if at_home(p, c) else (x, p ^ 1, y, 1 - c))
    second = moved(second, lambda x, p, y, c: (x, p, 1 - y, 1 - c) if at_home(p, c) else (x, p ^ 1, y, c))
    third = moved(third, lambda x, p, y, c: (x, p, y, 1 - c) if at_home(p, c) else (x, p ^ 1, 1 - y, c))
    fourth = moved(fourth, lambda x, p, y, c: None if at_home(p, c) else (x, p ^ 1, 1 - y, 1 - c))
    rows, width = keep.shape
    return kernel_call(
        join_kernel,
        jax.ShapeDtypeStruct((rows, width * SPATIAL), keep.dtype),
        (keep, first, second, third, fourth),
        (),
        [],
        4 * MIB,
        0,
    )


def small_operands(norm_gain, step_scale, counts, entries):
    features = norm_gain.shape[0]
    _, _, plane, _, c = here()
    live = jnp.arange(features, dtype=jnp.int32) % entries < counts[(plane // 2) * 2 + c]
    scales = [jnp.full((features,), step_scale[number]) for number in range(STEPS)]
    return jnp.stack([norm_gain, *scales, live.astype(jnp.float32)])


def paired_planes(
    latent, norm_gain, w_query, w_key, w_value, mem_cache, intersection, counts, slot_of, step_scale
):
    late = late_plane(lax.axis_size("frame"))
    pieces = sorted(all_pieces(*pack_weights(w_query, w_key, w_value)), key=lambda piece: piece[1][0])
    tokens = all_tokens(latent)
    keys, values = all_memory(*pack_memory(mem_cache, intersection, slot_of))
    extra = small_operands(norm_gain, step_scale, counts, intersection.shape[1])
    current, normed = prepare(extra, tokens)
    part = project(normed, [piece for piece in pieces if piece[1][0] < late])
    attended = step(extra, keys, values, normed, part, [piece for piece in pieces if piece[1][0] == late])
    updates = [
        (attended, (0, 0)),
        (moved(attended, lambda x, p, y, c: (x, p ^ 1, 1 - y, c)), (1, 1)),
        (moved(attended, lambda x, p, y, c: (x, p ^ 1, y, c)), (1, 0)),
        (moved(attended, lambda x, p, y, c: (x, p, 1 - y, c)), (0, 1)),
    ]
    shares = last_step(extra, keys, values, current, assemble(pieces), updates)
    return joined(*shares)


def fits_paired_planes(latent, norm_gain, w_query, w_key, w_value, mem_cache, *_):
    devices = lax.axis_size("frame")
    planes = devices // SPATIAL
    return (
        lax.axis_size("groups") == 2
        and devices == planes * SPATIAL
        and planes >= 2
        and planes & (planes - 1) == 0
        and w_query.shape[0] % 16 == 0
        and mem_cache.shape[1] == 1
    )


def from_partner(array, axis, bit):
    return lax.ppermute(array, axis, [(i, i ^ 1 << bit) for i in range(lax.axis_size(axis))])


def in_order(mine, theirs, upper, axis_dim):
    low_first = jnp.concatenate([mine, theirs], axis=axis_dim)
    high_first = jnp.concatenate([theirs, mine], axis=axis_dim)
    return jnp.where(upper, high_first, low_first)


def attend(queries, frame_pair, mem_keys, mem_values, live_keys, head_count):
    tok_rows, feature_width = queries.shape
    head_size = feature_width // head_count
    scale_dot = 1.0 / math.sqrt(head_size)
    q_heads = queries.reshape(tok_rows, head_count, head_size)
    k_heads = frame_pair[0].reshape(-1, head_count, head_size)
    v_heads = frame_pair[1].reshape(-1, head_count, head_size)
    frame_scores = (
        jnp.einsum("thd,khd->htk", q_heads, k_heads, preferred_element_type=jnp.float32) * scale_dot
    )
    remote_scores = (
        jnp.einsum("thd,khd->htk", q_heads, mem_keys, preferred_element_type=jnp.float32)
        * scale_dot
    )
    remote_scores = jnp.where(live_keys[None, None, :], remote_scores, -1e30)
    largest = jnp.maximum(
        jnp.max(frame_scores, axis=-1, keepdims=True),
        jnp.max(remote_scores, axis=-1, keepdims=True),
    )
    frame_weights = jnp.exp(frame_scores - largest)
    remote_weights = jnp.exp(remote_scores - largest)
    denominator = jnp.sum(frame_weights, axis=-1) + jnp.sum(remote_weights, axis=-1)
    blended = jnp.einsum(
        "htk,khd->thd",
        frame_weights.astype(jnp.bfloat16),
        v_heads,
        preferred_element_type=jnp.float32,
    )
    blended = blended + jnp.einsum(
        "htk,khd->thd",
        remote_weights.astype(jnp.bfloat16),
        mem_values,
        preferred_element_type=jnp.float32,
    )
    blended = blended / jnp.transpose(denominator)[:, :, None]
    return blended.reshape(tok_rows, feature_width).astype(jnp.bfloat16)


def rms_normed(current, norm_gain):
    widened = current.astype(jnp.float32)
    inverse = lax.rsqrt(jnp.mean(widened * widened, axis=-1, keepdims=True) + 1e-06)
    return (widened, (widened * inverse * norm_gain).astype(jnp.bfloat16))


def separate_frames(
    latent, norm_gain, w_query, w_key, w_value, mem_cache, intersection, counts, slot_of, step_scale
):
    devices = lax.axis_size("frame")
    position = lax.axis_index("frame")
    frame_index = position // SPATIAL
    doublings = SPATIAL.bit_length() - 1
    target_frame = jnp.arange(devices, dtype=jnp.int32) // SPATIAL
    current = latent
    feature_width = latent.shape[1]
    share_width = feature_width // SPATIAL
    head_share = HEADS // SPATIAL

    def column_pieces(weight):
        row_count = weight.shape[0]
        split_cols = jnp.transpose(weight.reshape(row_count, SPATIAL, share_width), (1, 0, 2))
        return jnp.tile(split_cols, (devices // SPATIAL, 1, 1))

    own_query, own_key, own_value = (
        lax.all_to_all(column_pieces(w_query), "frame", split_axis=0, concat_axis=1, tiled=True),
        lax.all_to_all(column_pieces(w_key), "frame", split_axis=0, concat_axis=1, tiled=True),
        lax.all_to_all(column_pieces(w_value), "frame", split_axis=0, concat_axis=1, tiled=True),
    )
    own_query, own_key, own_value = (own_query[0], own_key[0], own_value[0])
    listed = mem_cache[slot_of[intersection[target_frame]]]
    list_len = listed.shape[1]
    local_mem = listed.shape[2]
    grouped = listed.reshape(
        devices // SPATIAL, SPATIAL, list_len, local_mem, 2, SPATIAL, share_width
    )
    diagonal_part = jnp.diagonal(grouped, axis1=1, axis2=5)
    outgoing = jnp.moveaxis(diagonal_part, -1, 1).reshape(
        devices, list_len, local_mem, 2, share_width
    )
    fetched = lax.all_to_all(outgoing, "frame", split_axis=0, concat_axis=2, tiled=True)[0]
    mem_len = fetched.shape[1]
    mem_keys = fetched[:, :, 0, :].reshape(list_len * mem_len, head_share, HS)
    mem_values = fetched[:, :, 1, :].reshape(list_len * mem_len, head_share, HS)
    live_keys = jnp.arange(list_len * mem_len, dtype=jnp.int32) // mem_len < counts[frame_index]
    tok_rows = latent.shape[0]
    for step_index in range(STEPS):
        widened, normed = rms_normed(current, norm_gain)
        gathered = normed
        for bit_index in range(doublings):
            partner = from_partner(gathered, "frame", bit_index)
            gathered = in_order(gathered, partner, position >> bit_index & 1 == 1, 0)
        queries = jnp.dot(gathered, own_query, preferred_element_type=jnp.float32).astype(
            jnp.bfloat16
        )
        keys_frame = jnp.dot(gathered, own_key, preferred_element_type=jnp.float32).astype(
            jnp.bfloat16
        )
        values_frame = jnp.dot(gathered, own_value, preferred_element_type=jnp.float32).astype(
            jnp.bfloat16
        )
        frame_pair = jnp.stack([keys_frame, values_frame])
        attended = attend(queries, frame_pair, mem_keys, mem_values, live_keys, head_share)
        blocks = attended.reshape(SPATIAL, tok_rows, share_width)[:, None]
        for bit_index in range(doublings):
            upper = position >> bit_index & 1 == 1
            dest_count = blocks.shape[0]
            paired = blocks.reshape((dest_count // 2, 2) + blocks.shape[1:])
            kept = jnp.where(upper, paired[:, 1], paired[:, 0])
            sent = jnp.where(upper, paired[:, 0], paired[:, 1])
            arrived = from_partner(sent, "frame", bit_index)
            blocks = in_order(kept, arrived, upper, 1)
        joined = jnp.transpose(blocks[0], (1, 0, 2)).reshape(tok_rows, feature_width)
        current = (widened + step_scale[step_index] * joined.astype(jnp.float32)).astype(
            jnp.bfloat16
        )
    return current


def per_device(*arguments):
    return (paired_planes if fits_paired_planes(*arguments) else separate_frames)(*arguments)


def solution(mesh):
    placed = (
        P(("groups", "frame"), None),
        P(),
        P("frame", None),
        P("frame", None),
        P("frame", None),
        P("groups", "frame", None, None),
        P("groups", None),
        P("groups"),
        P("groups"),
        P(),
    )
    return jax.shard_map(
        per_device,
        mesh=mesh,
        in_specs=placed,
        out_specs=P(("groups", "frame"), None),
        check_vma=False,
    )
```

```python
import functools
import math

import jax
import jax.numpy as jnp
from jax import lax
from jax.experimental import pallas as pl
from jax.experimental.pallas import tpu as pltpu
from jax.sharding import PartitionSpec as P


HEADS = 12
HS = 128
SPATIAL = 4
STEPS = 2
AXES = ("groups", "frame")


def coords(index):
    return index // 4, (index // 2) % 2, index % 2


def quarter_of(plane, y):
    return (plane % 2) * 2 + y


def moved(array, target):
    devices = lax.axis_size("frame")
    pairs = []
    for x in range(lax.axis_size("groups")):
        for index in range(devices):
            place = target(x, *coords(index))
            if place is not None:
                to_x, to_plane, to_y, to_c = place
                pairs.append((x * devices + index, to_x * devices + to_plane * 4 + to_y * 2 + to_c))
    return lax.ppermute(array, AXES, pairs)


def here():
    x = lax.axis_index("groups")
    index = lax.axis_index("frame")
    plane = index // 4
    rest = index - plane * 4
    y = rest // 2
    return x, index, plane, y, rest - y * 2


def flipped(value, bits):
    out = value
    bit = 1
    while bit <= bits:
        if bits & bit:
            out = out + bit - 2 * bit * ((value // bit) % 2)
        bit *= 2
    return out


def joined_bits(one, other):
    return one + other - 2 * one * other


def columns(quarter, width):
    return pl.ds(pl.multiple_of(quarter * width, 128), width)


def pack_weights_kernel(
    w_query, w_key, w_value, own_ref, beside_ref, even_ref, odd_ref, rows, row_sem, out_sem
):
    x, _, plane, y, c = here()
    width = own_ref.shape[1] // 3
    reads = []
    for number, weight in enumerate((w_query, w_key, w_value)):
        reads.append(pltpu.make_async_copy(weight, rows.at[number], row_sem.at[number]))
        reads[-1].start()
    across = joined_bits(joined_bits(x, y), c)
    low = plane % 2
    quarters = (low * 2 + across, (1 - low) * 2 + across, low * 2 + 1 - y, quarter_of(plane, y))
    gives = []
    for number, read in enumerate(reads):
        read.wait()
        for place, (quarter, out) in enumerate(zip(quarters, (even_ref, odd_ref, beside_ref, own_ref))):
            gives.append(
                pltpu.make_async_copy(
                    rows.at[number, :, columns(quarter, width)],
                    out.at[:, pl.ds(number * width, width)],
                    out_sem.at[number, place],
                )
            )
            gives[-1].start()
    for give in gives:
        give.wait()


def pack_weights(w_query, w_key, w_value):
    shard_rows, features = w_query.shape
    piece = jax.ShapeDtypeStruct((shard_rows, 3 * (features // SPATIAL)), w_query.dtype)
    anywhere = pl.BlockSpec(memory_space=pl.ANY)
    held = pl.BlockSpec(memory_space=pltpu.HBM)
    return pl.pallas_call(
        pack_weights_kernel,
        out_shape=(piece,) * 4,
        in_specs=[held] * 3,
        out_specs=(anywhere,) * 4,
        scratch_shapes=[
            pltpu.VMEM((3, shard_rows, features), w_query.dtype),
            pltpu.SemaphoreType.DMA((3,)),
            pltpu.SemaphoreType.DMA((3, 4)),
        ],
        name="pack_weights",
    )(w_query, w_key, w_value)


def pack_memory_kernel(
    list_hbm, slot_hbm, count_hbm, scale_hbm, gain_hbm, mem_ref, kept_ref, sent_ref, extra_ref,
    list_ref, slot_ref, count_ref, scale_ref, stored, extra, scalar_sem, mem_sem, give_sem,
):
    _, index, plane, _, c = here()
    devices = lax.axis_size("frame")
    frames, entries = list_ref.shape
    width = kept_ref.shape[-1]
    scalars = [
        pltpu.make_async_copy(list_hbm, list_ref, scalar_sem.at[0]),
        pltpu.make_async_copy(slot_hbm, slot_ref, scalar_sem.at[1]),
        pltpu.make_async_copy(count_hbm, count_ref, scalar_sem.at[2]),
        pltpu.make_async_copy(scale_hbm, scale_ref, scalar_sem.at[3]),
        pltpu.make_async_copy(gain_hbm, extra.at[pl.ds(0, 1)], scalar_sem.at[4]),
    ]
    for copy in scalars:
        copy.start()
    for copy in scalars[:2]:
        copy.wait()
    picks = []
    for frame in range(frames):
        for entry in range(entries):
            number = frame * entries + entry
            row = slot_ref[list_ref[frame, entry]]
            picks.append(pltpu.make_async_copy(mem_ref.at[row, 0], stored.at[number], mem_sem.at[number]))
            picks[-1].start()
    for copy in scalars[2:]:
        copy.wait()
    row = (1, extra.shape[1])
    for number in range(STEPS):
        extra[1 + number : 2 + number, :] = jnp.full(row, scale_ref[number], jnp.float32)
    live = lax.broadcasted_iota(jnp.int32, row, 1) % entries < count_ref[(plane // 2) * 2 + c]
    extra[1 + STEPS : 2 + STEPS, :] = jnp.where(live, 1.0, 0.0)
    for pick in picks:
        pick.wait()
    gives = [pltpu.make_async_copy(extra, extra_ref, scalar_sem.at[5])]
    gives[0].start()
    bits = devices.bit_length() - 1
    for away in range(devices):
        target = flipped(index, away)
        to_plane, to_y, to_c = coords(target)
        to_frame = (to_plane // 2) * 2 + to_c
        place = 0
        for bit in range(1, bits):
            place = place * 2 + (away >> bit & 1)
        out = sent_ref if away & 1 else kept_ref
        gives.append(
            pltpu.make_async_copy(
                stored.at[pl.ds(to_frame * entries, entries), :, columns(quarter_of(to_plane, to_y), width)],
                out.at[place],
                give_sem.at[away],
            )
        )
        gives[-1].start()
    for give in gives:
        give.wait()


def pack_memory(mem_cache, intersection, slot_of, counts, step_scale, norm_gain):
    devices = lax.axis_size("frame")
    features = mem_cache.shape[-1]
    frames, entries = intersection.shape
    half = jax.ShapeDtypeStruct((devices // 2, entries, 2, features // SPATIAL), mem_cache.dtype)
    anywhere = pl.BlockSpec(memory_space=pl.ANY)
    held = pl.BlockSpec(memory_space=pltpu.HBM)
    return pl.pallas_call(
        pack_memory_kernel,
        out_shape=(half, half, jax.ShapeDtypeStruct((2 + STEPS, features), jnp.float32)),
        in_specs=[held] * 6,
        out_specs=(anywhere,) * 3,
        scratch_shapes=[
            pltpu.SMEM(intersection.shape, intersection.dtype),
            pltpu.SMEM(slot_of.shape, slot_of.dtype),
            pltpu.SMEM(counts.shape, counts.dtype),
            pltpu.SMEM(step_scale.shape, step_scale.dtype),
            pltpu.VMEM((frames * entries, 2, features), mem_cache.dtype),
            pltpu.VMEM((2 + STEPS, features), jnp.float32),
            pltpu.SemaphoreType.DMA((6,)),
            pltpu.SemaphoreType.DMA((frames * entries,)),
            pltpu.SemaphoreType.DMA((devices,)),
        ],
        name="pack_memory",
    )(intersection, slot_of, counts, step_scale, norm_gain.reshape(1, -1), mem_cache)


def all_pieces(own, beside, even, odd):
    planes = lax.axis_size("frame") // 4
    pieces = [("own", own, (0, 0, False))]
    pieces.append(("near", moved(beside, lambda x, p, y, c: (x, p, 1 - y, c)), (0, 1, False)))
    for bits in range(1, planes):
        name = f"plane{bits}"
        sent = even if bits % 2 == 0 else odd
        direct = moved(sent, lambda x, p, y, c, bits=bits: (x, p ^ bits, y ^ x ^ c, c))
        pieces.append((name, direct, (bits, 0, True)))
        name = f"cross{bits}"
        pieces.append((name, moved(direct, lambda x, p, y, c: (1 - x, p, y, c)), (bits, 1, True)))
    places = [(array, place + (0,)) for _, array, place in pieces]
    for name, array, place in pieces:
        places.append((moved(array, lambda x, p, y, c: (x, p, y, 1 - c)), place + (1,)))
    return places


def all_memory(kept, sent):
    devices = lax.axis_size("frame")
    held = jnp.stack([kept, hop(sent, 0)])
    for bit in range(1, devices.bit_length() - 1):
        half = held.shape[1] // 2
        held = jnp.concatenate([held[:, :half], hop(held[:, half:], bit)])
    keys, values = held[:, 0, :, 0, :], held[:, 0, :, 1, :]
    return keys.reshape(-1, keys.shape[-1]), values.reshape(-1, values.shape[-1])


def hop(array, bit):
    return lax.ppermute(array, "frame", [(i, i ^ 1 << bit) for i in range(lax.axis_size("frame"))])


def all_tokens(latent):
    other = moved(latent, lambda x, p, y, c: (x, p, y, 1 - c) if c != p % 2 else None)
    block = jnp.concatenate([latent, other])
    near = moved(block, lambda x, p, y, c: (x, p, 1 - y, c) if c == p % 2 else None)
    far = moved(block, lambda x, p, y, c: (x, p ^ 1, y, c) if c == p % 2 else None)
    far_near = moved(far, lambda x, p, y, c: (x, p, 1 - y, c) if c != p % 2 else None)
    return block, near, far, far_near


def late_plane(devices):
    return devices // 4 - 1


def piece_start(place, shard_rows, plane_number):
    x, _, _, y, c = here()
    _, y_bits, with_x, c_bits = place
    from_y, from_c = flipped(y, y_bits), flipped(c, c_bits)
    if with_x:
        from_y = joined_bits(joined_bits(from_y, x), from_c)
    return pl.multiple_of((plane_number * 4 + from_y * 2 + from_c) * shard_rows, 16)


def gather_pieces(piece_refs, places, first_plane, weights):
    for ref, place in zip(piece_refs, places):
        start = piece_start(place, ref.shape[0], place[0] - first_plane)
        weights[pl.ds(start, ref.shape[0]), :] = ref[...]


def store_normed(current, rows, inverse, gain_ref, normed):
    _, _, plane, _, _ = here()
    planes = lax.axis_size("frame") // 4
    span = current.shape[1] // planes
    for bits in range(planes):
        spot = columns(flipped(plane, bits), span)
        widened = current[rows, spot].astype(jnp.float32)
        normed[rows, bits * span : (bits + 1) * span] = (widened * inverse * gain_ref[0:1, spot]).astype(normed.dtype)


BLOCK = 32


def prepare_kernel(extra_ref, block, near, far, far_near, extra, current, normed, token_sem):
    _, _, plane, y, c = here()
    chip_rows = block.shape[0]
    at_home = plane % 2 == c
    extra_copy = pltpu.make_async_copy(extra_ref, extra, token_sem.at[2])
    extra_copy.start()

    def token_copies(first, second):
        return (
            pltpu.make_async_copy(first, current.at[pl.ds(y * chip_rows, chip_rows)], token_sem.at[0]),
            pltpu.make_async_copy(second, current.at[pl.ds((1 - y) * chip_rows, chip_rows)], token_sem.at[1]),
        )

    @pl.when(at_home)
    def _():
        for copy in token_copies(block, near):
            copy.start()

    @pl.when(jnp.logical_not(at_home))
    def _():
        for copy in token_copies(far, far_near):
            copy.start()

    for copy in token_copies(block, near):
        copy.wait()
    extra_copy.wait()

    @pl.loop(0, current.shape[0] // BLOCK)
    def _(number):
        rows = pl.ds(pl.multiple_of(number * BLOCK, BLOCK), BLOCK)
        widened = current[rows, :].astype(jnp.float32)
        inverse = lax.rsqrt(jnp.mean(widened * widened, axis=-1, keepdims=True) + 1e-06)
        store_normed(current, rows, inverse, extra, normed)


def project_kernel(places, *refs):
    normed = refs[0]
    piece_refs = refs[1 : 1 + len(places)]
    out, weights = refs[1 + len(places) :]
    gather_pieces(piece_refs, places, 0, weights)
    out[...] = jnp.dot(normed[:, : weights.shape[0]], weights[...], preferred_element_type=jnp.float32)


def assemble_kernel(places, *refs):
    gather_pieces(refs[:-1], places, 0, refs[-1])


def attend_heads(projected, key_ref, value_ref, extra_ref, attended, head_count):
    width = projected.shape[1] // 3
    head_size = width // head_count
    scale_dot = 1.0 / math.sqrt(head_size)
    mem_rows = key_ref.shape[0]
    live = extra_ref[3:4, :mem_rows] > 0.5
    contract_last = (((1,), (1,)), ((), ()))
    frame_rows = projected.shape[0]
    half = frame_rows // 2
    for head in range(head_count):
        span = slice(head * head_size, (head + 1) * head_size)
        keys = projected[:, width + head * head_size : width + (head + 1) * head_size]
        values = projected[:, 2 * width + head * head_size : 2 * width + (head + 1) * head_size]
        for start in range(0, frame_rows, half):
            queries = projected[start : start + half, span]
            frame_scores = (
                lax.dot_general(queries, keys, contract_last, preferred_element_type=jnp.float32) * scale_dot
            )
            mem_scores = (
                lax.dot_general(queries, key_ref[:, span], contract_last, preferred_element_type=jnp.float32)
                * scale_dot
            )
            mem_scores = jnp.where(live, mem_scores, -1e30)
            largest = jnp.maximum(
                jnp.max(frame_scores, axis=-1, keepdims=True), jnp.max(mem_scores, axis=-1, keepdims=True)
            )
            frame_weights = jnp.exp(frame_scores - largest)
            mem_weights = jnp.exp(mem_scores - largest)
            denominator = jnp.sum(frame_weights, axis=-1, keepdims=True) + jnp.sum(
                mem_weights, axis=-1, keepdims=True
            )
            blended = jnp.dot(
                frame_weights.astype(jnp.bfloat16), values, preferred_element_type=jnp.float32
            ) + jnp.dot(mem_weights.astype(jnp.bfloat16), value_ref[:, span], preferred_element_type=jnp.float32)
            attended[start : start + half, span] = (blended / denominator).astype(attended.dtype)


def step_kernel(places, first_plane, head_count, extra_ref, key_ref, value_ref, normed, part_ref, *refs):
    piece_refs = refs[: len(places)]
    attended, weights, projected = refs[len(places) :]
    gather_pieces(piece_refs, places, first_plane, weights)
    early = normed.shape[1] - weights.shape[0]
    projected[...] = (
        part_ref[...] + jnp.dot(normed[:, early:], weights[...], preferred_element_type=jnp.float32)
    ).astype(projected.dtype)
    attend_heads(projected, key_ref, value_ref, extra_ref, attended, head_count)


def last_step_kernel(
    update_places, head_count, extra_ref, key_ref, value_ref, current_ref, weights, first_part, second_part, third_part,
    fourth_part, keep, first, second, third, fourth, current, normed, projected, attended,
):
    _, _, plane, y, c = here()
    width = first_part.shape[1]
    at_home = plane % 2 == c

    @pl.loop(0, current.shape[0] // BLOCK)
    def _(number):
        rows = pl.ds(pl.multiple_of(number * BLOCK, BLOCK), BLOCK)
        total = jnp.zeros((BLOCK, 1), jnp.float32)
        for part, (plane_bits, y_bits) in zip((first_part, second_part, third_part, fourth_part), update_places):
            spot = columns(quarter_of(flipped(plane, plane_bits), flipped(y, y_bits)), width)
            updated = (
                current_ref[rows, spot].astype(jnp.float32)
                + extra_ref[1:2, :width] * part[rows, :].astype(jnp.float32)
            ).astype(current.dtype)
            current[rows, spot] = updated
            widened = updated.astype(jnp.float32)
            total = total + jnp.sum(widened * widened, axis=-1, keepdims=True)
        inverse = lax.rsqrt(total / current.shape[1] + 1e-06)
        store_normed(current, rows, inverse, extra_ref, normed)

    projected[...] = jnp.dot(normed[...], weights[...], preferred_element_type=jnp.float32).astype(projected.dtype)
    attend_heads(projected, key_ref, value_ref, extra_ref, attended, head_count)
    spot = columns(quarter_of(plane, y), width)
    attended[...] = (
        current[:, spot].astype(jnp.float32) + extra_ref[2:3, :width] * attended[...].astype(jnp.float32)
    ).astype(attended.dtype)
    chip_rows = attended.shape[0] // 2
    rows = chip_rows // 2
    here_rows, there_rows = y * chip_rows, (1 - y) * chip_rows

    def part(start):
        return attended[pl.ds(pl.multiple_of(start, rows), rows), :]

    keep[...] = part(here_rows)
    fourth[...] = part(there_rows + rows)

    @pl.when(at_home)
    def _():
        first[...] = part(there_rows)
        second[...] = part(there_rows + rows)
        third[...] = part(here_rows + rows)

    @pl.when(jnp.logical_not(at_home))
    def _():
        first[...] = part(here_rows + rows)
        second[...] = part(here_rows)
        third[...] = part(there_rows)


MIB = 1024 * 1024


def kernel_call(kernel, out_shape, operands, anywhere, scratch_shapes, limit, flops):
    vectors = pl.BlockSpec(memory_space=pltpu.VMEM)
    free = pl.BlockSpec(memory_space=pl.ANY)
    moved_bytes = sum(operand.size * operand.dtype.itemsize for operand in operands)
    return pl.pallas_call(
        kernel,
        out_shape=out_shape,
        in_specs=[free if number in anywhere else vectors for number in range(len(operands))],
        out_specs=jax.tree.map(lambda _: vectors, out_shape),
        scratch_shapes=scratch_shapes,
        compiler_params=pltpu.CompilerParams(vmem_limit_bytes=limit),
        cost_estimate=pl.CostEstimate(flops=flops, transcendentals=0, bytes_accessed=moved_bytes),
    )(*operands)


def prepare(extra, tokens):
    frame = jax.ShapeDtypeStruct((2 * tokens[0].shape[0], tokens[0].shape[1]), tokens[0].dtype)
    return kernel_call(
        prepare_kernel,
        (jax.ShapeDtypeStruct(extra.shape, extra.dtype), frame, frame),
        (extra, *tokens),
        range(5),
        [pltpu.SemaphoreType.DMA((3,))],
        8 * MIB,
        0,
    )


def project(normed, pieces):
    rows, width = pieces[0][0].shape
    depth = rows * len(pieces)
    return kernel_call(
        functools.partial(project_kernel, tuple(place for _, place in pieces)),
        jax.ShapeDtypeStruct((normed.shape[0], width), jnp.float32),
        (normed, *[array for array, _ in pieces]),
        (),
        [pltpu.VMEM((depth, width), normed.dtype)],
        16 * MIB,
        2 * normed.shape[0] * depth * width,
    )


def assemble(pieces):
    rows, width = pieces[0][0].shape
    return kernel_call(
        functools.partial(assemble_kernel, tuple(place for _, place in pieces)),
        jax.ShapeDtypeStruct((rows * len(pieces), width), pieces[0][0].dtype),
        [array for array, _ in pieces],
        (),
        [],
        8 * MIB,
        0,
    )


def step(extra, keys, values, normed, part, pieces):
    rows, width = pieces[0][0].shape
    depth = rows * len(pieces)
    frame_rows = normed.shape[0]
    return kernel_call(
        functools.partial(step_kernel, tuple(place for _, place in pieces), pieces[0][1][0], HEADS // SPATIAL),
        jax.ShapeDtypeStruct((frame_rows, width // 3), normed.dtype),
        (extra, keys, values, normed, part, *[array for array, _ in pieces]),
        (),
        [pltpu.VMEM((depth, width), normed.dtype), pltpu.VMEM((frame_rows, width), normed.dtype)],
        16 * MIB,
        2 * frame_rows * width * (depth + frame_rows),
    )


def last_step(extra, keys, values, current, weights, updates):
    frame_rows, features = current.shape
    width = weights.shape[1] // 3
    share = jax.ShapeDtypeStruct((frame_rows // 4, width), current.dtype)
    return kernel_call(
        functools.partial(last_step_kernel, tuple(place for _, place in updates), HEADS // SPATIAL),
        (share,) * 5,
        (extra, keys, values, current, weights, *[array for array, _ in updates]),
        (),
        [
            pltpu.VMEM((frame_rows, features), current.dtype),
            pltpu.VMEM((frame_rows, features), current.dtype),
            pltpu.VMEM((frame_rows, 3 * width), current.dtype),
            pltpu.VMEM((frame_rows, width), current.dtype),
        ],
        16 * MIB,
        2 * frame_rows * 3 * width * (features + frame_rows),
    )


def join_kernel(keep, first, second, third, fourth, out):
    _, _, plane, y, c = here()
    low = plane % 2
    width = keep.shape[1]

    def put(ref, plane_low, at_y):
        out[:, columns(plane_low * 2 + at_y, width)] = ref[...]

    @pl.when(low == c)
    def _():
        put(keep, low, y)
        put(first, low, 1 - y)
        put(second, 1 - low, y)
        put(third, 1 - low, 1 - y)

    @pl.when(low != c)
    def _():
        put(first, 1 - low, y)
        put(second, low, 1 - y)
        put(third, low, y)
        put(fourth, 1 - low, 1 - y)


def joined(keep, first, second, third, fourth):
    def at_home(p, c):
        return c == p % 2

    first = moved(first, lambda x, p, y, c: (x, p, 1 - y, c) if at_home(p, c) else (x, p ^ 1, y, 1 - c))
    second = moved(second, lambda x, p, y, c: (x, p, 1 - y, 1 - c) if at_home(p, c) else (x, p ^ 1, y, c))
    third = moved(third, lambda x, p, y, c: (x, p, y, 1 - c) if at_home(p, c) else (x, p ^ 1, 1 - y, c))
    fourth = moved(fourth, lambda x, p, y, c: None if at_home(p, c) else (x, p ^ 1, 1 - y, 1 - c))
    rows, width = keep.shape
    return kernel_call(
        join_kernel,
        jax.ShapeDtypeStruct((rows, width * SPATIAL), keep.dtype),
        (keep, first, second, third, fourth),
        (),
        [],
        4 * MIB,
        0,
    )


def paired_planes(
    latent, norm_gain, w_query, w_key, w_value, mem_cache, intersection, counts, slot_of, step_scale
):
    late = late_plane(lax.axis_size("frame"))
    pieces = sorted(all_pieces(*pack_weights(w_query, w_key, w_value)), key=lambda piece: piece[1][0])
    tokens = all_tokens(latent)
    kept, sent, extra = pack_memory(mem_cache, intersection, slot_of, counts, step_scale, norm_gain)
    keys, values = all_memory(kept, sent)
    extra, current, normed = prepare(extra, tokens)
    part = project(normed, [piece for piece in pieces if piece[1][0] < late])
    attended = step(extra, keys, values, normed, part, [piece for piece in pieces if piece[1][0] == late])
    updates = [
        (attended, (0, 0)),
        (moved(attended, lambda x, p, y, c: (x, p ^ 1, 1 - y, c)), (1, 1)),
        (moved(attended, lambda x, p, y, c: (x, p ^ 1, y, c)), (1, 0)),
        (moved(attended, lambda x, p, y, c: (x, p, 1 - y, c)), (0, 1)),
    ]
    shares = last_step(extra, keys, values, current, assemble(pieces), updates)
    return joined(*shares)


def fits_paired_planes(latent, norm_gain, w_query, w_key, w_value, mem_cache, *_):
    devices = lax.axis_size("frame")
    planes = devices // SPATIAL
    return (
        lax.axis_size("groups") == 2
        and devices == planes * SPATIAL
        and planes >= 2
        and planes & (planes - 1) == 0
        and w_query.shape[0] % 16 == 0
        and mem_cache.shape[1] == 1
    )


def from_partner(array, axis, bit):
    return lax.ppermute(array, axis, [(i, i ^ 1 << bit) for i in range(lax.axis_size(axis))])


def in_order(mine, theirs, upper, axis_dim):
    low_first = jnp.concatenate([mine, theirs], axis=axis_dim)
    high_first = jnp.concatenate([theirs, mine], axis=axis_dim)
    return jnp.where(upper, high_first, low_first)


def attend(queries, frame_pair, mem_keys, mem_values, live_keys, head_count):
    tok_rows, feature_width = queries.shape
    head_size = feature_width // head_count
    scale_dot = 1.0 / math.sqrt(head_size)
    q_heads = queries.reshape(tok_rows, head_count, head_size)
    k_heads = frame_pair[0].reshape(-1, head_count, head_size)
    v_heads = frame_pair[1].reshape(-1, head_count, head_size)
    frame_scores = (
        jnp.einsum("thd,khd->htk", q_heads, k_heads, preferred_element_type=jnp.float32) * scale_dot
    )
    remote_scores = (
        jnp.einsum("thd,khd->htk", q_heads, mem_keys, preferred_element_type=jnp.float32)
        * scale_dot
    )
    remote_scores = jnp.where(live_keys[None, None, :], remote_scores, -1e30)
    largest = jnp.maximum(
        jnp.max(frame_scores, axis=-1, keepdims=True),
        jnp.max(remote_scores, axis=-1, keepdims=True),
    )
    frame_weights = jnp.exp(frame_scores - largest)
    remote_weights = jnp.exp(remote_scores - largest)
    denominator = jnp.sum(frame_weights, axis=-1) + jnp.sum(remote_weights, axis=-1)
    blended = jnp.einsum(
        "htk,khd->thd",
        frame_weights.astype(jnp.bfloat16),
        v_heads,
        preferred_element_type=jnp.float32,
    )
    blended = blended + jnp.einsum(
        "htk,khd->thd",
        remote_weights.astype(jnp.bfloat16),
        mem_values,
        preferred_element_type=jnp.float32,
    )
    blended = blended / jnp.transpose(denominator)[:, :, None]
    return blended.reshape(tok_rows, feature_width).astype(jnp.bfloat16)


def rms_normed(current, norm_gain):
    widened = current.astype(jnp.float32)
    inverse = lax.rsqrt(jnp.mean(widened * widened, axis=-1, keepdims=True) + 1e-06)
    return (widened, (widened * inverse * norm_gain).astype(jnp.bfloat16))


def separate_frames(
    latent, norm_gain, w_query, w_key, w_value, mem_cache, intersection, counts, slot_of, step_scale
):
    devices = lax.axis_size("frame")
    position = lax.axis_index("frame")
    frame_index = position // SPATIAL
    doublings = SPATIAL.bit_length() - 1
    target_frame = jnp.arange(devices, dtype=jnp.int32) // SPATIAL
    current = latent
    feature_width = latent.shape[1]
    share_width = feature_width // SPATIAL
    head_share = HEADS // SPATIAL

    def column_pieces(weight):
        row_count = weight.shape[0]
        split_cols = jnp.transpose(weight.reshape(row_count, SPATIAL, share_width), (1, 0, 2))
        return jnp.tile(split_cols, (devices // SPATIAL, 1, 1))

    own_query, own_key, own_value = (
        lax.all_to_all(column_pieces(w_query), "frame", split_axis=0, concat_axis=1, tiled=True),
        lax.all_to_all(column_pieces(w_key), "frame", split_axis=0, concat_axis=1, tiled=True),
        lax.all_to_all(column_pieces(w_value), "frame", split_axis=0, concat_axis=1, tiled=True),
    )
    own_query, own_key, own_value = (own_query[0], own_key[0], own_value[0])
    listed = mem_cache[slot_of[intersection[target_frame]]]
    list_len = listed.shape[1]
    local_mem = listed.shape[2]
    grouped = listed.reshape(
        devices // SPATIAL, SPATIAL, list_len, local_mem, 2, SPATIAL, share_width
    )
    diagonal_part = jnp.diagonal(grouped, axis1=1, axis2=5)
    outgoing = jnp.moveaxis(diagonal_part, -1, 1).reshape(
        devices, list_len, local_mem, 2, share_width
    )
    fetched = lax.all_to_all(outgoing, "frame", split_axis=0, concat_axis=2, tiled=True)[0]
    mem_len = fetched.shape[1]
    mem_keys = fetched[:, :, 0, :].reshape(list_len * mem_len, head_share, HS)
    mem_values = fetched[:, :, 1, :].reshape(list_len * mem_len, head_share, HS)
    live_keys = jnp.arange(list_len * mem_len, dtype=jnp.int32) // mem_len < counts[frame_index]
    tok_rows = latent.shape[0]
    for step_index in range(STEPS):
        widened, normed = rms_normed(current, norm_gain)
        gathered = normed
        for bit_index in range(doublings):
            partner = from_partner(gathered, "frame", bit_index)
            gathered = in_order(gathered, partner, position >> bit_index & 1 == 1, 0)
        queries = jnp.dot(gathered, own_query, preferred_element_type=jnp.float32).astype(
            jnp.bfloat16
        )
        keys_frame = jnp.dot(gathered, own_key, preferred_element_type=jnp.float32).astype(
            jnp.bfloat16
        )
        values_frame = jnp.dot(gathered, own_value, preferred_element_type=jnp.float32).astype(
            jnp.bfloat16
        )
        frame_pair = jnp.stack([keys_frame, values_frame])
        attended = attend(queries, frame_pair, mem_keys, mem_values, live_keys, head_share)
        blocks = attended.reshape(SPATIAL, tok_rows, share_width)[:, None]
        for bit_index in range(doublings):
            upper = position >> bit_index & 1 == 1
            dest_count = blocks.shape[0]
            paired = blocks.reshape((dest_count // 2, 2) + blocks.shape[1:])
            kept = jnp.where(upper, paired[:, 1], paired[:, 0])
            sent = jnp.where(upper, paired[:, 0], paired[:, 1])
            arrived = from_partner(sent, "frame", bit_index)
            blocks = in_order(kept, arrived, upper, 1)
        joined = jnp.transpose(blocks[0], (1, 0, 2)).reshape(tok_rows, feature_width)
        current = (widened + step_scale[step_index] * joined.astype(jnp.float32)).astype(
            jnp.bfloat16
        )
    return current


def per_device(*arguments):
    return (paired_planes if fits_paired_planes(*arguments) else separate_frames)(*arguments)


def solution(mesh):
    placed = (
        P(("groups", "frame"), None),
        P(),
        P("frame", None),
        P("frame", None),
        P("frame", None),
        P("groups", "frame", None, None),
        P("groups", None),
        P("groups"),
        P("groups"),
        P(),
    )
    return jax.shard_map(
        per_device,
        mesh=mesh,
        in_specs=placed,
        out_specs=P(("groups", "frame"), None),
        check_vma=False,
    )
```

```python
import functools
import math

import jax
import jax.numpy as jnp
from jax import lax
from jax.experimental import pallas as pl
from jax.experimental.pallas import tpu as pltpu
from jax.sharding import PartitionSpec as P


HEADS = 12
HS = 128
SPATIAL = 4
STEPS = 2
AXES = ("groups", "frame")


def coords(index):
    return index // 4, (index // 2) % 2, index % 2


def quarter_of(plane, y):
    return (plane % 2) * 2 + y


def moved(array, target):
    devices = lax.axis_size("frame")
    pairs = []
    for x in range(lax.axis_size("groups")):
        for index in range(devices):
            place = target(x, *coords(index))
            if place is not None:
                to_x, to_plane, to_y, to_c = place
                pairs.append((x * devices + index, to_x * devices + to_plane * 4 + to_y * 2 + to_c))
    return lax.ppermute(array, AXES, pairs)


def here():
    x = lax.axis_index("groups")
    index = lax.axis_index("frame")
    plane = index // 4
    rest = index - plane * 4
    y = rest // 2
    return x, index, plane, y, rest - y * 2


def flipped(value, bits):
    out = value
    bit = 1
    while bit <= bits:
        if bits & bit:
            out = out + bit - 2 * bit * ((value // bit) % 2)
        bit *= 2
    return out


def joined_bits(one, other):
    return one + other - 2 * one * other


def columns(quarter, width):
    return pl.ds(pl.multiple_of(quarter * width, 128), width)


def pack_kernel(
    w_query, w_key, w_value, list_hbm, slot_hbm, count_hbm, scale_hbm, gain_hbm, mem_ref,
    own_ref, beside_ref, even_ref, odd_ref, extra_ref, *refs,
):
    near_count = SPATIAL
    memory_refs = refs[:near_count]
    (
        list_ref, slot_ref, count_ref, scale_ref, gain, rows, stored, extra, row_sem, out_sem, scalar_sem, mem_sem, give_sem,
    ) = refs[near_count:]
    x, index, plane, y, c = here()
    devices = lax.axis_size("frame")
    frames, entries = list_ref.shape
    width = own_ref.shape[1] // 3
    scalars = [
        pltpu.make_async_copy(source, target, scalar_sem.at[number])
        for number, (source, target) in enumerate(
            (
                (list_hbm, list_ref),
                (slot_hbm, slot_ref),
                (count_hbm, count_ref),
                (scale_hbm, scale_ref),
                (gain_hbm, gain),
            )
        )
    ]
    for copy in scalars[:2]:
        copy.start()
    reads = []
    for number, weight in enumerate((w_query, w_key, w_value)):
        reads.append(pltpu.make_async_copy(weight, rows.at[number], row_sem.at[number]))
        reads[-1].start()
    for copy in scalars[2:]:
        copy.start()
    for copy in scalars[:2]:
        copy.wait()
    picks = []
    for frame in range(frames):
        for entry in range(entries):
            number = frame * entries + entry
            row = slot_ref[list_ref[frame, entry]]
            picks.append(pltpu.make_async_copy(mem_ref.at[row, 0], stored.at[number], mem_sem.at[number]))
            picks[-1].start()
    across = joined_bits(joined_bits(x, y), c)
    low = plane % 2
    quarters = (low * 2 + across, (1 - low) * 2 + across, low * 2 + 1 - y, quarter_of(plane, y))
    gives = []
    for number, read in enumerate(reads):
        read.wait()
        for place, (quarter, out) in enumerate(zip(quarters, (even_ref, odd_ref, beside_ref, own_ref))):
            gives.append(
                pltpu.make_async_copy(
                    rows.at[number, :, columns(quarter, width)],
                    out.at[:, pl.ds(number * width, width)],
                    out_sem.at[number, place],
                )
            )
            gives[-1].start()
    for copy in scalars[2:]:
        copy.wait()
    row = (1, extra.shape[1])
    extra[0:1, :] = gain[...].reshape(row)
    for number in range(STEPS):
        extra[1 + number : 2 + number, :] = jnp.full(row, scale_ref[number], jnp.float32)
    live = lax.broadcasted_iota(jnp.int32, row, 1) % entries < count_ref[(plane // 2) * 2 + c]
    extra[1 + STEPS : 2 + STEPS, :] = jnp.where(live, 1.0, 0.0)
    gives.append(pltpu.make_async_copy(extra, extra_ref, scalar_sem.at[5]))
    gives[-1].start()
    for pick in picks:
        pick.wait()
    for away in range(devices):
        to_plane, to_y, to_c = coords(flipped(index, away))
        to_frame = (to_plane // 2) * 2 + to_c
        gives.append(
            pltpu.make_async_copy(
                stored.at[pl.ds(to_frame * entries, entries), :, columns(quarter_of(to_plane, to_y), width)],
                memory_refs[away % SPATIAL].at[away // SPATIAL],
                give_sem.at[away],
            )
        )
        gives[-1].start()
    for give in gives:
        give.wait()


def pack(w_query, w_key, w_value, intersection, slot_of, counts, step_scale, norm_gain, mem_cache):
    devices = lax.axis_size("frame")
    shard_rows, features = w_query.shape
    frames, entries = intersection.shape
    piece = jax.ShapeDtypeStruct((shard_rows, 3 * (features // SPATIAL)), w_query.dtype)
    small = jax.ShapeDtypeStruct((2 + STEPS, features), jnp.float32)
    memory = jax.ShapeDtypeStruct((devices // SPATIAL, entries, 2, features // SPATIAL), mem_cache.dtype)
    out_shape = (piece,) * 4 + (small,) + (memory,) * SPATIAL
    anywhere = pl.BlockSpec(memory_space=pl.ANY)
    held = pl.BlockSpec(memory_space=pltpu.HBM)
    outs = pl.pallas_call(
        pack_kernel,
        out_shape=out_shape,
        in_specs=[held] * 9,
        out_specs=(anywhere,) * len(out_shape),
        scratch_shapes=[
            pltpu.SMEM(intersection.shape, intersection.dtype),
            pltpu.SMEM(slot_of.shape, slot_of.dtype),
            pltpu.SMEM(counts.shape, counts.dtype),
            pltpu.SMEM(step_scale.shape, step_scale.dtype),
            pltpu.VMEM(norm_gain.shape, norm_gain.dtype),
            pltpu.VMEM((3, shard_rows, features), w_query.dtype),
            pltpu.VMEM((frames * entries, 2, features), mem_cache.dtype),
            pltpu.VMEM(small.shape, small.dtype),
            pltpu.SemaphoreType.DMA((3,)),
            pltpu.SemaphoreType.DMA((3, 4)),
            pltpu.SemaphoreType.DMA((6,)),
            pltpu.SemaphoreType.DMA((frames * entries,)),
            pltpu.SemaphoreType.DMA((devices,)),
        ],
        name="pack",
    )(w_query, w_key, w_value, intersection, slot_of, counts, step_scale, norm_gain, mem_cache)
    return outs[:4], outs[4], outs[5:]


def all_pieces(own, beside, even, odd):
    planes = lax.axis_size("frame") // 4
    pieces = [("own", own, (0, 0, False))]
    pieces.append(("near", moved(beside, lambda x, p, y, c: (x, p, 1 - y, c)), (0, 1, False)))
    for bits in range(1, planes):
        name = f"plane{bits}"
        sent = even if bits % 2 == 0 else odd
        direct = moved(sent, lambda x, p, y, c, bits=bits: (x, p ^ bits, y ^ x ^ c, c))
        pieces.append((name, direct, (bits, 0, True)))
        name = f"cross{bits}"
        pieces.append((name, moved(direct, lambda x, p, y, c: (1 - x, p, y, c)), (bits, 1, True)))
    places = [(array, place + (0,)) for _, array, place in pieces]
    for name, array, place in pieces:
        places.append((moved(array, lambda x, p, y, c: (x, p, y, 1 - c)), place + (1,)))
    return places


def all_memory(parts):
    planes = lax.axis_size("frame") // SPATIAL
    near = [parts[0]] + [hop(part, place) for place, part in enumerate(parts) if place]
    held = jnp.stack(near, axis=1)
    arrived = [held[0]] + [hop(held[bits], bits * SPATIAL) for bits in range(1, planes)]
    held = jnp.concatenate(arrived)
    keys, values = held[:, :, 0, :], held[:, :, 1, :]
    return keys.reshape(-1, keys.shape[-1]), values.reshape(-1, values.shape[-1])


def hop(array, bits):
    return lax.ppermute(array, "frame", [(i, i ^ bits) for i in range(lax.axis_size("frame"))])


def all_tokens(latent):
    other = moved(latent, lambda x, p, y, c: (x, p, y, 1 - c) if c != p % 2 else None)
    block = jnp.concatenate([latent, other])
    near = moved(block, lambda x, p, y, c: (x, p, 1 - y, c) if c == p % 2 else None)
    far = moved(block, lambda x, p, y, c: (x, p ^ 1, y, c) if c == p % 2 else None)
    both = moved(block, lambda x, p, y, c: (x, p ^ 1, 1 - y, c) if c == p % 2 else None)
    return block, near, far, both


def late_plane(devices):
    return devices // 4 - 1


def piece_start(place, shard_rows, plane_number):
    x, _, _, y, c = here()
    _, y_bits, with_x, c_bits = place
    from_y, from_c = flipped(y, y_bits), flipped(c, c_bits)
    if with_x:
        from_y = joined_bits(joined_bits(from_y, x), from_c)
    return pl.multiple_of((plane_number * 4 + from_y * 2 + from_c) * shard_rows, 16)


def gather_pieces(piece_refs, places, first_plane, weights):
    for ref, place in zip(piece_refs, places):
        start = piece_start(place, ref.shape[0], place[0] - first_plane)
        weights[pl.ds(start, ref.shape[0]), :] = ref[...]


def store_normed(current, rows, inverse, gain_ref, normed):
    _, _, plane, _, _ = here()
    planes = lax.axis_size("frame") // 4
    span = current.shape[1] // planes
    for bits in range(planes):
        spot = columns(flipped(plane, bits), span)
        widened = current[rows, spot].astype(jnp.float32)
        normed[rows, bits * span : (bits + 1) * span] = (widened * inverse * gain_ref[0:1, spot]).astype(normed.dtype)


BLOCK = 32


def prepare_kernel(extra_ref, block, near, far, far_near, extra, current, normed, token_sem):
    _, _, plane, y, c = here()
    chip_rows = block.shape[0]
    at_home = plane % 2 == c
    extra_copy = pltpu.make_async_copy(extra_ref, extra, token_sem.at[2])
    extra_copy.start()

    def token_copies(first, second):
        return (
            pltpu.make_async_copy(first, current.at[pl.ds(y * chip_rows, chip_rows)], token_sem.at[0]),
            pltpu.make_async_copy(second, current.at[pl.ds((1 - y) * chip_rows, chip_rows)], token_sem.at[1]),
        )

    @pl.when(at_home)
    def _():
        for copy in token_copies(block, near):
            copy.start()

    @pl.when(jnp.logical_not(at_home))
    def _():
        for copy in token_copies(far, far_near):
            copy.start()

    for copy in token_copies(block, near):
        copy.wait()
    extra_copy.wait()

    @pl.loop(0, current.shape[0] // BLOCK)
    def _(number):
        rows = pl.ds(pl.multiple_of(number * BLOCK, BLOCK), BLOCK)
        widened = current[rows, :].astype(jnp.float32)
        inverse = lax.rsqrt(jnp.mean(widened * widened, axis=-1, keepdims=True) + 1e-06)
        store_normed(current, rows, inverse, extra, normed)


def project_kernel(places, *refs):
    normed = refs[0]
    piece_refs = refs[1 : 1 + len(places)]
    out, weights = refs[1 + len(places) :]
    gather_pieces(piece_refs, places, 0, weights)
    out[...] = jnp.dot(normed[:, : weights.shape[0]], weights[...], preferred_element_type=jnp.float32)


def assemble_kernel(places, *refs):
    gather_pieces(refs[:-1], places, 0, refs[-1])


def attend_heads(projected, key_ref, value_ref, extra_ref, attended, head_count):
    width = projected.shape[1] // 3
    head_size = width // head_count
    scale_dot = 1.0 / math.sqrt(head_size)
    mem_rows = key_ref.shape[0]
    live = extra_ref[3:4, :mem_rows] > 0.5
    contract_last = (((1,), (1,)), ((), ()))
    frame_rows = projected.shape[0]
    half = frame_rows // 2
    for head in range(head_count):
        span = slice(head * head_size, (head + 1) * head_size)
        keys = projected[:, width + head * head_size : width + (head + 1) * head_size]
        values = projected[:, 2 * width + head * head_size : 2 * width + (head + 1) * head_size]
        for start in range(0, frame_rows, half):
            queries = projected[start : start + half, span]
            frame_scores = (
                lax.dot_general(queries, keys, contract_last, preferred_element_type=jnp.float32) * scale_dot
            )
            mem_scores = (
                lax.dot_general(queries, key_ref[:, span], contract_last, preferred_element_type=jnp.float32)
                * scale_dot
            )
            mem_scores = jnp.where(live, mem_scores, -1e30)
            largest = jnp.maximum(
                jnp.max(frame_scores, axis=-1, keepdims=True), jnp.max(mem_scores, axis=-1, keepdims=True)
            )
            frame_weights = jnp.exp(frame_scores - largest)
            mem_weights = jnp.exp(mem_scores - largest)
            denominator = jnp.sum(frame_weights, axis=-1, keepdims=True) + jnp.sum(
                mem_weights, axis=-1, keepdims=True
            )
            blended = jnp.dot(
                frame_weights.astype(jnp.bfloat16), values, preferred_element_type=jnp.float32
            ) + jnp.dot(mem_weights.astype(jnp.bfloat16), value_ref[:, span], preferred_element_type=jnp.float32)
            attended[start : start + half, span] = (blended / denominator).astype(attended.dtype)


def step_kernel(places, first_plane, head_count, extra_ref, key_ref, value_ref, normed, part_ref, *refs):
    piece_refs = refs[: len(places)]
    attended, weights, projected = refs[len(places) :]
    gather_pieces(piece_refs, places, first_plane, weights)
    early = normed.shape[1] - weights.shape[0]
    projected[...] = (
        part_ref[...] + jnp.dot(normed[:, early:], weights[...], preferred_element_type=jnp.float32)
    ).astype(projected.dtype)
    attend_heads(projected, key_ref, value_ref, extra_ref, attended, head_count)


def last_step_kernel(
    update_places, head_count, extra_ref, key_ref, value_ref, current_ref, weights, first_part, second_part, third_part,
    fourth_part, keep, first, second, third, fourth, current, normed, projected, attended,
):
    _, _, plane, y, c = here()
    width = first_part.shape[1]
    at_home = plane % 2 == c

    @pl.loop(0, current.shape[0] // BLOCK)
    def _(number):
        rows = pl.ds(pl.multiple_of(number * BLOCK, BLOCK), BLOCK)
        total = jnp.zeros((BLOCK, 1), jnp.float32)
        for part, (plane_bits, y_bits) in zip((first_part, second_part, third_part, fourth_part), update_places):
            spot = columns(quarter_of(flipped(plane, plane_bits), flipped(y, y_bits)), width)
            updated = (
                current_ref[rows, spot].astype(jnp.float32)
                + extra_ref[1:2, :width] * part[rows, :].astype(jnp.float32)
            ).astype(current.dtype)
            current[rows, spot] = updated
            widened = updated.astype(jnp.float32)
            total = total + jnp.sum(widened * widened, axis=-1, keepdims=True)
        inverse = lax.rsqrt(total / current.shape[1] + 1e-06)
        store_normed(current, rows, inverse, extra_ref, normed)

    projected[...] = jnp.dot(normed[...], weights[...], preferred_element_type=jnp.float32).astype(projected.dtype)
    attend_heads(projected, key_ref, value_ref, extra_ref, attended, head_count)
    spot = columns(quarter_of(plane, y), width)
    attended[...] = (
        current[:, spot].astype(jnp.float32) + extra_ref[2:3, :width] * attended[...].astype(jnp.float32)
    ).astype(attended.dtype)
    chip_rows = attended.shape[0] // 2
    rows = chip_rows // 2
    here_rows, there_rows = y * chip_rows, (1 - y) * chip_rows

    def part(start):
        return attended[pl.ds(pl.multiple_of(start, rows), rows), :]

    keep[...] = part(here_rows)
    fourth[...] = part(there_rows + rows)

    @pl.when(at_home)
    def _():
        first[...] = part(there_rows)
        second[...] = part(there_rows + rows)
        third[...] = part(here_rows + rows)

    @pl.when(jnp.logical_not(at_home))
    def _():
        first[...] = part(here_rows + rows)
        second[...] = part(here_rows)
        third[...] = part(there_rows)


MIB = 1024 * 1024


def kernel_call(kernel, out_shape, operands, anywhere, scratch_shapes, limit, flops):
    vectors = pl.BlockSpec(memory_space=pltpu.VMEM)
    free = pl.BlockSpec(memory_space=pl.ANY)
    moved_bytes = sum(operand.size * operand.dtype.itemsize for operand in operands)
    return pl.pallas_call(
        kernel,
        out_shape=out_shape,
        in_specs=[free if number in anywhere else vectors for number in range(len(operands))],
        out_specs=jax.tree.map(lambda _: vectors, out_shape),
        scratch_shapes=scratch_shapes,
        compiler_params=pltpu.CompilerParams(vmem_limit_bytes=limit),
        cost_estimate=pl.CostEstimate(flops=flops, transcendentals=0, bytes_accessed=moved_bytes),
    )(*operands)


def prepare(extra, tokens):
    frame = jax.ShapeDtypeStruct((2 * tokens[0].shape[0], tokens[0].shape[1]), tokens[0].dtype)
    return kernel_call(
        prepare_kernel,
        (jax.ShapeDtypeStruct(extra.shape, extra.dtype), frame, frame),
        (extra, *tokens),
        range(5),
        [pltpu.SemaphoreType.DMA((3,))],
        8 * MIB,
        0,
    )


def project(normed, pieces):
    rows, width = pieces[0][0].shape
    depth = rows * len(pieces)
    return kernel_call(
        functools.partial(project_kernel, tuple(place for _, place in pieces)),
        jax.ShapeDtypeStruct((normed.shape[0], width), jnp.float32),
        (normed, *[array for array, _ in pieces]),
        (),
        [pltpu.VMEM((depth, width), normed.dtype)],
        16 * MIB,
        2 * normed.shape[0] * depth * width,
    )


def assemble(pieces):
    rows, width = pieces[0][0].shape
    return kernel_call(
        functools.partial(assemble_kernel, tuple(place for _, place in pieces)),
        jax.ShapeDtypeStruct((rows * len(pieces), width), pieces[0][0].dtype),
        [array for array, _ in pieces],
        (),
        [],
        8 * MIB,
        0,
    )


def step(extra, keys, values, normed, part, pieces):
    rows, width = pieces[0][0].shape
    depth = rows * len(pieces)
    frame_rows = normed.shape[0]
    return kernel_call(
        functools.partial(step_kernel, tuple(place for _, place in pieces), pieces[0][1][0], HEADS // SPATIAL),
        jax.ShapeDtypeStruct((frame_rows, width // 3), normed.dtype),
        (extra, keys, values, normed, part, *[array for array, _ in pieces]),
        (),
        [pltpu.VMEM((depth, width), normed.dtype), pltpu.VMEM((frame_rows, width), normed.dtype)],
        16 * MIB,
        2 * frame_rows * width * (depth + frame_rows),
    )


def last_step(extra, keys, values, current, weights, updates):
    frame_rows, features = current.shape
    width = weights.shape[1] // 3
    share = jax.ShapeDtypeStruct((frame_rows // 4, width), current.dtype)
    return kernel_call(
        functools.partial(last_step_kernel, tuple(place for _, place in updates), HEADS // SPATIAL),
        (share,) * 5,
        (extra, keys, values, current, weights, *[array for array, _ in updates]),
        (),
        [
            pltpu.VMEM((frame_rows, features), current.dtype),
            pltpu.VMEM((frame_rows, features), current.dtype),
            pltpu.VMEM((frame_rows, 3 * width), current.dtype),
            pltpu.VMEM((frame_rows, width), current.dtype),
        ],
        16 * MIB,
        2 * frame_rows * 3 * width * (features + frame_rows),
    )


def join_kernel(keep, first, second, third, fourth, out):
    _, _, plane, y, c = here()
    low = plane % 2
    width = keep.shape[1]

    def put(ref, plane_low, at_y):
        out[:, columns(plane_low * 2 + at_y, width)] = ref[...]

    @pl.when(low == c)
    def _():
        put(keep, low, y)
        put(first, low, 1 - y)
        put(second, 1 - low, y)
        put(third, 1 - low, 1 - y)

    @pl.when(low != c)
    def _():
        put(first, 1 - low, y)
        put(second, low, 1 - y)
        put(third, low, y)
        put(fourth, 1 - low, 1 - y)


def joined(keep, first, second, third, fourth):
    def at_home(p, c):
        return c == p % 2

    first = moved(first, lambda x, p, y, c: (x, p, 1 - y, c) if at_home(p, c) else (x, p ^ 1, y, 1 - c))
    second = moved(second, lambda x, p, y, c: (x, p, 1 - y, 1 - c) if at_home(p, c) else (x, p ^ 1, y, c))
    third = moved(third, lambda x, p, y, c: (x, p, y, 1 - c) if at_home(p, c) else (x, p ^ 1, 1 - y, c))
    fourth = moved(fourth, lambda x, p, y, c: None if at_home(p, c) else (x, p ^ 1, 1 - y, 1 - c))
    rows, width = keep.shape
    return kernel_call(
        join_kernel,
        jax.ShapeDtypeStruct((rows, width * SPATIAL), keep.dtype),
        (keep, first, second, third, fourth),
        (),
        [],
        4 * MIB,
        0,
    )


def paired_planes(
    latent, norm_gain, w_query, w_key, w_value, mem_cache, intersection, counts, slot_of, step_scale
):
    late = late_plane(lax.axis_size("frame"))
    weights, extra, memory = pack(
        w_query, w_key, w_value, intersection, slot_of, counts, step_scale, norm_gain, mem_cache
    )
    pieces = sorted(all_pieces(*weights), key=lambda piece: piece[1][0])
    tokens = all_tokens(latent)
    keys, values = all_memory(memory)
    extra, current, normed = prepare(extra, tokens)
    part = project(normed, [piece for piece in pieces if piece[1][0] < late])
    attended = step(extra, keys, values, normed, part, [piece for piece in pieces if piece[1][0] == late])
    updates = [
        (attended, (0, 0)),
        (moved(attended, lambda x, p, y, c: (x, p ^ 1, 1 - y, c)), (1, 1)),
        (moved(attended, lambda x, p, y, c: (x, p ^ 1, y, c)), (1, 0)),
        (moved(attended, lambda x, p, y, c: (x, p, 1 - y, c)), (0, 1)),
    ]
    shares = last_step(extra, keys, values, current, assemble(pieces), updates)
    return joined(*shares)


def fits_paired_planes(latent, norm_gain, w_query, w_key, w_value, mem_cache, *_):
    devices = lax.axis_size("frame")
    planes = devices // SPATIAL
    return (
        lax.axis_size("groups") == 2
        and devices == planes * SPATIAL
        and planes >= 2
        and planes & (planes - 1) == 0
        and w_query.shape[0] % 16 == 0
        and mem_cache.shape[1] == 1
    )


def from_partner(array, axis, bit):
    return lax.ppermute(array, axis, [(i, i ^ 1 << bit) for i in range(lax.axis_size(axis))])


def in_order(mine, theirs, upper, axis_dim):
    low_first = jnp.concatenate([mine, theirs], axis=axis_dim)
    high_first = jnp.concatenate([theirs, mine], axis=axis_dim)
    return jnp.where(upper, high_first, low_first)


def attend(queries, frame_pair, mem_keys, mem_values, live_keys, head_count):
    tok_rows, feature_width = queries.shape
    head_size = feature_width // head_count
    scale_dot = 1.0 / math.sqrt(head_size)
    q_heads = queries.reshape(tok_rows, head_count, head_size)
    k_heads = frame_pair[0].reshape(-1, head_count, head_size)
    v_heads = frame_pair[1].reshape(-1, head_count, head_size)
    frame_scores = (
        jnp.einsum("thd,khd->htk", q_heads, k_heads, preferred_element_type=jnp.float32) * scale_dot
    )
    remote_scores = (
        jnp.einsum("thd,khd->htk", q_heads, mem_keys, preferred_element_type=jnp.float32)
        * scale_dot
    )
    remote_scores = jnp.where(live_keys[None, None, :], remote_scores, -1e30)
    largest = jnp.maximum(
        jnp.max(frame_scores, axis=-1, keepdims=True),
        jnp.max(remote_scores, axis=-1, keepdims=True),
    )
    frame_weights = jnp.exp(frame_scores - largest)
    remote_weights = jnp.exp(remote_scores - largest)
    denominator = jnp.sum(frame_weights, axis=-1) + jnp.sum(remote_weights, axis=-1)
    blended = jnp.einsum(
        "htk,khd->thd",
        frame_weights.astype(jnp.bfloat16),
        v_heads,
        preferred_element_type=jnp.float32,
    )
    blended = blended + jnp.einsum(
        "htk,khd->thd",
        remote_weights.astype(jnp.bfloat16),
        mem_values,
        preferred_element_type=jnp.float32,
    )
    blended = blended / jnp.transpose(denominator)[:, :, None]
    return blended.reshape(tok_rows, feature_width).astype(jnp.bfloat16)


def rms_normed(current, norm_gain):
    widened = current.astype(jnp.float32)
    inverse = lax.rsqrt(jnp.mean(widened * widened, axis=-1, keepdims=True) + 1e-06)
    return (widened, (widened * inverse * norm_gain).astype(jnp.bfloat16))


def separate_frames(
    latent, norm_gain, w_query, w_key, w_value, mem_cache, intersection, counts, slot_of, step_scale
):
    devices = lax.axis_size("frame")
    position = lax.axis_index("frame")
    frame_index = position // SPATIAL
    doublings = SPATIAL.bit_length() - 1
    target_frame = jnp.arange(devices, dtype=jnp.int32) // SPATIAL
    current = latent
    feature_width = latent.shape[1]
    share_width = feature_width // SPATIAL
    head_share = HEADS // SPATIAL

    def column_pieces(weight):
        row_count = weight.shape[0]
        split_cols = jnp.transpose(weight.reshape(row_count, SPATIAL, share_width), (1, 0, 2))
        return jnp.tile(split_cols, (devices // SPATIAL, 1, 1))

    own_query, own_key, own_value = (
        lax.all_to_all(column_pieces(w_query), "frame", split_axis=0, concat_axis=1, tiled=True),
        lax.all_to_all(column_pieces(w_key), "frame", split_axis=0, concat_axis=1, tiled=True),
        lax.all_to_all(column_pieces(w_value), "frame", split_axis=0, concat_axis=1, tiled=True),
    )
    own_query, own_key, own_value = (own_query[0], own_key[0], own_value[0])
    listed = mem_cache[slot_of[intersection[target_frame]]]
    list_len = listed.shape[1]
    local_mem = listed.shape[2]
    grouped = listed.reshape(
        devices // SPATIAL, SPATIAL, list_len, local_mem, 2, SPATIAL, share_width
    )
    diagonal_part = jnp.diagonal(grouped, axis1=1, axis2=5)
    outgoing = jnp.moveaxis(diagonal_part, -1, 1).reshape(
        devices, list_len, local_mem, 2, share_width
    )
    fetched = lax.all_to_all(outgoing, "frame", split_axis=0, concat_axis=2, tiled=True)[0]
    mem_len = fetched.shape[1]
    mem_keys = fetched[:, :, 0, :].reshape(list_len * mem_len, head_share, HS)
    mem_values = fetched[:, :, 1, :].reshape(list_len * mem_len, head_share, HS)
    live_keys = jnp.arange(list_len * mem_len, dtype=jnp.int32) // mem_len < counts[frame_index]
    tok_rows = latent.shape[0]
    for step_index in range(STEPS):
        widened, normed = rms_normed(current, norm_gain)
        gathered = normed
        for bit_index in range(doublings):
            partner = from_partner(gathered, "frame", bit_index)
            gathered = in_order(gathered, partner, position >> bit_index & 1 == 1, 0)
        queries = jnp.dot(gathered, own_query, preferred_element_type=jnp.float32).astype(
            jnp.bfloat16
        )
        keys_frame = jnp.dot(gathered, own_key, preferred_element_type=jnp.float32).astype(
            jnp.bfloat16
        )
        values_frame = jnp.dot(gathered, own_value, preferred_element_type=jnp.float32).astype(
            jnp.bfloat16
        )
        frame_pair = jnp.stack([keys_frame, values_frame])
        attended = attend(queries, frame_pair, mem_keys, mem_values, live_keys, head_share)
        blocks = attended.reshape(SPATIAL, tok_rows, share_width)[:, None]
        for bit_index in range(doublings):
            upper = position >> bit_index & 1 == 1
            dest_count = blocks.shape[0]
            paired = blocks.reshape((dest_count // 2, 2) + blocks.shape[1:])
            kept = jnp.where(upper, paired[:, 1], paired[:, 0])
            sent = jnp.where(upper, paired[:, 0], paired[:, 1])
            arrived = from_partner(sent, "frame", bit_index)
            blocks = in_order(kept, arrived, upper, 1)
        joined = jnp.transpose(blocks[0], (1, 0, 2)).reshape(tok_rows, feature_width)
        current = (widened + step_scale[step_index] * joined.astype(jnp.float32)).astype(
            jnp.bfloat16
        )
    return current


def per_device(*arguments):
    return (paired_planes if fits_paired_planes(*arguments) else separate_frames)(*arguments)


def solution(mesh):
    placed = (
        P(("groups", "frame"), None),
        P(),
        P("frame", None),
        P("frame", None),
        P("frame", None),
        P("groups", "frame", None, None),
        P("groups", None),
        P("groups"),
        P("groups"),
        P(),
    )
    return jax.shard_map(
        per_device,
        mesh=mesh,
        in_specs=placed,
        out_specs=P(("groups", "frame"), None),
        check_vma=False,
    )
```

```python
import functools
import math

import jax
import jax.numpy as jnp
from jax import lax
from jax.experimental import pallas as pl
from jax.experimental.pallas import tpu as pltpu
from jax.sharding import PartitionSpec as P


HEADS = 12
HS = 128
SPATIAL = 4
STEPS = 2
AXES = ("groups", "frame")


def coords(index):
    return index // 4, (index // 2) % 2, index % 2


def quarter_of(plane, y):
    return (plane % 2) * 2 + y


def moved(array, target):
    devices = lax.axis_size("frame")
    pairs = []
    for x in range(lax.axis_size("groups")):
        for index in range(devices):
            place = target(x, *coords(index))
            if place is not None:
                to_x, to_plane, to_y, to_c = place
                pairs.append((x * devices + index, to_x * devices + to_plane * 4 + to_y * 2 + to_c))
    return lax.ppermute(array, AXES, pairs)


def here():
    x = lax.axis_index("groups")
    index = lax.axis_index("frame")
    plane = index // 4
    rest = index - plane * 4
    y = rest // 2
    return x, index, plane, y, rest - y * 2


def flipped(value, bits):
    out = value
    bit = 1
    while bit <= bits:
        if bits & bit:
            out = out + bit - 2 * bit * ((value // bit) % 2)
        bit *= 2
    return out


def joined_bits(one, other):
    return one + other - 2 * one * other


def columns(quarter, width):
    return pl.ds(pl.multiple_of(quarter * width, 128), width)


def pack_kernel(
    w_query, w_key, w_value, list_hbm, slot_hbm, count_hbm, scale_hbm, gain_hbm, mem_ref,
    own_ref, beside_ref, even_ref, odd_ref, extra_ref, *refs,
):
    near_count = SPATIAL
    memory_refs = refs[:near_count]
    (
        list_ref, slot_ref, count_ref, scale_ref, gain, rows, stored, extra, row_sem, out_sem, scalar_sem, mem_sem, give_sem,
    ) = refs[near_count:]
    x, index, plane, y, c = here()
    devices = lax.axis_size("frame")
    frames, entries = list_ref.shape
    width = own_ref.shape[1] // 3
    scalars = [
        pltpu.make_async_copy(source, target, scalar_sem.at[number])
        for number, (source, target) in enumerate(
            (
                (list_hbm, list_ref),
                (slot_hbm, slot_ref),
                (count_hbm, count_ref),
                (scale_hbm, scale_ref),
                (gain_hbm, gain),
            )
        )
    ]
    for copy in scalars[:2]:
        copy.start()
    reads = []
    for number, weight in enumerate((w_query, w_key, w_value)):
        reads.append(pltpu.make_async_copy(weight, rows.at[number], row_sem.at[number]))
        reads[-1].start()
    for copy in scalars[2:]:
        copy.start()
    for copy in scalars[:2]:
        copy.wait()
    picks = []
    for frame in range(frames):
        for entry in range(entries):
            number = frame * entries + entry
            row = slot_ref[list_ref[frame, entry]]
            picks.append(pltpu.make_async_copy(mem_ref.at[row, 0], stored.at[number], mem_sem.at[number]))
            picks[-1].start()
    across = joined_bits(joined_bits(x, y), c)
    low = plane % 2
    quarters = (low * 2 + across, (1 - low) * 2 + across, low * 2 + 1 - y, quarter_of(plane, y))
    gives = []
    for number, read in enumerate(reads):
        read.wait()
        for place, (quarter, out) in enumerate(zip(quarters, (even_ref, odd_ref, beside_ref, own_ref))):
            gives.append(
                pltpu.make_async_copy(
                    rows.at[number, :, columns(quarter, width)],
                    out.at[:, pl.ds(number * width, width)],
                    out_sem.at[number, place],
                )
            )
            gives[-1].start()
    for copy in scalars[2:]:
        copy.wait()
    row = (1, extra.shape[1])
    extra[0:1, :] = gain[...].reshape(row)
    for number in range(STEPS):
        extra[1 + number : 2 + number, :] = jnp.full(row, scale_ref[number], jnp.float32)
    live = lax.broadcasted_iota(jnp.int32, row, 1) % entries < count_ref[(plane // 2) * 2 + c]
    extra[1 + STEPS : 2 + STEPS, :] = jnp.where(live, 1.0, 0.0)
    gives.append(pltpu.make_async_copy(extra, extra_ref, scalar_sem.at[5]))
    gives[-1].start()
    for pick in picks:
        pick.wait()
    bits = devices.bit_length() - 1
    for away in range(devices):
        to_plane, to_y, to_c = coords(flipped(index, away))
        to_frame = (to_plane // 2) * 2 + to_c
        place = 0
        for bit in range(2, bits):
            place = place * 2 + (away >> bit & 1)
        gives.append(
            pltpu.make_async_copy(
                stored.at[pl.ds(to_frame * entries, entries), :, columns(quarter_of(to_plane, to_y), width)],
                memory_refs[away % SPATIAL].at[place],
                give_sem.at[away],
            )
        )
        gives[-1].start()
    for give in gives:
        give.wait()


def pack(w_query, w_key, w_value, intersection, slot_of, counts, step_scale, norm_gain, mem_cache):
    devices = lax.axis_size("frame")
    shard_rows, features = w_query.shape
    frames, entries = intersection.shape
    piece = jax.ShapeDtypeStruct((shard_rows, 3 * (features // SPATIAL)), w_query.dtype)
    small = jax.ShapeDtypeStruct((2 + STEPS, features), jnp.float32)
    memory = jax.ShapeDtypeStruct((devices // SPATIAL, entries, 2, features // SPATIAL), mem_cache.dtype)
    out_shape = (piece,) * 4 + (small,) + (memory,) * SPATIAL
    anywhere = pl.BlockSpec(memory_space=pl.ANY)
    held = pl.BlockSpec(memory_space=pltpu.HBM)
    outs = pl.pallas_call(
        pack_kernel,
        out_shape=out_shape,
        in_specs=[held] * 9,
        out_specs=(anywhere,) * len(out_shape),
        scratch_shapes=[
            pltpu.SMEM(intersection.shape, intersection.dtype),
            pltpu.SMEM(slot_of.shape, slot_of.dtype),
            pltpu.SMEM(counts.shape, counts.dtype),
            pltpu.SMEM(step_scale.shape, step_scale.dtype),
            pltpu.VMEM(norm_gain.shape, norm_gain.dtype),
            pltpu.VMEM((3, shard_rows, features), w_query.dtype),
            pltpu.VMEM((frames * entries, 2, features), mem_cache.dtype),
            pltpu.VMEM(small.shape, small.dtype),
            pltpu.SemaphoreType.DMA((3,)),
            pltpu.SemaphoreType.DMA((3, 4)),
            pltpu.SemaphoreType.DMA((6,)),
            pltpu.SemaphoreType.DMA((frames * entries,)),
            pltpu.SemaphoreType.DMA((devices,)),
        ],
        name="pack",
    )(w_query, w_key, w_value, intersection, slot_of, counts, step_scale, norm_gain, mem_cache)
    return outs[:4], outs[4], outs[5:]


def all_pieces(own, beside, even, odd):
    planes = lax.axis_size("frame") // 4
    pieces = [("own", own, (0, 0, False))]
    pieces.append(("near", moved(beside, lambda x, p, y, c: (x, p, 1 - y, c)), (0, 1, False)))
    for bits in range(1, planes):
        name = f"plane{bits}"
        sent = even if bits % 2 == 0 else odd
        direct = moved(sent, lambda x, p, y, c, bits=bits: (x, p ^ bits, y ^ x ^ c, c))
        pieces.append((name, direct, (bits, 0, True)))
        name = f"cross{bits}"
        pieces.append((name, moved(direct, lambda x, p, y, c: (1 - x, p, y, c)), (bits, 1, True)))
    places = [(array, place + (0,)) for _, array, place in pieces]
    for name, array, place in pieces:
        places.append((moved(array, lambda x, p, y, c: (x, p, y, 1 - c)), place + (1,)))
    return places


def all_memory(parts):
    devices = lax.axis_size("frame")
    near = [parts[0]] + [hop(part, place) for place, part in enumerate(parts) if place]
    held = jnp.stack(near)
    for bit in range(2, devices.bit_length() - 1):
        half = held.shape[1] // 2
        arrived = hop(held[:, half:], 1 << bit)
        held = jnp.concatenate([held[:, :half], arrived])
    keys, values = held[:, 0, :, 0, :], held[:, 0, :, 1, :]
    return keys.reshape(-1, keys.shape[-1]), values.reshape(-1, values.shape[-1])


def hop(array, bits):
    return lax.ppermute(array, "frame", [(i, i ^ bits) for i in range(lax.axis_size("frame"))])


def all_tokens(latent):
    other = moved(latent, lambda x, p, y, c: (x, p, y, 1 - c) if c != p % 2 else None)
    block = jnp.concatenate([latent, other])
    near = moved(block, lambda x, p, y, c: (x, p, 1 - y, c) if c == p % 2 else None)
    far = moved(block, lambda x, p, y, c: (x, p ^ 1, y, c) if c == p % 2 else None)
    far_near = moved(far, lambda x, p, y, c: (x, p, 1 - y, c) if c != p % 2 else None)
    return block, near, far, far_near


def late_plane(devices):
    return devices // 4 - 1


def piece_start(place, shard_rows, plane_number):
    x, _, _, y, c = here()
    _, y_bits, with_x, c_bits = place
    from_y, from_c = flipped(y, y_bits), flipped(c, c_bits)
    if with_x:
        from_y = joined_bits(joined_bits(from_y, x), from_c)
    return pl.multiple_of((plane_number * 4 + from_y * 2 + from_c) * shard_rows, 16)


def gather_pieces(piece_refs, places, first_plane, weights):
    for ref, place in zip(piece_refs, places):
        start = piece_start(place, ref.shape[0], place[0] - first_plane)
        weights[pl.ds(start, ref.shape[0]), :] = ref[...]


def store_normed(current, rows, inverse, gain_ref, normed):
    _, _, plane, _, _ = here()
    planes = lax.axis_size("frame") // 4
    span = current.shape[1] // planes
    for bits in range(planes):
        spot = columns(flipped(plane, bits), span)
        widened = current[rows, spot].astype(jnp.float32)
        normed[rows, bits * span : (bits + 1) * span] = (widened * inverse * gain_ref[0:1, spot]).astype(normed.dtype)


BLOCK = 32


def prepare_kernel(extra_ref, block, near, far, far_near, extra, current, normed, token_sem):
    _, _, plane, y, c = here()
    chip_rows = block.shape[0]
    at_home = plane % 2 == c
    extra_copy = pltpu.make_async_copy(extra_ref, extra, token_sem.at[2])
    extra_copy.start()

    def token_copies(first, second):
        return (
            pltpu.make_async_copy(first, current.at[pl.ds(y * chip_rows, chip_rows)], token_sem.at[0]),
            pltpu.make_async_copy(second, current.at[pl.ds((1 - y) * chip_rows, chip_rows)], token_sem.at[1]),
        )

    @pl.when(at_home)
    def _():
        for copy in token_copies(block, near):
            copy.start()

    @pl.when(jnp.logical_not(at_home))
    def _():
        for copy in token_copies(far, far_near):
            copy.start()

    for copy in token_copies(block, near):
        copy.wait()
    extra_copy.wait()

    @pl.loop(0, current.shape[0] // BLOCK)
    def _(number):
        rows = pl.ds(pl.multiple_of(number * BLOCK, BLOCK), BLOCK)
        widened = current[rows, :].astype(jnp.float32)
        inverse = lax.rsqrt(jnp.mean(widened * widened, axis=-1, keepdims=True) + 1e-06)
        store_normed(current, rows, inverse, extra, normed)


def project_kernel(places, *refs):
    normed = refs[0]
    piece_refs = refs[1 : 1 + len(places)]
    out, weights = refs[1 + len(places) :]
    gather_pieces(piece_refs, places, 0, weights)
    out[...] = jnp.dot(normed[:, : weights.shape[0]], weights[...], preferred_element_type=jnp.float32)


def assemble_kernel(places, *refs):
    gather_pieces(refs[:-1], places, 0, refs[-1])


def attend_heads(projected, key_ref, value_ref, extra_ref, attended, head_count):
    width = projected.shape[1] // 3
    head_size = width // head_count
    scale_dot = 1.0 / math.sqrt(head_size)
    mem_rows = key_ref.shape[0]
    live = extra_ref[3:4, :mem_rows] > 0.5
    contract_last = (((1,), (1,)), ((), ()))
    frame_rows = projected.shape[0]
    half = frame_rows // 2
    for head in range(head_count):
        span = slice(head * head_size, (head + 1) * head_size)
        keys = projected[:, width + head * head_size : width + (head + 1) * head_size]
        values = projected[:, 2 * width + head * head_size : 2 * width + (head + 1) * head_size]
        for start in range(0, frame_rows, half):
            queries = projected[start : start + half, span]
            frame_scores = (
                lax.dot_general(queries, keys, contract_last, preferred_element_type=jnp.float32) * scale_dot
            )
            mem_scores = (
                lax.dot_general(queries, key_ref[:, span], contract_last, preferred_element_type=jnp.float32)
                * scale_dot
            )
            mem_scores = jnp.where(live, mem_scores, -1e30)
            largest = jnp.maximum(
                jnp.max(frame_scores, axis=-1, keepdims=True), jnp.max(mem_scores, axis=-1, keepdims=True)
            )
            frame_weights = jnp.exp(frame_scores - largest)
            mem_weights = jnp.exp(mem_scores - largest)
            denominator = jnp.sum(frame_weights, axis=-1, keepdims=True) + jnp.sum(
                mem_weights, axis=-1, keepdims=True
            )
            blended = jnp.dot(
                frame_weights.astype(jnp.bfloat16), values, preferred_element_type=jnp.float32
            ) + jnp.dot(mem_weights.astype(jnp.bfloat16), value_ref[:, span], preferred_element_type=jnp.float32)
            attended[start : start + half, span] = (blended / denominator).astype(attended.dtype)


def step_kernel(places, first_plane, head_count, extra_ref, key_ref, value_ref, normed, part_ref, *refs):
    piece_refs = refs[: len(places)]
    attended, weights, projected = refs[len(places) :]
    gather_pieces(piece_refs, places, first_plane, weights)
    early = normed.shape[1] - weights.shape[0]
    projected[...] = (
        part_ref[...] + jnp.dot(normed[:, early:], weights[...], preferred_element_type=jnp.float32)
    ).astype(projected.dtype)
    attend_heads(projected, key_ref, value_ref, extra_ref, attended, head_count)


def last_step_kernel(
    update_places, head_count, extra_ref, key_ref, value_ref, current_ref, weights, first_part, second_part, third_part,
    fourth_part, keep, first, second, third, fourth, current, normed, projected, attended,
):
    _, _, plane, y, c = here()
    width = first_part.shape[1]
    at_home = plane % 2 == c

    @pl.loop(0, current.shape[0] // BLOCK)
    def _(number):
        rows = pl.ds(pl.multiple_of(number * BLOCK, BLOCK), BLOCK)
        total = jnp.zeros((BLOCK, 1), jnp.float32)
        for part, (plane_bits, y_bits) in zip((first_part, second_part, third_part, fourth_part), update_places):
            spot = columns(quarter_of(flipped(plane, plane_bits), flipped(y, y_bits)), width)
            updated = (
                current_ref[rows, spot].astype(jnp.float32)
                + extra_ref[1:2, :width] * part[rows, :].astype(jnp.float32)
            ).astype(current.dtype)
            current[rows, spot] = updated
            widened = updated.astype(jnp.float32)
            total = total + jnp.sum(widened * widened, axis=-1, keepdims=True)
        inverse = lax.rsqrt(total / current.shape[1] + 1e-06)
        store_normed(current, rows, inverse, extra_ref, normed)

    projected[...] = jnp.dot(normed[...], weights[...], preferred_element_type=jnp.float32).astype(projected.dtype)
    attend_heads(projected, key_ref, value_ref, extra_ref, attended, head_count)
    spot = columns(quarter_of(plane, y), width)
    attended[...] = (
        current[:, spot].astype(jnp.float32) + extra_ref[2:3, :width] * attended[...].astype(jnp.float32)
    ).astype(attended.dtype)
    chip_rows = attended.shape[0] // 2
    rows = chip_rows // 2
    here_rows, there_rows = y * chip_rows, (1 - y) * chip_rows

    def part(start):
        return attended[pl.ds(pl.multiple_of(start, rows), rows), :]

    keep[...] = part(here_rows)
    fourth[...] = part(there_rows + rows)

    @pl.when(at_home)
    def _():
        first[...] = part(there_rows)
        second[...] = part(there_rows + rows)
        third[...] = part(here_rows + rows)

    @pl.when(jnp.logical_not(at_home))
    def _():
        first[...] = part(here_rows + rows)
        second[...] = part(here_rows)
        third[...] = part(there_rows)


MIB = 1024 * 1024


def kernel_call(kernel, out_shape, operands, anywhere, scratch_shapes, limit, flops):
    vectors = pl.BlockSpec(memory_space=pltpu.VMEM)
    free = pl.BlockSpec(memory_space=pl.ANY)
    moved_bytes = sum(operand.size * operand.dtype.itemsize for operand in operands)
    return pl.pallas_call(
        kernel,
        out_shape=out_shape,
        in_specs=[free if number in anywhere else vectors for number in range(len(operands))],
        out_specs=jax.tree.map(lambda _: vectors, out_shape),
        scratch_shapes=scratch_shapes,
        compiler_params=pltpu.CompilerParams(vmem_limit_bytes=limit),
        cost_estimate=pl.CostEstimate(flops=flops, transcendentals=0, bytes_accessed=moved_bytes),
    )(*operands)


def prepare(extra, tokens):
    frame = jax.ShapeDtypeStruct((2 * tokens[0].shape[0], tokens[0].shape[1]), tokens[0].dtype)
    return kernel_call(
        prepare_kernel,
        (jax.ShapeDtypeStruct(extra.shape, extra.dtype), frame, frame),
        (extra, *tokens),
        range(5),
        [pltpu.SemaphoreType.DMA((3,))],
        8 * MIB,
        0,
    )


def project(normed, pieces):
    rows, width = pieces[0][0].shape
    depth = rows * len(pieces)
    return kernel_call(
        functools.partial(project_kernel, tuple(place for _, place in pieces)),
        jax.ShapeDtypeStruct((normed.shape[0], width), jnp.float32),
        (normed, *[array for array, _ in pieces]),
        (),
        [pltpu.VMEM((depth, width), normed.dtype)],
        16 * MIB,
        2 * normed.shape[0] * depth * width,
    )


def assemble(pieces):
    rows, width = pieces[0][0].shape
    return kernel_call(
        functools.partial(assemble_kernel, tuple(place for _, place in pieces)),
        jax.ShapeDtypeStruct((rows * len(pieces), width), pieces[0][0].dtype),
        [array for array, _ in pieces],
        (),
        [],
        8 * MIB,
        0,
    )


def step(extra, keys, values, normed, part, pieces):
    rows, width = pieces[0][0].shape
    depth = rows * len(pieces)
    frame_rows = normed.shape[0]
    return kernel_call(
        functools.partial(step_kernel, tuple(place for _, place in pieces), pieces[0][1][0], HEADS // SPATIAL),
        jax.ShapeDtypeStruct((frame_rows, width // 3), normed.dtype),
        (extra, keys, values, normed, part, *[array for array, _ in pieces]),
        (),
        [pltpu.VMEM((depth, width), normed.dtype), pltpu.VMEM((frame_rows, width), normed.dtype)],
        16 * MIB,
        2 * frame_rows * width * (depth + frame_rows),
    )


def last_step(extra, keys, values, current, weights, updates):
    frame_rows, features = current.shape
    width = weights.shape[1] // 3
    share = jax.ShapeDtypeStruct((frame_rows // 4, width), current.dtype)
    return kernel_call(
        functools.partial(last_step_kernel, tuple(place for _, place in updates), HEADS // SPATIAL),
        (share,) * 5,
        (extra, keys, values, current, weights, *[array for array, _ in updates]),
        (),
        [
            pltpu.VMEM((frame_rows, features), current.dtype),
            pltpu.VMEM((frame_rows, features), current.dtype),
            pltpu.VMEM((frame_rows, 3 * width), current.dtype),
            pltpu.VMEM((frame_rows, width), current.dtype),
        ],
        16 * MIB,
        2 * frame_rows * 3 * width * (features + frame_rows),
    )


def join_kernel(keep, first, second, third, fourth, out):
    _, _, plane, y, c = here()
    low = plane % 2
    width = keep.shape[1]

    def put(ref, plane_low, at_y):
        out[:, columns(plane_low * 2 + at_y, width)] = ref[...]

    @pl.when(low == c)
    def _():
        put(keep, low, y)
        put(first, low, 1 - y)
        put(second, 1 - low, y)
        put(third, 1 - low, 1 - y)

    @pl.when(low != c)
    def _():
        put(first, 1 - low, y)
        put(second, low, 1 - y)
        put(third, low, y)
        put(fourth, 1 - low, 1 - y)


def joined(keep, first, second, third, fourth):
    def at_home(p, c):
        return c == p % 2

    first = moved(first, lambda x, p, y, c: (x, p, 1 - y, c) if at_home(p, c) else (x, p ^ 1, y, 1 - c))
    second = moved(second, lambda x, p, y, c: (x, p, 1 - y, 1 - c) if at_home(p, c) else (x, p ^ 1, y, c))
    third = moved(third, lambda x, p, y, c: (x, p, y, 1 - c) if at_home(p, c) else (x, p ^ 1, 1 - y, c))
    fourth = moved(fourth, lambda x, p, y, c: None if at_home(p, c) else (x, p ^ 1, 1 - y, 1 - c))
    rows, width = keep.shape
    return kernel_call(
        join_kernel,
        jax.ShapeDtypeStruct((rows, width * SPATIAL), keep.dtype),
        (keep, first, second, third, fourth),
        (),
        [],
        4 * MIB,
        0,
    )


def paired_planes(
    latent, norm_gain, w_query, w_key, w_value, mem_cache, intersection, counts, slot_of, step_scale
):
    late = late_plane(lax.axis_size("frame"))
    weights, extra, memory = pack(
        w_query, w_key, w_value, intersection, slot_of, counts, step_scale, norm_gain, mem_cache
    )
    pieces = sorted(all_pieces(*weights), key=lambda piece: piece[1][0])
    tokens = all_tokens(latent)
    keys, values = all_memory(memory)
    extra, current, normed = prepare(extra, tokens)
    part = project(normed, [piece for piece in pieces if piece[1][0] < late])
    attended = step(extra, keys, values, normed, part, [piece for piece in pieces if piece[1][0] == late])
    updates = [
        (attended, (0, 0)),
        (moved(attended, lambda x, p, y, c: (x, p ^ 1, 1 - y, c)), (1, 1)),
        (moved(attended, lambda x, p, y, c: (x, p ^ 1, y, c)), (1, 0)),
        (moved(attended, lambda x, p, y, c: (x, p, 1 - y, c)), (0, 1)),
    ]
    shares = last_step(extra, keys, values, current, assemble(pieces), updates)
    return joined(*shares)


def fits_paired_planes(latent, norm_gain, w_query, w_key, w_value, mem_cache, *_):
    devices = lax.axis_size("frame")
    planes = devices // SPATIAL
    return (
        lax.axis_size("groups") == 2
        and devices == planes * SPATIAL
        and planes >= 2
        and planes & (planes - 1) == 0
        and w_query.shape[0] % 16 == 0
        and mem_cache.shape[1] == 1
    )


def from_partner(array, axis, bit):
    return lax.ppermute(array, axis, [(i, i ^ 1 << bit) for i in range(lax.axis_size(axis))])


def in_order(mine, theirs, upper, axis_dim):
    low_first = jnp.concatenate([mine, theirs], axis=axis_dim)
    high_first = jnp.concatenate([theirs, mine], axis=axis_dim)
    return jnp.where(upper, high_first, low_first)


def attend(queries, frame_pair, mem_keys, mem_values, live_keys, head_count):
    tok_rows, feature_width = queries.shape
    head_size = feature_width // head_count
    scale_dot = 1.0 / math.sqrt(head_size)
    q_heads = queries.reshape(tok_rows, head_count, head_size)
    k_heads = frame_pair[0].reshape(-1, head_count, head_size)
    v_heads = frame_pair[1].reshape(-1, head_count, head_size)
    frame_scores = (
        jnp.einsum("thd,khd->htk", q_heads, k_heads, preferred_element_type=jnp.float32) * scale_dot
    )
    remote_scores = (
        jnp.einsum("thd,khd->htk", q_heads, mem_keys, preferred_element_type=jnp.float32)
        * scale_dot
    )
    remote_scores = jnp.where(live_keys[None, None, :], remote_scores, -1e30)
    largest = jnp.maximum(
        jnp.max(frame_scores, axis=-1, keepdims=True),
        jnp.max(remote_scores, axis=-1, keepdims=True),
    )
    frame_weights = jnp.exp(frame_scores - largest)
    remote_weights = jnp.exp(remote_scores - largest)
    denominator = jnp.sum(frame_weights, axis=-1) + jnp.sum(remote_weights, axis=-1)
    blended = jnp.einsum(
        "htk,khd->thd",
        frame_weights.astype(jnp.bfloat16),
        v_heads,
        preferred_element_type=jnp.float32,
    )
    blended = blended + jnp.einsum(
        "htk,khd->thd",
        remote_weights.astype(jnp.bfloat16),
        mem_values,
        preferred_element_type=jnp.float32,
    )
    blended = blended / jnp.transpose(denominator)[:, :, None]
    return blended.reshape(tok_rows, feature_width).astype(jnp.bfloat16)


def rms_normed(current, norm_gain):
    widened = current.astype(jnp.float32)
    inverse = lax.rsqrt(jnp.mean(widened * widened, axis=-1, keepdims=True) + 1e-06)
    return (widened, (widened * inverse * norm_gain).astype(jnp.bfloat16))


def separate_frames(
    latent, norm_gain, w_query, w_key, w_value, mem_cache, intersection, counts, slot_of, step_scale
):
    devices = lax.axis_size("frame")
    position = lax.axis_index("frame")
    frame_index = position // SPATIAL
    doublings = SPATIAL.bit_length() - 1
    target_frame = jnp.arange(devices, dtype=jnp.int32) // SPATIAL
    current = latent
    feature_width = latent.shape[1]
    share_width = feature_width // SPATIAL
    head_share = HEADS // SPATIAL

    def column_pieces(weight):
        row_count = weight.shape[0]
        split_cols = jnp.transpose(weight.reshape(row_count, SPATIAL, share_width), (1, 0, 2))
        return jnp.tile(split_cols, (devices // SPATIAL, 1, 1))

    own_query, own_key, own_value = (
        lax.all_to_all(column_pieces(w_query), "frame", split_axis=0, concat_axis=1, tiled=True),
        lax.all_to_all(column_pieces(w_key), "frame", split_axis=0, concat_axis=1, tiled=True),
        lax.all_to_all(column_pieces(w_value), "frame", split_axis=0, concat_axis=1, tiled=True),
    )
    own_query, own_key, own_value = (own_query[0], own_key[0], own_value[0])
    listed = mem_cache[slot_of[intersection[target_frame]]]
    list_len = listed.shape[1]
    local_mem = listed.shape[2]
    grouped = listed.reshape(
        devices // SPATIAL, SPATIAL, list_len, local_mem, 2, SPATIAL, share_width
    )
    diagonal_part = jnp.diagonal(grouped, axis1=1, axis2=5)
    outgoing = jnp.moveaxis(diagonal_part, -1, 1).reshape(
        devices, list_len, local_mem, 2, share_width
    )
    fetched = lax.all_to_all(outgoing, "frame", split_axis=0, concat_axis=2, tiled=True)[0]
    mem_len = fetched.shape[1]
    mem_keys = fetched[:, :, 0, :].reshape(list_len * mem_len, head_share, HS)
    mem_values = fetched[:, :, 1, :].reshape(list_len * mem_len, head_share, HS)
    live_keys = jnp.arange(list_len * mem_len, dtype=jnp.int32) // mem_len < counts[frame_index]
    tok_rows = latent.shape[0]
    for step_index in range(STEPS):
        widened, normed = rms_normed(current, norm_gain)
        gathered = normed
        for bit_index in range(doublings):
            partner = from_partner(gathered, "frame", bit_index)
            gathered = in_order(gathered, partner, position >> bit_index & 1 == 1, 0)
        queries = jnp.dot(gathered, own_query, preferred_element_type=jnp.float32).astype(
            jnp.bfloat16
        )
        keys_frame = jnp.dot(gathered, own_key, preferred_element_type=jnp.float32).astype(
            jnp.bfloat16
        )
        values_frame = jnp.dot(gathered, own_value, preferred_element_type=jnp.float32).astype(
            jnp.bfloat16
        )
        frame_pair = jnp.stack([keys_frame, values_frame])
        attended = attend(queries, frame_pair, mem_keys, mem_values, live_keys, head_share)
        blocks = attended.reshape(SPATIAL, tok_rows, share_width)[:, None]
        for bit_index in range(doublings):
            upper = position >> bit_index & 1 == 1
            dest_count = blocks.shape[0]
            paired = blocks.reshape((dest_count // 2, 2) + blocks.shape[1:])
            kept = jnp.where(upper, paired[:, 1], paired[:, 0])
            sent = jnp.where(upper, paired[:, 0], paired[:, 1])
            arrived = from_partner(sent, "frame", bit_index)
            blocks = in_order(kept, arrived, upper, 1)
        joined = jnp.transpose(blocks[0], (1, 0, 2)).reshape(tok_rows, feature_width)
        current = (widened + step_scale[step_index] * joined.astype(jnp.float32)).astype(
            jnp.bfloat16
        )
    return current


def per_device(*arguments):
    return (paired_planes if fits_paired_planes(*arguments) else separate_frames)(*arguments)


def solution(mesh):
    placed = (
        P(("groups", "frame"), None),
        P(),
        P("frame", None),
        P("frame", None),
        P("frame", None),
        P("groups", "frame", None, None),
        P("groups", None),
        P("groups"),
        P("groups"),
        P(),
    )
    return jax.shard_map(
        per_device,
        mesh=mesh,
        in_specs=placed,
        out_specs=P(("groups", "frame"), None),
        check_vma=False,
    )
```

```python
import functools
import math

import jax
import jax.numpy as jnp
from jax import lax
from jax.experimental import pallas as pl
from jax.experimental.pallas import tpu as pltpu
from jax.sharding import PartitionSpec as P


HEADS = 12
HS = 128
SPATIAL = 4
STEPS = 2
AXES = ("groups", "frame")


def coords(index):
    return index // 4, (index // 2) % 2, index % 2


def quarter_of(plane, y):
    return (plane % 2) * 2 + y


def moved(array, target):
    devices = lax.axis_size("frame")
    pairs = []
    for x in range(lax.axis_size("groups")):
        for index in range(devices):
            place = target(x, *coords(index))
            if place is not None:
                to_x, to_plane, to_y, to_c = place
                pairs.append((x * devices + index, to_x * devices + to_plane * 4 + to_y * 2 + to_c))
    return lax.ppermute(array, AXES, pairs)


def here():
    x = lax.axis_index("groups")
    index = lax.axis_index("frame")
    plane = index // 4
    rest = index - plane * 4
    y = rest // 2
    return x, index, plane, y, rest - y * 2


def flipped(value, bits):
    out = value
    bit = 1
    while bit <= bits:
        if bits & bit:
            out = out + bit - 2 * bit * ((value // bit) % 2)
        bit *= 2
    return out


def joined_bits(one, other):
    return one + other - 2 * one * other


def columns(quarter, width):
    return pl.ds(pl.multiple_of(quarter * width, 128), width)


def pack_kernel(
    w_query, w_key, w_value, list_hbm, slot_hbm, count_hbm, scale_hbm, gain_hbm, mem_ref,
    own_ref, beside_ref, even_ref, odd_ref, extra_ref, *refs,
):
    near_count = SPATIAL
    memory_refs = refs[:near_count]
    (
        list_ref, slot_ref, count_ref, scale_ref, gain, rows, stored, extra, row_sem, out_sem, scalar_sem, mem_sem, give_sem,
    ) = refs[near_count:]
    x, index, plane, y, c = here()
    devices = lax.axis_size("frame")
    frames, entries = list_ref.shape
    width = own_ref.shape[1] // 3
    scalars = [
        pltpu.make_async_copy(source, target, scalar_sem.at[number])
        for number, (source, target) in enumerate(
            (
                (list_hbm, list_ref),
                (slot_hbm, slot_ref),
                (count_hbm, count_ref),
                (scale_hbm, scale_ref),
                (gain_hbm, gain),
            )
        )
    ]
    for copy in scalars[:2]:
        copy.start()
    reads = []
    for number, weight in enumerate((w_query, w_key, w_value)):
        reads.append(pltpu.make_async_copy(weight, rows.at[number], row_sem.at[number]))
        reads[-1].start()
    for copy in scalars[2:]:
        copy.start()
    for copy in scalars[:2]:
        copy.wait()
    picks = []
    for frame in range(frames):
        for entry in range(entries):
            number = frame * entries + entry
            row = slot_ref[list_ref[frame, entry]]
            picks.append(pltpu.make_async_copy(mem_ref.at[row, 0], stored.at[number], mem_sem.at[number]))
            picks[-1].start()
    across = joined_bits(joined_bits(x, y), c)
    low = plane % 2
    quarters = (low * 2 + across, (1 - low) * 2 + across, low * 2 + 1 - y, quarter_of(plane, y))
    gives = []
    for number, read in enumerate(reads):
        read.wait()
        for place, (quarter, out) in enumerate(zip(quarters, (even_ref, odd_ref, beside_ref, own_ref))):
            gives.append(
                pltpu.make_async_copy(
                    rows.at[number, :, columns(quarter, width)],
                    out.at[:, pl.ds(number * width, width)],
                    out_sem.at[number, place],
                )
            )
            gives[-1].start()
    for copy in scalars[2:]:
        copy.wait()
    row = (1, extra.shape[1])
    extra[0:1, :] = gain[...].reshape(row)
    for number in range(STEPS):
        extra[1 + number : 2 + number, :] = jnp.full(row, scale_ref[number], jnp.float32)
    live = lax.broadcasted_iota(jnp.int32, row, 1) % entries < count_ref[(plane // 2) * 2 + c]
    extra[1 + STEPS : 2 + STEPS, :] = jnp.where(live, 1.0, 0.0)
    gives.append(pltpu.make_async_copy(extra, extra_ref, scalar_sem.at[5]))
    gives[-1].start()
    for pick in picks:
        pick.wait()
    bits = devices.bit_length() - 1
    for away in range(devices):
        to_plane, to_y, to_c = coords(flipped(index, away))
        to_frame = (to_plane // 2) * 2 + to_c
        place = 0
        for bit in range(2, bits):
            place = place * 2 + (away >> bit & 1)
        gives.append(
            pltpu.make_async_copy(
                stored.at[pl.ds(to_frame * entries, entries), :, columns(quarter_of(to_plane, to_y), width)],
                memory_refs[away % SPATIAL].at[place],
                give_sem.at[away],
            )
        )
        gives[-1].start()
    for give in gives:
        give.wait()


def pack(w_query, w_key, w_value, intersection, slot_of, counts, step_scale, norm_gain, mem_cache):
    devices = lax.axis_size("frame")
    shard_rows, features = w_query.shape
    frames, entries = intersection.shape
    piece = jax.ShapeDtypeStruct((shard_rows, 3 * (features // SPATIAL)), w_query.dtype)
    small = jax.ShapeDtypeStruct((2 + STEPS, features), jnp.float32)
    memory = jax.ShapeDtypeStruct((devices // SPATIAL, entries, 2, features // SPATIAL), mem_cache.dtype)
    out_shape = (piece,) * 4 + (small,) + (memory,) * SPATIAL
    anywhere = pl.BlockSpec(memory_space=pl.ANY)
    held = pl.BlockSpec(memory_space=pltpu.HBM)
    outs = pl.pallas_call(
        pack_kernel,
        out_shape=out_shape,
        in_specs=[held] * 9,
        out_specs=(anywhere,) * len(out_shape),
        scratch_shapes=[
            pltpu.SMEM(intersection.shape, intersection.dtype),
            pltpu.SMEM(slot_of.shape, slot_of.dtype),
            pltpu.SMEM(counts.shape, counts.dtype),
            pltpu.SMEM(step_scale.shape, step_scale.dtype),
            pltpu.VMEM(norm_gain.shape, norm_gain.dtype),
            pltpu.VMEM((3, shard_rows, features), w_query.dtype),
            pltpu.VMEM((frames * entries, 2, features), mem_cache.dtype),
            pltpu.VMEM(small.shape, small.dtype),
            pltpu.SemaphoreType.DMA((3,)),
            pltpu.SemaphoreType.DMA((3, 4)),
            pltpu.SemaphoreType.DMA((6,)),
            pltpu.SemaphoreType.DMA((frames * entries,)),
            pltpu.SemaphoreType.DMA((devices,)),
        ],
        name="pack",
    )(w_query, w_key, w_value, intersection, slot_of, counts, step_scale, norm_gain, mem_cache)
    return outs[:4], outs[4], outs[5:]


def all_pieces(own, beside, even, odd):
    late = late_plane(lax.axis_size("frame"))

    def direct(bits):
        sent = even if bits % 2 == 0 else odd
        return moved(sent, lambda x, p, y, c: (x, p ^ bits, y ^ x ^ c, c))

    near = moved(beside, lambda x, p, y, c: (x, p, 1 - y, c))
    pieces = [("own", own, [(0, 0, False)]), ("near", near, [(0, 1, False)])]
    early = list(range(1, late))
    for name, bits_list in (("early", early), ("late", [late])):
        if not bits_list:
            continue
        arrays = [direct(bits) for bits in bits_list]
        if len(arrays) > 1:
            arrays = [jnp.concatenate(arrays)]
        pieces.append((name, arrays[0], [(bits, 0, True) for bits in bits_list]))
        crossed = moved(arrays[0], lambda x, p, y, c: (1 - x, p, y, c))
        pieces.append((f"cross_{name}", crossed, [(bits, 1, True) for bits in bits_list]))
    found = [(array, tuple(place + (0,) for place in places)) for _, array, places in pieces]
    for name, array, places in pieces:
        swapped = moved(array, lambda x, p, y, c: (x, p, y, 1 - c))
        found.append((swapped, tuple(place + (1,) for place in places)))
    return found


def all_memory(parts):
    devices = lax.axis_size("frame")
    near = [parts[0]] + [hop(part, place) for place, part in enumerate(parts) if place]
    held = jnp.stack(near)
    for bit in range(2, devices.bit_length() - 1):
        half = held.shape[1] // 2
        arrived = hop(held[:, half:], 1 << bit)
        held = jnp.concatenate([held[:, :half], arrived])
    keys, values = held[:, 0, :, 0, :], held[:, 0, :, 1, :]
    return keys.reshape(-1, keys.shape[-1]), values.reshape(-1, values.shape[-1])


def hop(array, bits):
    return lax.ppermute(array, "frame", [(i, i ^ bits) for i in range(lax.axis_size("frame"))])


def all_tokens(latent):
    other = moved(latent, lambda x, p, y, c: (x, p, y, 1 - c) if c != p % 2 else None)
    block = jnp.concatenate([latent, other])
    near = moved(block, lambda x, p, y, c: (x, p, 1 - y, c) if c == p % 2 else None)
    far = moved(block, lambda x, p, y, c: (x, p ^ 1, y, c) if c == p % 2 else None)
    far_near = moved(far, lambda x, p, y, c: (x, p, 1 - y, c) if c != p % 2 else None)
    return block, near, far, far_near


def late_plane(devices):
    return devices // 4 - 1


def piece_start(place, shard_rows, plane_number):
    x, _, _, y, c = here()
    _, y_bits, with_x, c_bits = place
    from_y, from_c = flipped(y, y_bits), flipped(c, c_bits)
    if with_x:
        from_y = joined_bits(joined_bits(from_y, x), from_c)
    return pl.multiple_of((plane_number * 4 + from_y * 2 + from_c) * shard_rows, 16)


def gather_pieces(piece_refs, places, first_plane, weights):
    for ref, shards in zip(piece_refs, places):
        rows = ref.shape[0] // len(shards)
        for number, place in enumerate(shards):
            start = piece_start(place, rows, place[0] - first_plane)
            weights[pl.ds(start, rows), :] = ref[number * rows : (number + 1) * rows, :]


def store_normed(current, rows, inverse, gain_ref, normed):
    _, _, plane, _, _ = here()
    planes = lax.axis_size("frame") // 4
    span = current.shape[1] // planes
    for bits in range(planes):
        spot = columns(flipped(plane, bits), span)
        widened = current[rows, spot].astype(jnp.float32)
        normed[rows, bits * span : (bits + 1) * span] = (widened * inverse * gain_ref[0:1, spot]).astype(normed.dtype)


BLOCK = 32


def prepare_kernel(extra_ref, block, near, far, far_near, extra, current, normed):
    _, _, plane, y, c = here()
    chip_rows = block.shape[0]
    blocks = chip_rows // BLOCK
    extra[...] = extra_ref[...]

    def fill(first, second):
        @pl.loop(0, blocks)
        def _(number):
            for ref, base in ((first, y * chip_rows), (second, (1 - y) * chip_rows)):
                tokens = ref[pl.ds(pl.multiple_of(number * BLOCK, BLOCK), BLOCK), :]
                rows = pl.ds(pl.multiple_of(base + number * BLOCK, BLOCK), BLOCK)
                current[rows, :] = tokens
                widened = tokens.astype(jnp.float32)
                inverse = lax.rsqrt(jnp.mean(widened * widened, axis=-1, keepdims=True) + 1e-06)
                store_normed(current, rows, inverse, extra, normed)

    pl.when(plane % 2 == c)(lambda: fill(block, near))
    pl.when(plane % 2 != c)(lambda: fill(far, far_near))


def project_kernel(places, *refs):
    normed = refs[0]
    piece_refs = refs[1 : 1 + len(places)]
    out, weights = refs[1 + len(places) :]
    gather_pieces(piece_refs, places, 0, weights)
    out[...] = jnp.dot(normed[:, : weights.shape[0]], weights[...], preferred_element_type=jnp.float32)


def assemble_kernel(places, *refs):
    gather_pieces(refs[:-1], places, 0, refs[-1])


def attend_heads(projected, key_ref, value_ref, extra_ref, attended, head_count):
    width = projected.shape[1] // 3
    head_size = width // head_count
    scale_dot = 1.0 / math.sqrt(head_size)
    mem_rows = key_ref.shape[0]
    live = extra_ref[3:4, :mem_rows] > 0.5
    contract_last = (((1,), (1,)), ((), ()))
    frame_rows = projected.shape[0]
    half = frame_rows // 2
    for head in range(head_count):
        span = slice(head * head_size, (head + 1) * head_size)
        keys = projected[:, width + head * head_size : width + (head + 1) * head_size]
        values = projected[:, 2 * width + head * head_size : 2 * width + (head + 1) * head_size]
        for start in range(0, frame_rows, half):
            queries = projected[start : start + half, span]
            frame_scores = (
                lax.dot_general(queries, keys, contract_last, preferred_element_type=jnp.float32) * scale_dot
            )
            mem_scores = (
                lax.dot_general(queries, key_ref[:, span], contract_last, preferred_element_type=jnp.float32)
                * scale_dot
            )
            scores = jnp.concatenate([frame_scores, jnp.where(live, mem_scores, -1e30)], axis=1)
            weights = jnp.exp(scores - jnp.max(scores, axis=-1, keepdims=True))
            denominator = jnp.sum(weights, axis=-1, keepdims=True)
            rounded = weights.astype(jnp.bfloat16)
            blended = jnp.dot(
                rounded[:, :frame_rows], values, preferred_element_type=jnp.float32
            ) + jnp.dot(rounded[:, frame_rows:], value_ref[:, span], preferred_element_type=jnp.float32)
            attended[start : start + half, span] = (blended / denominator).astype(attended.dtype)


def step_kernel(places, first_plane, head_count, extra_ref, key_ref, value_ref, normed, part_ref, *refs):
    piece_refs = refs[: len(places)]
    attended, weights, projected = refs[len(places) :]
    gather_pieces(piece_refs, places, first_plane, weights)
    early = normed.shape[1] - weights.shape[0]
    projected[...] = (
        part_ref[...] + jnp.dot(normed[:, early:], weights[...], preferred_element_type=jnp.float32)
    ).astype(projected.dtype)
    attend_heads(projected, key_ref, value_ref, extra_ref, attended, head_count)


def last_step_kernel(
    update_places, head_count, extra_ref, key_ref, value_ref, current_ref, weights, first_part, second_part, third_part,
    fourth_part, keep, first, second, third, fourth, current, normed, projected, attended,
):
    _, _, plane, y, c = here()
    width = first_part.shape[1]
    at_home = plane % 2 == c

    @pl.loop(0, current.shape[0] // BLOCK)
    def _(number):
        rows = pl.ds(pl.multiple_of(number * BLOCK, BLOCK), BLOCK)
        total = jnp.zeros((BLOCK, 1), jnp.float32)
        for part, (plane_bits, y_bits) in zip((first_part, second_part, third_part, fourth_part), update_places):
            spot = columns(quarter_of(flipped(plane, plane_bits), flipped(y, y_bits)), width)
            updated = (
                current_ref[rows, spot].astype(jnp.float32)
                + extra_ref[1:2, :width] * part[rows, :].astype(jnp.float32)
            ).astype(current.dtype)
            current[rows, spot] = updated
            widened = updated.astype(jnp.float32)
            total = total + jnp.sum(widened * widened, axis=-1, keepdims=True)
        inverse = lax.rsqrt(total / current.shape[1] + 1e-06)
        store_normed(current, rows, inverse, extra_ref, normed)

    projected[...] = jnp.dot(normed[...], weights[...], preferred_element_type=jnp.float32).astype(projected.dtype)
    attend_heads(projected, key_ref, value_ref, extra_ref, attended, head_count)
    spot = columns(quarter_of(plane, y), width)
    attended[...] = (
        current[:, spot].astype(jnp.float32) + extra_ref[2:3, :width] * attended[...].astype(jnp.float32)
    ).astype(attended.dtype)
    chip_rows = attended.shape[0] // 2
    rows = chip_rows // 2
    here_rows, there_rows = y * chip_rows, (1 - y) * chip_rows

    def part(start):
        return attended[pl.ds(pl.multiple_of(start, rows), rows), :]

    keep[...] = part(here_rows)
    fourth[...] = part(there_rows + rows)

    @pl.when(at_home)
    def _():
        first[...] = part(there_rows)
        second[...] = part(there_rows + rows)
        third[...] = part(here_rows + rows)

    @pl.when(jnp.logical_not(at_home))
    def _():
        first[...] = part(here_rows + rows)
        second[...] = part(here_rows)
        third[...] = part(there_rows)


MIB = 1024 * 1024


def kernel_call(kernel, out_shape, operands, anywhere, scratch_shapes, limit, flops):
    vectors = pl.BlockSpec(memory_space=pltpu.VMEM)
    free = pl.BlockSpec(memory_space=pl.ANY)
    moved_bytes = sum(operand.size * operand.dtype.itemsize for operand in operands)
    return pl.pallas_call(
        kernel,
        out_shape=out_shape,
        in_specs=[free if number in anywhere else vectors for number in range(len(operands))],
        out_specs=jax.tree.map(lambda _: vectors, out_shape),
        scratch_shapes=scratch_shapes,
        compiler_params=pltpu.CompilerParams(vmem_limit_bytes=limit),
        cost_estimate=pl.CostEstimate(flops=flops, transcendentals=0, bytes_accessed=moved_bytes),
    )(*operands)


def prepare(extra, tokens):
    frame = jax.ShapeDtypeStruct((2 * tokens[0].shape[0], tokens[0].shape[1]), tokens[0].dtype)
    return kernel_call(
        prepare_kernel,
        (jax.ShapeDtypeStruct(extra.shape, extra.dtype), frame, frame),
        (extra, *tokens),
        (),
        [],
        8 * MIB,
        0,
    )


def project(normed, pieces):
    width = pieces[0][0].shape[1]
    depth = sum(array.shape[0] for array, _ in pieces)
    return kernel_call(
        functools.partial(project_kernel, tuple(place for _, place in pieces)),
        jax.ShapeDtypeStruct((normed.shape[0], width), jnp.float32),
        (normed, *[array for array, _ in pieces]),
        (),
        [pltpu.VMEM((depth, width), normed.dtype)],
        16 * MIB,
        2 * normed.shape[0] * depth * width,
    )


def assemble(pieces):
    width = pieces[0][0].shape[1]
    depth = sum(array.shape[0] for array, _ in pieces)
    return kernel_call(
        functools.partial(assemble_kernel, tuple(place for _, place in pieces)),
        jax.ShapeDtypeStruct((depth, width), pieces[0][0].dtype),
        [array for array, _ in pieces],
        (),
        [],
        8 * MIB,
        0,
    )


def step(extra, keys, values, normed, part, pieces):
    width = pieces[0][0].shape[1]
    depth = sum(array.shape[0] for array, _ in pieces)
    frame_rows = normed.shape[0]
    return kernel_call(
        functools.partial(step_kernel, tuple(place for _, place in pieces), pieces[0][1][0][0], HEADS // SPATIAL),
        jax.ShapeDtypeStruct((frame_rows, width // 3), normed.dtype),
        (extra, keys, values, normed, part, *[array for array, _ in pieces]),
        (),
        [pltpu.VMEM((depth, width), normed.dtype), pltpu.VMEM((frame_rows, width), normed.dtype)],
        16 * MIB,
        2 * frame_rows * width * (depth + frame_rows),
    )


def last_step(extra, keys, values, current, weights, updates):
    frame_rows, features = current.shape
    width = weights.shape[1] // 3
    share = jax.ShapeDtypeStruct((frame_rows // 4, width), current.dtype)
    return kernel_call(
        functools.partial(last_step_kernel, tuple(place for _, place in updates), HEADS // SPATIAL),
        (share,) * 5,
        (extra, keys, values, current, weights, *[array for array, _ in updates]),
        (),
        [
            pltpu.VMEM((frame_rows, features), current.dtype),
            pltpu.VMEM((frame_rows, features), current.dtype),
            pltpu.VMEM((frame_rows, 3 * width), current.dtype),
            pltpu.VMEM((frame_rows, width), current.dtype),
        ],
        16 * MIB,
        2 * frame_rows * 3 * width * (features + frame_rows),
    )


def join_kernel(keep, first, second, third, fourth, out):
    _, _, plane, y, c = here()
    low = plane % 2
    width = keep.shape[1]

    def put(ref, plane_low, at_y):
        out[:, columns(plane_low * 2 + at_y, width)] = ref[...]

    @pl.when(low == c)
    def _():
        put(keep, low, y)
        put(first, low, 1 - y)
        put(second, 1 - low, y)
        put(third, 1 - low, 1 - y)

    @pl.when(low != c)
    def _():
        put(first, 1 - low, y)
        put(second, low, 1 - y)
        put(third, low, y)
        put(fourth, 1 - low, 1 - y)


def joined(keep, first, second, third, fourth):
    def at_home(p, c):
        return c == p % 2

    first = moved(first, lambda x, p, y, c: (x, p, 1 - y, c) if at_home(p, c) else (x, p ^ 1, y, 1 - c))
    second = moved(second, lambda x, p, y, c: (x, p, 1 - y, 1 - c) if at_home(p, c) else (x, p ^ 1, y, c))
    third = moved(third, lambda x, p, y, c: (x, p, y, 1 - c) if at_home(p, c) else (x, p ^ 1, 1 - y, c))
    fourth = moved(fourth, lambda x, p, y, c: None if at_home(p, c) else (x, p ^ 1, 1 - y, 1 - c))
    rows, width = keep.shape
    return kernel_call(
        join_kernel,
        jax.ShapeDtypeStruct((rows, width * SPATIAL), keep.dtype),
        (keep, first, second, third, fourth),
        (),
        [],
        4 * MIB,
        0,
    )


def paired_planes(
    latent, norm_gain, w_query, w_key, w_value, mem_cache, intersection, counts, slot_of, step_scale
):
    late = late_plane(lax.axis_size("frame"))
    weights, extra, memory = pack(
        w_query, w_key, w_value, intersection, slot_of, counts, step_scale, norm_gain, mem_cache
    )
    pieces = all_pieces(*weights)
    tokens = all_tokens(latent)
    keys, values = all_memory(memory)
    extra, current, normed = prepare(extra, tokens)
    part = project(normed, [piece for piece in pieces if piece[1][0][0] < late])
    attended = step(extra, keys, values, normed, part, [piece for piece in pieces if piece[1][0][0] == late])
    updates = [
        (attended, (0, 0)),
        (moved(attended, lambda x, p, y, c: (x, p ^ 1, 1 - y, c)), (1, 1)),
        (moved(attended, lambda x, p, y, c: (x, p ^ 1, y, c)), (1, 0)),
        (moved(attended, lambda x, p, y, c: (x, p, 1 - y, c)), (0, 1)),
    ]
    shares = last_step(extra, keys, values, current, assemble(pieces), updates)
    return joined(*shares)


def fits_paired_planes(latent, norm_gain, w_query, w_key, w_value, mem_cache, *_):
    devices = lax.axis_size("frame")
    planes = devices // SPATIAL
    return (
        lax.axis_size("groups") == 2
        and devices == planes * SPATIAL
        and planes >= 2
        and planes & (planes - 1) == 0
        and w_query.shape[0] % 16 == 0
        and mem_cache.shape[1] == 1
    )


def from_partner(array, axis, bit):
    return lax.ppermute(array, axis, [(i, i ^ 1 << bit) for i in range(lax.axis_size(axis))])


def in_order(mine, theirs, upper, axis_dim):
    low_first = jnp.concatenate([mine, theirs], axis=axis_dim)
    high_first = jnp.concatenate([theirs, mine], axis=axis_dim)
    return jnp.where(upper, high_first, low_first)


def attend(queries, frame_pair, mem_keys, mem_values, live_keys, head_count):
    tok_rows, feature_width = queries.shape
    head_size = feature_width // head_count
    scale_dot = 1.0 / math.sqrt(head_size)
    q_heads = queries.reshape(tok_rows, head_count, head_size)
    k_heads = frame_pair[0].reshape(-1, head_count, head_size)
    v_heads = frame_pair[1].reshape(-1, head_count, head_size)
    frame_scores = (
        jnp.einsum("thd,khd->htk", q_heads, k_heads, preferred_element_type=jnp.float32) * scale_dot
    )
    remote_scores = (
        jnp.einsum("thd,khd->htk", q_heads, mem_keys, preferred_element_type=jnp.float32)
        * scale_dot
    )
    remote_scores = jnp.where(live_keys[None, None, :], remote_scores, -1e30)
    largest = jnp.maximum(
        jnp.max(frame_scores, axis=-1, keepdims=True),
        jnp.max(remote_scores, axis=-1, keepdims=True),
    )
    frame_weights = jnp.exp(frame_scores - largest)
    remote_weights = jnp.exp(remote_scores - largest)
    denominator = jnp.sum(frame_weights, axis=-1) + jnp.sum(remote_weights, axis=-1)
    blended = jnp.einsum(
        "htk,khd->thd",
        frame_weights.astype(jnp.bfloat16),
        v_heads,
        preferred_element_type=jnp.float32,
    )
    blended = blended + jnp.einsum(
        "htk,khd->thd",
        remote_weights.astype(jnp.bfloat16),
        mem_values,
        preferred_element_type=jnp.float32,
    )
    blended = blended / jnp.transpose(denominator)[:, :, None]
    return blended.reshape(tok_rows, feature_width).astype(jnp.bfloat16)


def rms_normed(current, norm_gain):
    widened = current.astype(jnp.float32)
    inverse = lax.rsqrt(jnp.mean(widened * widened, axis=-1, keepdims=True) + 1e-06)
    return (widened, (widened * inverse * norm_gain).astype(jnp.bfloat16))


def separate_frames(
    latent, norm_gain, w_query, w_key, w_value, mem_cache, intersection, counts, slot_of, step_scale
):
    devices = lax.axis_size("frame")
    position = lax.axis_index("frame")
    frame_index = position // SPATIAL
    doublings = SPATIAL.bit_length() - 1
    target_frame = jnp.arange(devices, dtype=jnp.int32) // SPATIAL
    current = latent
    feature_width = latent.shape[1]
    share_width = feature_width // SPATIAL
    head_share = HEADS // SPATIAL

    def column_pieces(weight):
        row_count = weight.shape[0]
        split_cols = jnp.transpose(weight.reshape(row_count, SPATIAL, share_width), (1, 0, 2))
        return jnp.tile(split_cols, (devices // SPATIAL, 1, 1))

    own_query, own_key, own_value = (
        lax.all_to_all(column_pieces(w_query), "frame", split_axis=0, concat_axis=1, tiled=True),
        lax.all_to_all(column_pieces(w_key), "frame", split_axis=0, concat_axis=1, tiled=True),
        lax.all_to_all(column_pieces(w_value), "frame", split_axis=0, concat_axis=1, tiled=True),
    )
    own_query, own_key, own_value = (own_query[0], own_key[0], own_value[0])
    listed = mem_cache[slot_of[intersection[target_frame]]]
    list_len = listed.shape[1]
    local_mem = listed.shape[2]
    grouped = listed.reshape(
        devices // SPATIAL, SPATIAL, list_len, local_mem, 2, SPATIAL, share_width
    )
    diagonal_part = jnp.diagonal(grouped, axis1=1, axis2=5)
    outgoing = jnp.moveaxis(diagonal_part, -1, 1).reshape(
        devices, list_len, local_mem, 2, share_width
    )
    fetched = lax.all_to_all(outgoing, "frame", split_axis=0, concat_axis=2, tiled=True)[0]
    mem_len = fetched.shape[1]
    mem_keys = fetched[:, :, 0, :].reshape(list_len * mem_len, head_share, HS)
    mem_values = fetched[:, :, 1, :].reshape(list_len * mem_len, head_share, HS)
    live_keys = jnp.arange(list_len * mem_len, dtype=jnp.int32) // mem_len < counts[frame_index]
    tok_rows = latent.shape[0]
    for step_index in range(STEPS):
        widened, normed = rms_normed(current, norm_gain)
        gathered = normed
        for bit_index in range(doublings):
            partner = from_partner(gathered, "frame", bit_index)
            gathered = in_order(gathered, partner, position >> bit_index & 1 == 1, 0)
        queries = jnp.dot(gathered, own_query, preferred_element_type=jnp.float32).astype(
            jnp.bfloat16
        )
        keys_frame = jnp.dot(gathered, own_key, preferred_element_type=jnp.float32).astype(
            jnp.bfloat16
        )
        values_frame = jnp.dot(gathered, own_value, preferred_element_type=jnp.float32).astype(
            jnp.bfloat16
        )
        frame_pair = jnp.stack([keys_frame, values_frame])
        attended = attend(queries, frame_pair, mem_keys, mem_values, live_keys, head_share)
        blocks = attended.reshape(SPATIAL, tok_rows, share_width)[:, None]
        for bit_index in range(doublings):
            upper = position >> bit_index & 1 == 1
            dest_count = blocks.shape[0]
            paired = blocks.reshape((dest_count // 2, 2) + blocks.shape[1:])
            kept = jnp.where(upper, paired[:, 1], paired[:, 0])
            sent = jnp.where(upper, paired[:, 0], paired[:, 1])
            arrived = from_partner(sent, "frame", bit_index)
            blocks = in_order(kept, arrived, upper, 1)
        joined = jnp.transpose(blocks[0], (1, 0, 2)).reshape(tok_rows, feature_width)
        current = (widened + step_scale[step_index] * joined.astype(jnp.float32)).astype(
            jnp.bfloat16
        )
    return current


def per_device(*arguments):
    return (paired_planes if fits_paired_planes(*arguments) else separate_frames)(*arguments)


def solution(mesh):
    placed = (
        P(("groups", "frame"), None),
        P(),
        P("frame", None),
        P("frame", None),
        P("frame", None),
        P("groups", "frame", None, None),
        P("groups", None),
        P("groups"),
        P("groups"),
        P(),
    )
    return jax.shard_map(
        per_device,
        mesh=mesh,
        in_specs=placed,
        out_specs=P(("groups", "frame"), None),
        check_vma=False,
    )
```

```python
import functools
import math

import jax
import jax.numpy as jnp
from jax import lax
from jax.experimental import pallas as pl
from jax.experimental.pallas import tpu as pltpu
from jax.sharding import PartitionSpec as P


HEADS = 12
HS = 128
SPATIAL = 4
STEPS = 2
AXES = ("groups", "frame")


def coords(index):
    return index // 4, (index // 2) % 2, index % 2


def quarter_of(plane, y):
    return (plane % 2) * 2 + y


def moved(array, target):
    devices = lax.axis_size("frame")
    pairs = []
    for x in range(lax.axis_size("groups")):
        for index in range(devices):
            place = target(x, *coords(index))
            if place is not None:
                to_x, to_plane, to_y, to_c = place
                pairs.append((x * devices + index, to_x * devices + to_plane * 4 + to_y * 2 + to_c))
    return lax.ppermute(array, AXES, pairs)


def here():
    x = lax.axis_index("groups")
    index = lax.axis_index("frame")
    plane = index // 4
    rest = index - plane * 4
    y = rest // 2
    return x, index, plane, y, rest - y * 2


def flipped(value, bits):
    out = value
    bit = 1
    while bit <= bits:
        if bits & bit:
            out = out + bit - 2 * bit * ((value // bit) % 2)
        bit *= 2
    return out


def joined_bits(one, other):
    return one + other - 2 * one * other


def columns(quarter, width):
    return pl.ds(pl.multiple_of(quarter * width, 128), width)


def pack_kernel(
    w_query, w_key, w_value, list_hbm, slot_hbm, count_hbm, scale_hbm, gain_hbm, mem_ref,
    own_ref, beside_ref, even_ref, odd_ref, extra_ref, *refs,
):
    near_count = SPATIAL
    memory_refs = refs[:near_count]
    (
        list_ref, slot_ref, count_ref, scale_ref, gain, rows, stored, extra, row_sem, out_sem, scalar_sem, mem_sem, give_sem,
    ) = refs[near_count:]
    x, index, plane, y, c = here()
    devices = lax.axis_size("frame")
    frames, entries = list_ref.shape
    width = own_ref.shape[1] // 3
    scalars = [
        pltpu.make_async_copy(source, target, scalar_sem.at[number])
        for number, (source, target) in enumerate(
            (
                (list_hbm, list_ref),
                (slot_hbm, slot_ref),
                (count_hbm, count_ref),
                (scale_hbm, scale_ref),
                (gain_hbm, gain),
            )
        )
    ]
    for copy in scalars[:2]:
        copy.start()
    reads = []
    for number, weight in enumerate((w_query, w_key, w_value)):
        reads.append(pltpu.make_async_copy(weight, rows.at[number], row_sem.at[number]))
        reads[-1].start()
    for copy in scalars[2:]:
        copy.start()
    for copy in scalars[:2]:
        copy.wait()
    picks = []
    for frame in range(frames):
        for entry in range(entries):
            number = frame * entries + entry
            row = slot_ref[list_ref[frame, entry]]
            picks.append(pltpu.make_async_copy(mem_ref.at[row, 0], stored.at[number], mem_sem.at[number]))
            picks[-1].start()
    across = joined_bits(joined_bits(x, y), c)
    low = plane % 2
    quarters = (low * 2 + across, (1 - low) * 2 + across, low * 2 + 1 - y, quarter_of(plane, y))
    gives = []
    for number, read in enumerate(reads):
        read.wait()
        for place, (quarter, out) in enumerate(zip(quarters, (even_ref, odd_ref, beside_ref, own_ref))):
            gives.append(
                pltpu.make_async_copy(
                    rows.at[number, :, columns(quarter, width)],
                    out.at[:, pl.ds(number * width, width)],
                    out_sem.at[number, place],
                )
            )
            gives[-1].start()
    for copy in scalars[2:]:
        copy.wait()
    row = (1, extra.shape[1])
    extra[0:1, :] = gain[...].reshape(row)
    for number in range(STEPS):
        extra[1 + number : 2 + number, :] = jnp.full(row, scale_ref[number], jnp.float32)
    live = lax.broadcasted_iota(jnp.int32, row, 1) % entries < count_ref[(plane // 2) * 2 + c]
    extra[1 + STEPS : 2 + STEPS, :] = jnp.where(live, 1.0, 0.0)
    gives.append(pltpu.make_async_copy(extra, extra_ref, scalar_sem.at[5]))
    gives[-1].start()
    for pick in picks:
        pick.wait()
    bits = devices.bit_length() - 1
    for away in range(devices):
        to_plane, to_y, to_c = coords(flipped(index, away))
        to_frame = (to_plane // 2) * 2 + to_c
        place = 0
        for bit in range(2, bits):
            place = place * 2 + (away >> bit & 1)
        gives.append(
            pltpu.make_async_copy(
                stored.at[pl.ds(to_frame * entries, entries), :, columns(quarter_of(to_plane, to_y), width)],
                memory_refs[away % SPATIAL].at[place],
                give_sem.at[away],
            )
        )
        gives[-1].start()
    for give in gives:
        give.wait()


def pack(w_query, w_key, w_value, intersection, slot_of, counts, step_scale, norm_gain, mem_cache):
    devices = lax.axis_size("frame")
    shard_rows, features = w_query.shape
    frames, entries = intersection.shape
    piece = jax.ShapeDtypeStruct((shard_rows, 3 * (features // SPATIAL)), w_query.dtype)
    small = jax.ShapeDtypeStruct((2 + STEPS, features), jnp.float32)
    memory = jax.ShapeDtypeStruct((devices // SPATIAL, entries, 2, features // SPATIAL), mem_cache.dtype)
    out_shape = (piece,) * 4 + (small,) + (memory,) * SPATIAL
    anywhere = pl.BlockSpec(memory_space=pl.ANY)
    held = pl.BlockSpec(memory_space=pltpu.HBM)
    outs = pl.pallas_call(
        pack_kernel,
        out_shape=out_shape,
        in_specs=[held] * 9,
        out_specs=(anywhere,) * len(out_shape),
        scratch_shapes=[
            pltpu.SMEM(intersection.shape, intersection.dtype),
            pltpu.SMEM(slot_of.shape, slot_of.dtype),
            pltpu.SMEM(counts.shape, counts.dtype),
            pltpu.SMEM(step_scale.shape, step_scale.dtype),
            pltpu.VMEM(norm_gain.shape, norm_gain.dtype),
            pltpu.VMEM((3, shard_rows, features), w_query.dtype),
            pltpu.VMEM((frames * entries, 2, features), mem_cache.dtype),
            pltpu.VMEM(small.shape, small.dtype),
            pltpu.SemaphoreType.DMA((3,)),
            pltpu.SemaphoreType.DMA((3, 4)),
            pltpu.SemaphoreType.DMA((6,)),
            pltpu.SemaphoreType.DMA((frames * entries,)),
            pltpu.SemaphoreType.DMA((devices,)),
        ],
        name="pack",
    )(w_query, w_key, w_value, intersection, slot_of, counts, step_scale, norm_gain, mem_cache)
    return outs[:4], outs[4], outs[5:]


def all_pieces(own, beside, even, odd):
    late = late_plane(lax.axis_size("frame"))

    def direct(bits):
        sent = even if bits % 2 == 0 else odd
        return moved(sent, lambda x, p, y, c: (x, p ^ bits, y ^ x ^ c, c))

    near = moved(beside, lambda x, p, y, c: (x, p, 1 - y, c))
    pieces = [("own", own, [(0, 0, False)]), ("near", near, [(0, 1, False)])]
    early = list(range(1, late))
    for name, bits_list in (("early", early), ("late", [late])):
        if not bits_list:
            continue
        arrays = [direct(bits) for bits in bits_list]
        if len(arrays) > 1:
            arrays = [jnp.concatenate(arrays)]
        pieces.append((name, arrays[0], [(bits, 0, True) for bits in bits_list]))
        crossed = moved(arrays[0], lambda x, p, y, c: (1 - x, p, y, c))
        pieces.append((f"cross_{name}", crossed, [(bits, 1, True) for bits in bits_list]))
    found = [(array, tuple(place + (0,) for place in places)) for _, array, places in pieces]
    for name, array, places in pieces:
        swapped = moved(array, lambda x, p, y, c: (x, p, y, 1 - c))
        found.append((swapped, tuple(place + (1,) for place in places)))
    return found


def all_memory(parts):
    devices = lax.axis_size("frame")
    near = [parts[0]] + [hop(part, place) for place, part in enumerate(parts) if place]
    held = jnp.stack(near)
    for bit in range(2, devices.bit_length() - 1):
        half = held.shape[1] // 2
        arrived = hop(held[:, half:], 1 << bit)
        held = jnp.concatenate([held[:, :half], arrived])
    keys, values = held[:, 0, :, 0, :], held[:, 0, :, 1, :]
    return keys.reshape(-1, keys.shape[-1]), values.reshape(-1, values.shape[-1])


def hop(array, bits):
    return lax.ppermute(array, "frame", [(i, i ^ bits) for i in range(lax.axis_size("frame"))])


def all_tokens(latent):
    def to_home(array):
        return moved(array, lambda x, p, y, c: (x, p, y, 1 - c) if c != p % 2 else None)

    def from_home(array):
        return moved(array, lambda x, p, y, c: (x, p, y, 1 - c) if c == p % 2 else None)

    far = moved(latent, lambda x, p, y, c: (x, p ^ 1, y, c))
    near = moved(latent, lambda x, p, y, c: (x, p, 1 - y, c))
    far_near = moved(far, lambda x, p, y, c: (x, p, 1 - y, c))
    home = (latent, near, to_home(latent), to_home(near))
    return home + (far, far_near, from_home(far), from_home(far_near))


def late_plane(devices):
    return devices // 4 - 1


def piece_start(place, shard_rows, plane_number):
    x, _, _, y, c = here()
    _, y_bits, with_x, c_bits = place
    from_y, from_c = flipped(y, y_bits), flipped(c, c_bits)
    if with_x:
        from_y = joined_bits(joined_bits(from_y, x), from_c)
    return pl.multiple_of((plane_number * 4 + from_y * 2 + from_c) * shard_rows, 16)


def gather_pieces(piece_refs, places, first_plane, weights):
    for ref, shards in zip(piece_refs, places):
        rows = ref.shape[0] // len(shards)
        for number, place in enumerate(shards):
            start = piece_start(place, rows, place[0] - first_plane)
            weights[pl.ds(start, rows), :] = ref[number * rows : (number + 1) * rows, :]


def store_normed(current, rows, inverse, gain_ref, normed):
    _, _, plane, _, _ = here()
    planes = lax.axis_size("frame") // 4
    span = current.shape[1] // planes
    for bits in range(planes):
        spot = columns(flipped(plane, bits), span)
        widened = current[rows, spot].astype(jnp.float32)
        normed[rows, bits * span : (bits + 1) * span] = (widened * inverse * gain_ref[0:1, spot]).astype(normed.dtype)


BLOCK = 32


def prepare_kernel(extra_ref, *refs):
    token_refs, (extra, current, normed) = refs[:8], refs[8:]
    _, _, plane, y, c = here()
    rows = token_refs[0].shape[0]
    extra[...] = extra_ref[...]
    bases = [at_y * 2 * rows + core * rows for core in (0, 1) for at_y in (y, 1 - y)]

    def fill(refs):
        @pl.loop(0, rows // BLOCK)
        def _(number):
            for ref, base in zip(refs, bases):
                tokens = ref[pl.ds(pl.multiple_of(number * BLOCK, BLOCK), BLOCK), :]
                spot = pl.ds(pl.multiple_of(base + number * BLOCK, BLOCK), BLOCK)
                current[spot, :] = tokens
                widened = tokens.astype(jnp.float32)
                inverse = lax.rsqrt(jnp.mean(widened * widened, axis=-1, keepdims=True) + 1e-06)
                store_normed(current, spot, inverse, extra, normed)

    pl.when(plane % 2 == c)(lambda: fill(token_refs[:4]))
    pl.when(plane % 2 != c)(lambda: fill(token_refs[4:]))


def project_kernel(places, *refs):
    normed = refs[0]
    piece_refs = refs[1 : 1 + len(places)]
    out, weights = refs[1 + len(places) :]
    gather_pieces(piece_refs, places, 0, weights)
    out[...] = jnp.dot(normed[:, : weights.shape[0]], weights[...], preferred_element_type=jnp.float32)


def assemble_kernel(places, *refs):
    gather_pieces(refs[:-1], places, 0, refs[-1])


def attend_heads(projected, key_ref, value_ref, extra_ref, attended, head_count):
    width = projected.shape[1] // 3
    head_size = width // head_count
    scale_dot = 1.0 / math.sqrt(head_size)
    mem_rows = key_ref.shape[0]
    live = extra_ref[3:4, :mem_rows] > 0.5
    contract_last = (((1,), (1,)), ((), ()))
    frame_rows = projected.shape[0]
    half = frame_rows // 2
    for head in range(head_count):
        span = slice(head * head_size, (head + 1) * head_size)
        keys = projected[:, width + head * head_size : width + (head + 1) * head_size]
        values = projected[:, 2 * width + head * head_size : 2 * width + (head + 1) * head_size]
        for start in range(0, frame_rows, half):
            queries = projected[start : start + half, span]
            frame_scores = (
                lax.dot_general(queries, keys, contract_last, preferred_element_type=jnp.float32) * scale_dot
            )
            mem_scores = (
                lax.dot_general(queries, key_ref[:, span], contract_last, preferred_element_type=jnp.float32)
                * scale_dot
            )
            scores = jnp.concatenate([frame_scores, jnp.where(live, mem_scores, -1e30)], axis=1)
            weights = jnp.exp(scores - jnp.max(scores, axis=-1, keepdims=True))
            denominator = jnp.sum(weights, axis=-1, keepdims=True)
            rounded = weights.astype(jnp.bfloat16)
            blended = jnp.dot(
                rounded[:, :frame_rows], values, preferred_element_type=jnp.float32
            ) + jnp.dot(rounded[:, frame_rows:], value_ref[:, span], preferred_element_type=jnp.float32)
            attended[start : start + half, span] = (blended / denominator).astype(attended.dtype)


def step_kernel(places, first_plane, head_count, extra_ref, key_ref, value_ref, normed, part_ref, *refs):
    piece_refs = refs[: len(places)]
    attended, weights, projected = refs[len(places) :]
    gather_pieces(piece_refs, places, first_plane, weights)
    early = normed.shape[1] - weights.shape[0]
    projected[...] = (
        part_ref[...] + jnp.dot(normed[:, early:], weights[...], preferred_element_type=jnp.float32)
    ).astype(projected.dtype)
    attend_heads(projected, key_ref, value_ref, extra_ref, attended, head_count)


def last_step_kernel(
    update_places, head_count, extra_ref, key_ref, value_ref, current_ref, weights, first_part, second_part, third_part,
    fourth_part, keep, first, second, third, fourth, current, normed, projected, attended,
):
    _, _, plane, y, c = here()
    width = first_part.shape[1]
    at_home = plane % 2 == c

    @pl.loop(0, current.shape[0] // BLOCK)
    def _(number):
        rows = pl.ds(pl.multiple_of(number * BLOCK, BLOCK), BLOCK)
        total = jnp.zeros((BLOCK, 1), jnp.float32)
        for part, (plane_bits, y_bits) in zip((first_part, second_part, third_part, fourth_part), update_places):
            spot = columns(quarter_of(flipped(plane, plane_bits), flipped(y, y_bits)), width)
            updated = (
                current_ref[rows, spot].astype(jnp.float32)
                + extra_ref[1:2, :width] * part[rows, :].astype(jnp.float32)
            ).astype(current.dtype)
            current[rows, spot] = updated
            widened = updated.astype(jnp.float32)
            total = total + jnp.sum(widened * widened, axis=-1, keepdims=True)
        inverse = lax.rsqrt(total / current.shape[1] + 1e-06)
        store_normed(current, rows, inverse, extra_ref, normed)

    projected[...] = jnp.dot(normed[...], weights[...], preferred_element_type=jnp.float32).astype(projected.dtype)
    attend_heads(projected, key_ref, value_ref, extra_ref, attended, head_count)
    spot = columns(quarter_of(plane, y), width)
    attended[...] = (
        current[:, spot].astype(jnp.float32) + extra_ref[2:3, :width] * attended[...].astype(jnp.float32)
    ).astype(attended.dtype)
    chip_rows = attended.shape[0] // 2
    rows = chip_rows // 2
    here_rows, there_rows = y * chip_rows, (1 - y) * chip_rows

    def part(start):
        return attended[pl.ds(pl.multiple_of(start, rows), rows), :]

    keep[...] = part(here_rows)
    fourth[...] = part(there_rows + rows)

    @pl.when(at_home)
    def _():
        first[...] = part(there_rows)
        second[...] = part(there_rows + rows)
        third[...] = part(here_rows + rows)

    @pl.when(jnp.logical_not(at_home))
    def _():
        first[...] = part(here_rows + rows)
        second[...] = part(here_rows)
        third[...] = part(there_rows)


MIB = 1024 * 1024


def kernel_call(kernel, out_shape, operands, anywhere, scratch_shapes, limit, flops):
    vectors = pl.BlockSpec(memory_space=pltpu.VMEM)
    free = pl.BlockSpec(memory_space=pl.ANY)
    moved_bytes = sum(operand.size * operand.dtype.itemsize for operand in operands)
    return pl.pallas_call(
        kernel,
        out_shape=out_shape,
        in_specs=[free if number in anywhere else vectors for number in range(len(operands))],
        out_specs=jax.tree.map(lambda _: vectors, out_shape),
        scratch_shapes=scratch_shapes,
        compiler_params=pltpu.CompilerParams(vmem_limit_bytes=limit),
        cost_estimate=pl.CostEstimate(flops=flops, transcendentals=0, bytes_accessed=moved_bytes),
    )(*operands)


def prepare(extra, tokens):
    frame = jax.ShapeDtypeStruct((4 * tokens[0].shape[0], tokens[0].shape[1]), tokens[0].dtype)
    return kernel_call(
        prepare_kernel,
        (jax.ShapeDtypeStruct(extra.shape, extra.dtype), frame, frame),
        (extra, *tokens),
        (),
        [],
        8 * MIB,
        0,
    )


def project(normed, pieces):
    width = pieces[0][0].shape[1]
    depth = sum(array.shape[0] for array, _ in pieces)
    return kernel_call(
        functools.partial(project_kernel, tuple(place for _, place in pieces)),
        jax.ShapeDtypeStruct((normed.shape[0], width), jnp.float32),
        (normed, *[array for array, _ in pieces]),
        (),
        [pltpu.VMEM((depth, width), normed.dtype)],
        16 * MIB,
        2 * normed.shape[0] * depth * width,
    )


def assemble(pieces):
    width = pieces[0][0].shape[1]
    depth = sum(array.shape[0] for array, _ in pieces)
    return kernel_call(
        functools.partial(assemble_kernel, tuple(place for _, place in pieces)),
        jax.ShapeDtypeStruct((depth, width), pieces[0][0].dtype),
        [array for array, _ in pieces],
        (),
        [],
        8 * MIB,
        0,
    )


def step(extra, keys, values, normed, part, pieces):
    width = pieces[0][0].shape[1]
    depth = sum(array.shape[0] for array, _ in pieces)
    frame_rows = normed.shape[0]
    return kernel_call(
        functools.partial(step_kernel, tuple(place for _, place in pieces), pieces[0][1][0][0], HEADS // SPATIAL),
        jax.ShapeDtypeStruct((frame_rows, width // 3), normed.dtype),
        (extra, keys, values, normed, part, *[array for array, _ in pieces]),
        (),
        [pltpu.VMEM((depth, width), normed.dtype), pltpu.VMEM((frame_rows, width), normed.dtype)],
        16 * MIB,
        2 * frame_rows * width * (depth + frame_rows),
    )


def last_step(extra, keys, values, current, weights, updates):
    frame_rows, features = current.shape
    width = weights.shape[1] // 3
    share = jax.ShapeDtypeStruct((frame_rows // 4, width), current.dtype)
    return kernel_call(
        functools.partial(last_step_kernel, tuple(place for _, place in updates), HEADS // SPATIAL),
        (share,) * 5,
        (extra, keys, values, current, weights, *[array for array, _ in updates]),
        (),
        [
            pltpu.VMEM((frame_rows, features), current.dtype),
            pltpu.VMEM((frame_rows, features), current.dtype),
            pltpu.VMEM((frame_rows, 3 * width), current.dtype),
            pltpu.VMEM((frame_rows, width), current.dtype),
        ],
        16 * MIB,
        2 * frame_rows * 3 * width * (features + frame_rows),
    )


def join_kernel(keep, first, second, third, fourth, out):
    _, _, plane, y, c = here()
    low = plane % 2
    width = keep.shape[1]

    def put(ref, plane_low, at_y):
        out[:, columns(plane_low * 2 + at_y, width)] = ref[...]

    @pl.when(low == c)
    def _():
        put(keep, low, y)
        put(first, low, 1 - y)
        put(second, 1 - low, y)
        put(third, 1 - low, 1 - y)

    @pl.when(low != c)
    def _():
        put(first, 1 - low, y)
        put(second, low, 1 - y)
        put(third, low, y)
        put(fourth, 1 - low, 1 - y)


def joined(keep, first, second, third, fourth):
    def at_home(p, c):
        return c == p % 2

    first = moved(first, lambda x, p, y, c: (x, p, 1 - y, c) if at_home(p, c) else (x, p ^ 1, y, 1 - c))
    second = moved(second, lambda x, p, y, c: (x, p, 1 - y, 1 - c) if at_home(p, c) else (x, p ^ 1, y, c))
    third = moved(third, lambda x, p, y, c: (x, p, y, 1 - c) if at_home(p, c) else (x, p ^ 1, 1 - y, c))
    fourth = moved(fourth, lambda x, p, y, c: None if at_home(p, c) else (x, p ^ 1, 1 - y, 1 - c))
    rows, width = keep.shape
    return kernel_call(
        join_kernel,
        jax.ShapeDtypeStruct((rows, width * SPATIAL), keep.dtype),
        (keep, first, second, third, fourth),
        (),
        [],
        4 * MIB,
        0,
    )


def paired_planes(
    latent, norm_gain, w_query, w_key, w_value, mem_cache, intersection, counts, slot_of, step_scale
):
    late = late_plane(lax.axis_size("frame"))
    weights, extra, memory = pack(
        w_query, w_key, w_value, intersection, slot_of, counts, step_scale, norm_gain, mem_cache
    )
    pieces = all_pieces(*weights)
    tokens = all_tokens(latent)
    keys, values = all_memory(memory)
    extra, current, normed = prepare(extra, tokens)
    part = project(normed, [piece for piece in pieces if piece[1][0][0] < late])
    attended = step(extra, keys, values, normed, part, [piece for piece in pieces if piece[1][0][0] == late])
    updates = [
        (attended, (0, 0)),
        (moved(attended, lambda x, p, y, c: (x, p ^ 1, 1 - y, c)), (1, 1)),
        (moved(attended, lambda x, p, y, c: (x, p ^ 1, y, c)), (1, 0)),
        (moved(attended, lambda x, p, y, c: (x, p, 1 - y, c)), (0, 1)),
    ]
    shares = last_step(extra, keys, values, current, assemble(pieces), updates)
    return joined(*shares)


def fits_paired_planes(latent, norm_gain, w_query, w_key, w_value, mem_cache, *_):
    devices = lax.axis_size("frame")
    planes = devices // SPATIAL
    return (
        lax.axis_size("groups") == 2
        and devices == planes * SPATIAL
        and planes >= 2
        and planes & (planes - 1) == 0
        and w_query.shape[0] % 16 == 0
        and mem_cache.shape[1] == 1
    )


def from_partner(array, axis, bit):
    return lax.ppermute(array, axis, [(i, i ^ 1 << bit) for i in range(lax.axis_size(axis))])


def in_order(mine, theirs, upper, axis_dim):
    low_first = jnp.concatenate([mine, theirs], axis=axis_dim)
    high_first = jnp.concatenate([theirs, mine], axis=axis_dim)
    return jnp.where(upper, high_first, low_first)


def attend(queries, frame_pair, mem_keys, mem_values, live_keys, head_count):
    tok_rows, feature_width = queries.shape
    head_size = feature_width // head_count
    scale_dot = 1.0 / math.sqrt(head_size)
    q_heads = queries.reshape(tok_rows, head_count, head_size)
    k_heads = frame_pair[0].reshape(-1, head_count, head_size)
    v_heads = frame_pair[1].reshape(-1, head_count, head_size)
    frame_scores = (
        jnp.einsum("thd,khd->htk", q_heads, k_heads, preferred_element_type=jnp.float32) * scale_dot
    )
    remote_scores = (
        jnp.einsum("thd,khd->htk", q_heads, mem_keys, preferred_element_type=jnp.float32)
        * scale_dot
    )
    remote_scores = jnp.where(live_keys[None, None, :], remote_scores, -1e30)
    largest = jnp.maximum(
        jnp.max(frame_scores, axis=-1, keepdims=True),
        jnp.max(remote_scores, axis=-1, keepdims=True),
    )
    frame_weights = jnp.exp(frame_scores - largest)
    remote_weights = jnp.exp(remote_scores - largest)
    denominator = jnp.sum(frame_weights, axis=-1) + jnp.sum(remote_weights, axis=-1)
    blended = jnp.einsum(
        "htk,khd->thd",
        frame_weights.astype(jnp.bfloat16),
        v_heads,
        preferred_element_type=jnp.float32,
    )
    blended = blended + jnp.einsum(
        "htk,khd->thd",
        remote_weights.astype(jnp.bfloat16),
        mem_values,
        preferred_element_type=jnp.float32,
    )
    blended = blended / jnp.transpose(denominator)[:, :, None]
    return blended.reshape(tok_rows, feature_width).astype(jnp.bfloat16)


def rms_normed(current, norm_gain):
    widened = current.astype(jnp.float32)
    inverse = lax.rsqrt(jnp.mean(widened * widened, axis=-1, keepdims=True) + 1e-06)
    return (widened, (widened * inverse * norm_gain).astype(jnp.bfloat16))


def separate_frames(
    latent, norm_gain, w_query, w_key, w_value, mem_cache, intersection, counts, slot_of, step_scale
):
    devices = lax.axis_size("frame")
    position = lax.axis_index("frame")
    frame_index = position // SPATIAL
    doublings = SPATIAL.bit_length() - 1
    target_frame = jnp.arange(devices, dtype=jnp.int32) // SPATIAL
    current = latent
    feature_width = latent.shape[1]
    share_width = feature_width // SPATIAL
    head_share = HEADS // SPATIAL

    def column_pieces(weight):
        row_count = weight.shape[0]
        split_cols = jnp.transpose(weight.reshape(row_count, SPATIAL, share_width), (1, 0, 2))
        return jnp.tile(split_cols, (devices // SPATIAL, 1, 1))

    own_query, own_key, own_value = (
        lax.all_to_all(column_pieces(w_query), "frame", split_axis=0, concat_axis=1, tiled=True),
        lax.all_to_all(column_pieces(w_key), "frame", split_axis=0, concat_axis=1, tiled=True),
        lax.all_to_all(column_pieces(w_value), "frame", split_axis=0, concat_axis=1, tiled=True),
    )
    own_query, own_key, own_value = (own_query[0], own_key[0], own_value[0])
    listed = mem_cache[slot_of[intersection[target_frame]]]
    list_len = listed.shape[1]
    local_mem = listed.shape[2]
    grouped = listed.reshape(
        devices // SPATIAL, SPATIAL, list_len, local_mem, 2, SPATIAL, share_width
    )
    diagonal_part = jnp.diagonal(grouped, axis1=1, axis2=5)
    outgoing = jnp.moveaxis(diagonal_part, -1, 1).reshape(
        devices, list_len, local_mem, 2, share_width
    )
    fetched = lax.all_to_all(outgoing, "frame", split_axis=0, concat_axis=2, tiled=True)[0]
    mem_len = fetched.shape[1]
    mem_keys = fetched[:, :, 0, :].reshape(list_len * mem_len, head_share, HS)
    mem_values = fetched[:, :, 1, :].reshape(list_len * mem_len, head_share, HS)
    live_keys = jnp.arange(list_len * mem_len, dtype=jnp.int32) // mem_len < counts[frame_index]
    tok_rows = latent.shape[0]
    for step_index in range(STEPS):
        widened, normed = rms_normed(current, norm_gain)
        gathered = normed
        for bit_index in range(doublings):
            partner = from_partner(gathered, "frame", bit_index)
            gathered = in_order(gathered, partner, position >> bit_index & 1 == 1, 0)
        queries = jnp.dot(gathered, own_query, preferred_element_type=jnp.float32).astype(
            jnp.bfloat16
        )
        keys_frame = jnp.dot(gathered, own_key, preferred_element_type=jnp.float32).astype(
            jnp.bfloat16
        )
        values_frame = jnp.dot(gathered, own_value, preferred_element_type=jnp.float32).astype(
            jnp.bfloat16
        )
        frame_pair = jnp.stack([keys_frame, values_frame])
        attended = attend(queries, frame_pair, mem_keys, mem_values, live_keys, head_share)
        blocks = attended.reshape(SPATIAL, tok_rows, share_width)[:, None]
        for bit_index in range(doublings):
            upper = position >> bit_index & 1 == 1
            dest_count = blocks.shape[0]
            paired = blocks.reshape((dest_count // 2, 2) + blocks.shape[1:])
            kept = jnp.where(upper, paired[:, 1], paired[:, 0])
            sent = jnp.where(upper, paired[:, 0], paired[:, 1])
            arrived = from_partner(sent, "frame", bit_index)
            blocks = in_order(kept, arrived, upper, 1)
        joined = jnp.transpose(blocks[0], (1, 0, 2)).reshape(tok_rows, feature_width)
        current = (widened + step_scale[step_index] * joined.astype(jnp.float32)).astype(
            jnp.bfloat16
        )
    return current


def per_device(*arguments):
    return (paired_planes if fits_paired_planes(*arguments) else separate_frames)(*arguments)


def solution(mesh):
    placed = (
        P(("groups", "frame"), None),
        P(),
        P("frame", None),
        P("frame", None),
        P("frame", None),
        P("groups", "frame", None, None),
        P("groups", None),
        P("groups"),
        P("groups"),
        P(),
    )
    return jax.shard_map(
        per_device,
        mesh=mesh,
        in_specs=placed,
        out_specs=P(("groups", "frame"), None),
        check_vma=False,
    )
```

```python
import functools
import math

import jax
import jax.numpy as jnp
from jax import lax
from jax.experimental import pallas as pl
from jax.experimental.pallas import tpu as pltpu
from jax.sharding import PartitionSpec as P


HEADS = 12
HS = 128
SPATIAL = 4
STEPS = 2
AXES = ("groups", "frame")


def coords(index):
    return index // 4, (index // 2) % 2, index % 2


def quarter_of(plane, y):
    return (plane % 2) * 2 + y


def moved(array, target):
    devices = lax.axis_size("frame")
    pairs = []
    for x in range(lax.axis_size("groups")):
        for index in range(devices):
            place = target(x, *coords(index))
            if place is not None:
                to_x, to_plane, to_y, to_c = place
                pairs.append((x * devices + index, to_x * devices + to_plane * 4 + to_y * 2 + to_c))
    return lax.ppermute(array, AXES, pairs)


def here():
    x = lax.axis_index("groups")
    index = lax.axis_index("frame")
    plane = index // 4
    rest = index - plane * 4
    y = rest // 2
    return x, index, plane, y, rest - y * 2


def flipped(value, bits):
    out = value
    bit = 1
    while bit <= bits:
        if bits & bit:
            out = out + bit - 2 * bit * ((value // bit) % 2)
        bit *= 2
    return out


def joined_bits(one, other):
    return one + other - 2 * one * other


def columns(quarter, width):
    return pl.ds(pl.multiple_of(quarter * width, 128), width)


def pack_kernel(
    w_query, w_key, w_value, list_hbm, slot_hbm, count_hbm, scale_hbm, gain_hbm, mem_ref,
    own_ref, beside_ref, even_ref, odd_ref, extra_ref, *refs,
):
    near_count = SPATIAL
    memory_refs = refs[:near_count]
    (
        list_ref, slot_ref, count_ref, scale_ref, gain, rows, stored, extra, row_sem, out_sem, scalar_sem, mem_sem, give_sem,
    ) = refs[near_count:]
    x, index, plane, y, c = here()
    devices = lax.axis_size("frame")
    frames, entries = list_ref.shape
    width = own_ref.shape[1] // 3
    scalars = [
        pltpu.make_async_copy(source, target, scalar_sem.at[number])
        for number, (source, target) in enumerate(
            (
                (list_hbm, list_ref),
                (slot_hbm, slot_ref),
                (count_hbm, count_ref),
                (scale_hbm, scale_ref),
                (gain_hbm, gain),
            )
        )
    ]
    for copy in scalars[:2]:
        copy.start()
    reads = []
    for number, weight in enumerate((w_query, w_key, w_value)):
        reads.append(pltpu.make_async_copy(weight, rows.at[number], row_sem.at[number]))
        reads[-1].start()
    for copy in scalars[2:]:
        copy.start()
    for copy in scalars[:2]:
        copy.wait()
    picks = []
    for frame in range(frames):
        for entry in range(entries):
            number = frame * entries + entry
            row = slot_ref[list_ref[frame, entry]]
            picks.append(pltpu.make_async_copy(mem_ref.at[row, 0], stored.at[number], mem_sem.at[number]))
            picks[-1].start()
    across = joined_bits(joined_bits(x, y), c)
    low = plane % 2
    quarters = (low * 2 + across, (1 - low) * 2 + across, low * 2 + 1 - y, quarter_of(plane, y))
    gives = []
    for number, read in enumerate(reads):
        read.wait()
        for place, (quarter, out) in enumerate(zip(quarters, (even_ref, odd_ref, beside_ref, own_ref))):
            gives.append(
                pltpu.make_async_copy(
                    rows.at[number, :, columns(quarter, width)],
                    out.at[:, pl.ds(number * width, width)],
                    out_sem.at[number, place],
                )
            )
            gives[-1].start()
    for copy in scalars[2:]:
        copy.wait()
    row = (1, extra.shape[1])
    extra[0:1, :] = gain[...].reshape(row)
    for number in range(STEPS):
        extra[1 + number : 2 + number, :] = jnp.full(row, scale_ref[number], jnp.float32)
    live = lax.broadcasted_iota(jnp.int32, row, 1) % entries < count_ref[(plane // 2) * 2 + c]
    extra[1 + STEPS : 2 + STEPS, :] = jnp.where(live, 1.0, 0.0)
    gives.append(pltpu.make_async_copy(extra, extra_ref, scalar_sem.at[5]))
    gives[-1].start()
    for pick in picks:
        pick.wait()
    bits = devices.bit_length() - 1
    for away in range(devices):
        to_plane, to_y, to_c = coords(flipped(index, away))
        to_frame = (to_plane // 2) * 2 + to_c
        place = 0
        for bit in range(2, bits):
            place = place * 2 + (away >> bit & 1)
        gives.append(
            pltpu.make_async_copy(
                stored.at[pl.ds(to_frame * entries, entries), :, columns(quarter_of(to_plane, to_y), width)],
                memory_refs[away % SPATIAL].at[place],
                give_sem.at[away],
            )
        )
        gives[-1].start()
    for give in gives:
        give.wait()


def pack(w_query, w_key, w_value, intersection, slot_of, counts, step_scale, norm_gain, mem_cache):
    devices = lax.axis_size("frame")
    shard_rows, features = w_query.shape
    frames, entries = intersection.shape
    piece = jax.ShapeDtypeStruct((shard_rows, 3 * (features // SPATIAL)), w_query.dtype)
    small = jax.ShapeDtypeStruct((2 + STEPS, features), jnp.float32)
    memory = jax.ShapeDtypeStruct((devices // SPATIAL, entries, 2, features // SPATIAL), mem_cache.dtype)
    out_shape = (piece,) * 4 + (small,) + (memory,) * SPATIAL
    anywhere = pl.BlockSpec(memory_space=pl.ANY)
    held = pl.BlockSpec(memory_space=pltpu.HBM)
    outs = pl.pallas_call(
        pack_kernel,
        out_shape=out_shape,
        in_specs=[held] * 9,
        out_specs=(anywhere,) * len(out_shape),
        scratch_shapes=[
            pltpu.SMEM(intersection.shape, intersection.dtype),
            pltpu.SMEM(slot_of.shape, slot_of.dtype),
            pltpu.SMEM(counts.shape, counts.dtype),
            pltpu.SMEM(step_scale.shape, step_scale.dtype),
            pltpu.VMEM(norm_gain.shape, norm_gain.dtype),
            pltpu.VMEM((3, shard_rows, features), w_query.dtype),
            pltpu.VMEM((frames * entries, 2, features), mem_cache.dtype),
            pltpu.VMEM(small.shape, small.dtype),
            pltpu.SemaphoreType.DMA((3,)),
            pltpu.SemaphoreType.DMA((3, 4)),
            pltpu.SemaphoreType.DMA((6,)),
            pltpu.SemaphoreType.DMA((frames * entries,)),
            pltpu.SemaphoreType.DMA((devices,)),
        ],
        name="pack",
    )(w_query, w_key, w_value, intersection, slot_of, counts, step_scale, norm_gain, mem_cache)
    return outs[:4], outs[4], outs[5:]


def all_pieces(own, beside, even, odd):
    late = late_plane(lax.axis_size("frame"))

    def direct(bits):
        sent = even if bits % 2 == 0 else odd
        return moved(sent, lambda x, p, y, c: (x, p ^ bits, y ^ x ^ c, c))

    near = moved(beside, lambda x, p, y, c: (x, p, 1 - y, c))
    pieces = [("own", own, [(0, 0, False)]), ("near", near, [(0, 1, False)])]
    early = list(range(1, late))
    for name, bits_list in (("early", early), ("late", [late])):
        if not bits_list:
            continue
        arrays = [direct(bits) for bits in bits_list]
        if len(arrays) > 1:
            arrays = [jnp.concatenate(arrays)]
        pieces.append((name, arrays[0], [(bits, 0, True) for bits in bits_list]))
        crossed = moved(arrays[0], lambda x, p, y, c: (1 - x, p, y, c))
        pieces.append((f"cross_{name}", crossed, [(bits, 1, True) for bits in bits_list]))
    found = [(array, tuple(place + (0,) for place in places)) for _, array, places in pieces]
    for name, array, places in pieces:
        swapped = moved(array, lambda x, p, y, c: (x, p, y, 1 - c))
        found.append((swapped, tuple(place + (1,) for place in places)))
    return found


def all_memory(parts):
    devices = lax.axis_size("frame")
    near = [parts[0]] + [hop(part, place) for place, part in enumerate(parts) if place]
    held = jnp.stack(near)
    for bit in range(2, devices.bit_length() - 1):
        half = held.shape[1] // 2
        arrived = hop(held[:, half:], 1 << bit)
        held = jnp.concatenate([held[:, :half], arrived])
    keys, values = held[:, 0, :, 0, :], held[:, 0, :, 1, :]
    return keys.reshape(-1, keys.shape[-1]), values.reshape(-1, values.shape[-1])


def hop(array, bits):
    return lax.ppermute(array, "frame", [(i, i ^ bits) for i in range(lax.axis_size("frame"))])


def all_tokens(latent):
    def swapped(array):
        return moved(array, lambda x, p, y, c: (x, p, y, 1 - c))

    far = moved(latent, lambda x, p, y, c: (x, p ^ 1, y, c))
    near = moved(latent, lambda x, p, y, c: (x, p, 1 - y, c))
    far_near = moved(far, lambda x, p, y, c: (x, p, 1 - y, c))
    home = (latent, near, swapped(latent), swapped(near))
    return home + (far, far_near, swapped(far), swapped(far_near))


def late_plane(devices):
    return devices // 4 - 1


def piece_start(place, shard_rows, plane_number):
    x, _, _, y, c = here()
    _, y_bits, with_x, c_bits = place
    from_y, from_c = flipped(y, y_bits), flipped(c, c_bits)
    if with_x:
        from_y = joined_bits(joined_bits(from_y, x), from_c)
    return pl.multiple_of((plane_number * 4 + from_y * 2 + from_c) * shard_rows, 16)


def gather_pieces(piece_refs, places, first_plane, weights):
    for ref, shards in zip(piece_refs, places):
        rows = ref.shape[0] // len(shards)
        for number, place in enumerate(shards):
            start = piece_start(place, rows, place[0] - first_plane)
            weights[pl.ds(start, rows), :] = ref[number * rows : (number + 1) * rows, :]


def store_normed(current, rows, inverse, gain_ref, normed):
    _, _, plane, _, _ = here()
    planes = lax.axis_size("frame") // 4
    span = current.shape[1] // planes
    for bits in range(planes):
        spot = columns(flipped(plane, bits), span)
        widened = current[rows, spot].astype(jnp.float32)
        normed[rows, bits * span : (bits + 1) * span] = (widened * inverse * gain_ref[0:1, spot]).astype(normed.dtype)


BLOCK = 32


def prepare_kernel(extra_ref, *refs):
    token_refs, (extra, current, normed) = refs[:8], refs[8:]
    _, _, plane, y, c = here()
    rows = token_refs[0].shape[0]
    extra[...] = extra_ref[...]
    bases = [at_y * 2 * rows + core * rows for core in (0, 1) for at_y in (y, 1 - y)]

    def fill(refs):
        @pl.loop(0, rows // BLOCK)
        def _(number):
            for ref, base in zip(refs, bases):
                tokens = ref[pl.ds(pl.multiple_of(number * BLOCK, BLOCK), BLOCK), :]
                spot = pl.ds(pl.multiple_of(base + number * BLOCK, BLOCK), BLOCK)
                current[spot, :] = tokens
                widened = tokens.astype(jnp.float32)
                inverse = lax.rsqrt(jnp.mean(widened * widened, axis=-1, keepdims=True) + 1e-06)
                store_normed(current, spot, inverse, extra, normed)

    pl.when(plane % 2 == c)(lambda: fill(token_refs[:4]))
    pl.when(plane % 2 != c)(lambda: fill(token_refs[4:]))


def project_kernel(places, *refs):
    normed = refs[0]
    piece_refs = refs[1 : 1 + len(places)]
    out, weights = refs[1 + len(places) :]
    gather_pieces(piece_refs, places, 0, weights)
    out[...] = jnp.dot(normed[:, : weights.shape[0]], weights[...], preferred_element_type=jnp.float32)


def assemble_kernel(places, *refs):
    gather_pieces(refs[:-1], places, 0, refs[-1])


def attend_heads(projected, key_ref, value_ref, extra_ref, attended, head_count):
    width = projected.shape[1] // 3
    head_size = width // head_count
    scale_dot = 1.0 / math.sqrt(head_size)
    mem_rows = key_ref.shape[0]
    live = extra_ref[3:4, :mem_rows] > 0.5
    contract_last = (((1,), (1,)), ((), ()))
    frame_rows = projected.shape[0]
    half = frame_rows // 2
    for head in range(head_count):
        span = slice(head * head_size, (head + 1) * head_size)
        keys = projected[:, width + head * head_size : width + (head + 1) * head_size]
        values = projected[:, 2 * width + head * head_size : 2 * width + (head + 1) * head_size]
        for start in range(0, frame_rows, half):
            queries = projected[start : start + half, span]
            frame_scores = (
                lax.dot_general(queries, keys, contract_last, preferred_element_type=jnp.float32) * scale_dot
            )
            mem_scores = (
                lax.dot_general(queries, key_ref[:, span], contract_last, preferred_element_type=jnp.float32)
                * scale_dot
            )
            scores = jnp.concatenate([frame_scores, jnp.where(live, mem_scores, -1e30)], axis=1)
            weights = jnp.exp(scores - jnp.max(scores, axis=-1, keepdims=True))
            denominator = jnp.sum(weights, axis=-1, keepdims=True)
            rounded = weights.astype(jnp.bfloat16)
            blended = jnp.dot(
                rounded[:, :frame_rows], values, preferred_element_type=jnp.float32
            ) + jnp.dot(rounded[:, frame_rows:], value_ref[:, span], preferred_element_type=jnp.float32)
            attended[start : start + half, span] = (blended / denominator).astype(attended.dtype)


def step_kernel(places, first_plane, head_count, extra_ref, key_ref, value_ref, normed, part_ref, *refs):
    piece_refs = refs[: len(places)]
    attended, weights, projected = refs[len(places) :]
    gather_pieces(piece_refs, places, first_plane, weights)
    early = normed.shape[1] - weights.shape[0]
    projected[...] = (
        part_ref[...] + jnp.dot(normed[:, early:], weights[...], preferred_element_type=jnp.float32)
    ).astype(projected.dtype)
    attend_heads(projected, key_ref, value_ref, extra_ref, attended, head_count)


def last_step_kernel(
    update_places, head_count, extra_ref, key_ref, value_ref, current_ref, weights, first_part, second_part, third_part,
    fourth_part, keep, first, second, third, fourth, current, normed, projected, attended,
):
    _, _, plane, y, c = here()
    width = first_part.shape[1]
    at_home = plane % 2 == c

    @pl.loop(0, current.shape[0] // BLOCK)
    def _(number):
        rows = pl.ds(pl.multiple_of(number * BLOCK, BLOCK), BLOCK)
        total = jnp.zeros((BLOCK, 1), jnp.float32)
        for part, (plane_bits, y_bits) in zip((first_part, second_part, third_part, fourth_part), update_places):
            spot = columns(quarter_of(flipped(plane, plane_bits), flipped(y, y_bits)), width)
            updated = (
                current_ref[rows, spot].astype(jnp.float32)
                + extra_ref[1:2, :width] * part[rows, :].astype(jnp.float32)
            ).astype(current.dtype)
            current[rows, spot] = updated
            widened = updated.astype(jnp.float32)
            total = total + jnp.sum(widened * widened, axis=-1, keepdims=True)
        inverse = lax.rsqrt(total / current.shape[1] + 1e-06)
        store_normed(current, rows, inverse, extra_ref, normed)

    projected[...] = jnp.dot(normed[...], weights[...], preferred_element_type=jnp.float32).astype(projected.dtype)
    attend_heads(projected, key_ref, value_ref, extra_ref, attended, head_count)
    spot = columns(quarter_of(plane, y), width)
    attended[...] = (
        current[:, spot].astype(jnp.float32) + extra_ref[2:3, :width] * attended[...].astype(jnp.float32)
    ).astype(attended.dtype)
    chip_rows = attended.shape[0] // 2
    rows = chip_rows // 2
    here_rows, there_rows = y * chip_rows, (1 - y) * chip_rows

    def part(start):
        return attended[pl.ds(pl.multiple_of(start, rows), rows), :]

    keep[...] = part(here_rows)
    fourth[...] = part(there_rows + rows)

    @pl.when(at_home)
    def _():
        first[...] = part(there_rows)
        second[...] = part(there_rows + rows)
        third[...] = part(here_rows + rows)

    @pl.when(jnp.logical_not(at_home))
    def _():
        first[...] = part(here_rows + rows)
        second[...] = part(here_rows)
        third[...] = part(there_rows)


MIB = 1024 * 1024


def kernel_call(kernel, out_shape, operands, anywhere, scratch_shapes, limit, flops):
    vectors = pl.BlockSpec(memory_space=pltpu.VMEM)
    free = pl.BlockSpec(memory_space=pl.ANY)
    moved_bytes = sum(operand.size * operand.dtype.itemsize for operand in operands)
    return pl.pallas_call(
        kernel,
        out_shape=out_shape,
        in_specs=[free if number in anywhere else vectors for number in range(len(operands))],
        out_specs=jax.tree.map(lambda _: vectors, out_shape),
        scratch_shapes=scratch_shapes,
        compiler_params=pltpu.CompilerParams(vmem_limit_bytes=limit),
        cost_estimate=pl.CostEstimate(flops=flops, transcendentals=0, bytes_accessed=moved_bytes),
    )(*operands)


def prepare(extra, tokens):
    frame = jax.ShapeDtypeStruct((4 * tokens[0].shape[0], tokens[0].shape[1]), tokens[0].dtype)
    return kernel_call(
        prepare_kernel,
        (jax.ShapeDtypeStruct(extra.shape, extra.dtype), frame, frame),
        (extra, *tokens),
        (),
        [],
        8 * MIB,
        0,
    )


def project(normed, pieces):
    width = pieces[0][0].shape[1]
    depth = sum(array.shape[0] for array, _ in pieces)
    return kernel_call(
        functools.partial(project_kernel, tuple(place for _, place in pieces)),
        jax.ShapeDtypeStruct((normed.shape[0], width), jnp.float32),
        (normed, *[array for array, _ in pieces]),
        (),
        [pltpu.VMEM((depth, width), normed.dtype)],
        16 * MIB,
        2 * normed.shape[0] * depth * width,
    )


def assemble(pieces):
    width = pieces[0][0].shape[1]
    depth = sum(array.shape[0] for array, _ in pieces)
    return kernel_call(
        functools.partial(assemble_kernel, tuple(place for _, place in pieces)),
        jax.ShapeDtypeStruct((depth, width), pieces[0][0].dtype),
        [array for array, _ in pieces],
        (),
        [],
        8 * MIB,
        0,
    )


def step(extra, keys, values, normed, part, pieces):
    width = pieces[0][0].shape[1]
    depth = sum(array.shape[0] for array, _ in pieces)
    frame_rows = normed.shape[0]
    return kernel_call(
        functools.partial(step_kernel, tuple(place for _, place in pieces), pieces[0][1][0][0], HEADS // SPATIAL),
        jax.ShapeDtypeStruct((frame_rows, width // 3), normed.dtype),
        (extra, keys, values, normed, part, *[array for array, _ in pieces]),
        (),
        [pltpu.VMEM((depth, width), normed.dtype), pltpu.VMEM((frame_rows, width), normed.dtype)],
        16 * MIB,
        2 * frame_rows * width * (depth + frame_rows),
    )


def last_step(extra, keys, values, current, weights, updates):
    frame_rows, features = current.shape
    width = weights.shape[1] // 3
    share = jax.ShapeDtypeStruct((frame_rows // 4, width), current.dtype)
    return kernel_call(
        functools.partial(last_step_kernel, tuple(place for _, place in updates), HEADS // SPATIAL),
        (share,) * 5,
        (extra, keys, values, current, weights, *[array for array, _ in updates]),
        (),
        [
            pltpu.VMEM((frame_rows, features), current.dtype),
            pltpu.VMEM((frame_rows, features), current.dtype),
            pltpu.VMEM((frame_rows, 3 * width), current.dtype),
            pltpu.VMEM((frame_rows, width), current.dtype),
        ],
        16 * MIB,
        2 * frame_rows * 3 * width * (features + frame_rows),
    )


def join_kernel(keep, first, second, third, fourth, out):
    _, _, plane, y, c = here()
    low = plane % 2
    width = keep.shape[1]

    def put(ref, plane_low, at_y):
        out[:, columns(plane_low * 2 + at_y, width)] = ref[...]

    @pl.when(low == c)
    def _():
        put(keep, low, y)
        put(first, low, 1 - y)
        put(second, 1 - low, y)
        put(third, 1 - low, 1 - y)

    @pl.when(low != c)
    def _():
        put(first, 1 - low, y)
        put(second, low, 1 - y)
        put(third, low, y)
        put(fourth, 1 - low, 1 - y)


def joined(keep, first, second, third, fourth):
    def at_home(p, c):
        return c == p % 2

    first = moved(first, lambda x, p, y, c: (x, p, 1 - y, c) if at_home(p, c) else (x, p ^ 1, y, 1 - c))
    second = moved(second, lambda x, p, y, c: (x, p, 1 - y, 1 - c) if at_home(p, c) else (x, p ^ 1, y, c))
    third = moved(third, lambda x, p, y, c: (x, p, y, 1 - c) if at_home(p, c) else (x, p ^ 1, 1 - y, c))
    fourth = moved(fourth, lambda x, p, y, c: None if at_home(p, c) else (x, p ^ 1, 1 - y, 1 - c))
    rows, width = keep.shape
    return kernel_call(
        join_kernel,
        jax.ShapeDtypeStruct((rows, width * SPATIAL), keep.dtype),
        (keep, first, second, third, fourth),
        (),
        [],
        4 * MIB,
        0,
    )


def paired_planes(
    latent, norm_gain, w_query, w_key, w_value, mem_cache, intersection, counts, slot_of, step_scale
):
    late = late_plane(lax.axis_size("frame"))
    weights, extra, memory = pack(
        w_query, w_key, w_value, intersection, slot_of, counts, step_scale, norm_gain, mem_cache
    )
    pieces = all_pieces(*weights)
    tokens = all_tokens(latent)
    keys, values = all_memory(memory)
    extra, current, normed = prepare(extra, tokens)
    part = project(normed, [piece for piece in pieces if piece[1][0][0] < late])
    attended = step(extra, keys, values, normed, part, [piece for piece in pieces if piece[1][0][0] == late])
    updates = [
        (attended, (0, 0)),
        (moved(attended, lambda x, p, y, c: (x, p ^ 1, 1 - y, c)), (1, 1)),
        (moved(attended, lambda x, p, y, c: (x, p ^ 1, y, c)), (1, 0)),
        (moved(attended, lambda x, p, y, c: (x, p, 1 - y, c)), (0, 1)),
    ]
    shares = last_step(extra, keys, values, current, assemble(pieces), updates)
    return joined(*shares)


def fits_paired_planes(latent, norm_gain, w_query, w_key, w_value, mem_cache, *_):
    devices = lax.axis_size("frame")
    planes = devices // SPATIAL
    return (
        lax.axis_size("groups") == 2
        and devices == planes * SPATIAL
        and planes >= 2
        and planes & (planes - 1) == 0
        and w_query.shape[0] % 16 == 0
        and mem_cache.shape[1] == 1
    )


def from_partner(array, axis, bit):
    return lax.ppermute(array, axis, [(i, i ^ 1 << bit) for i in range(lax.axis_size(axis))])


def in_order(mine, theirs, upper, axis_dim):
    low_first = jnp.concatenate([mine, theirs], axis=axis_dim)
    high_first = jnp.concatenate([theirs, mine], axis=axis_dim)
    return jnp.where(upper, high_first, low_first)


def attend(queries, frame_pair, mem_keys, mem_values, live_keys, head_count):
    tok_rows, feature_width = queries.shape
    head_size = feature_width // head_count
    scale_dot = 1.0 / math.sqrt(head_size)
    q_heads = queries.reshape(tok_rows, head_count, head_size)
    k_heads = frame_pair[0].reshape(-1, head_count, head_size)
    v_heads = frame_pair[1].reshape(-1, head_count, head_size)
    frame_scores = (
        jnp.einsum("thd,khd->htk", q_heads, k_heads, preferred_element_type=jnp.float32) * scale_dot
    )
    remote_scores = (
        jnp.einsum("thd,khd->htk", q_heads, mem_keys, preferred_element_type=jnp.float32)
        * scale_dot
    )
    remote_scores = jnp.where(live_keys[None, None, :], remote_scores, -1e30)
    largest = jnp.maximum(
        jnp.max(frame_scores, axis=-1, keepdims=True),
        jnp.max(remote_scores, axis=-1, keepdims=True),
    )
    frame_weights = jnp.exp(frame_scores - largest)
    remote_weights = jnp.exp(remote_scores - largest)
    denominator = jnp.sum(frame_weights, axis=-1) + jnp.sum(remote_weights, axis=-1)
    blended = jnp.einsum(
        "htk,khd->thd",
        frame_weights.astype(jnp.bfloat16),
        v_heads,
        preferred_element_type=jnp.float32,
    )
    blended = blended + jnp.einsum(
        "htk,khd->thd",
        remote_weights.astype(jnp.bfloat16),
        mem_values,
        preferred_element_type=jnp.float32,
    )
    blended = blended / jnp.transpose(denominator)[:, :, None]
    return blended.reshape(tok_rows, feature_width).astype(jnp.bfloat16)


def rms_normed(current, norm_gain):
    widened = current.astype(jnp.float32)
    inverse = lax.rsqrt(jnp.mean(widened * widened, axis=-1, keepdims=True) + 1e-06)
    return (widened, (widened * inverse * norm_gain).astype(jnp.bfloat16))


def separate_frames(
    latent, norm_gain, w_query, w_key, w_value, mem_cache, intersection, counts, slot_of, step_scale
):
    devices = lax.axis_size("frame")
    position = lax.axis_index("frame")
    frame_index = position // SPATIAL
    doublings = SPATIAL.bit_length() - 1
    target_frame = jnp.arange(devices, dtype=jnp.int32) // SPATIAL
    current = latent
    feature_width = latent.shape[1]
    share_width = feature_width // SPATIAL
    head_share = HEADS // SPATIAL

    def column_pieces(weight):
        row_count = weight.shape[0]
        split_cols = jnp.transpose(weight.reshape(row_count, SPATIAL, share_width), (1, 0, 2))
        return jnp.tile(split_cols, (devices // SPATIAL, 1, 1))

    own_query, own_key, own_value = (
        lax.all_to_all(column_pieces(w_query), "frame", split_axis=0, concat_axis=1, tiled=True),
        lax.all_to_all(column_pieces(w_key), "frame", split_axis=0, concat_axis=1, tiled=True),
        lax.all_to_all(column_pieces(w_value), "frame", split_axis=0, concat_axis=1, tiled=True),
    )
    own_query, own_key, own_value = (own_query[0], own_key[0], own_value[0])
    listed = mem_cache[slot_of[intersection[target_frame]]]
    list_len = listed.shape[1]
    local_mem = listed.shape[2]
    grouped = listed.reshape(
        devices // SPATIAL, SPATIAL, list_len, local_mem, 2, SPATIAL, share_width
    )
    diagonal_part = jnp.diagonal(grouped, axis1=1, axis2=5)
    outgoing = jnp.moveaxis(diagonal_part, -1, 1).reshape(
        devices, list_len, local_mem, 2, share_width
    )
    fetched = lax.all_to_all(outgoing, "frame", split_axis=0, concat_axis=2, tiled=True)[0]
    mem_len = fetched.shape[1]
    mem_keys = fetched[:, :, 0, :].reshape(list_len * mem_len, head_share, HS)
    mem_values = fetched[:, :, 1, :].reshape(list_len * mem_len, head_share, HS)
    live_keys = jnp.arange(list_len * mem_len, dtype=jnp.int32) // mem_len < counts[frame_index]
    tok_rows = latent.shape[0]
    for step_index in range(STEPS):
        widened, normed = rms_normed(current, norm_gain)
        gathered = normed
        for bit_index in range(doublings):
            partner = from_partner(gathered, "frame", bit_index)
            gathered = in_order(gathered, partner, position >> bit_index & 1 == 1, 0)
        queries = jnp.dot(gathered, own_query, preferred_element_type=jnp.float32).astype(
            jnp.bfloat16
        )
        keys_frame = jnp.dot(gathered, own_key, preferred_element_type=jnp.float32).astype(
            jnp.bfloat16
        )
        values_frame = jnp.dot(gathered, own_value, preferred_element_type=jnp.float32).astype(
            jnp.bfloat16
        )
        frame_pair = jnp.stack([keys_frame, values_frame])
        attended = attend(queries, frame_pair, mem_keys, mem_values, live_keys, head_share)
        blocks = attended.reshape(SPATIAL, tok_rows, share_width)[:, None]
        for bit_index in range(doublings):
            upper = position >> bit_index & 1 == 1
            dest_count = blocks.shape[0]
            paired = blocks.reshape((dest_count // 2, 2) + blocks.shape[1:])
            kept = jnp.where(upper, paired[:, 1], paired[:, 0])
            sent = jnp.where(upper, paired[:, 0], paired[:, 1])
            arrived = from_partner(sent, "frame", bit_index)
            blocks = in_order(kept, arrived, upper, 1)
        joined = jnp.transpose(blocks[0], (1, 0, 2)).reshape(tok_rows, feature_width)
        current = (widened + step_scale[step_index] * joined.astype(jnp.float32)).astype(
            jnp.bfloat16
        )
    return current


def per_device(*arguments):
    return (paired_planes if fits_paired_planes(*arguments) else separate_frames)(*arguments)


def solution(mesh):
    placed = (
        P(("groups", "frame"), None),
        P(),
        P("frame", None),
        P("frame", None),
        P("frame", None),
        P("groups", "frame", None, None),
        P("groups", None),
        P("groups"),
        P("groups"),
        P(),
    )
    return jax.shard_map(
        per_device,
        mesh=mesh,
        in_specs=placed,
        out_specs=P(("groups", "frame"), None),
        check_vma=False,
    )
```

```python
import functools
import math

import jax
import jax.numpy as jnp
from jax import lax
from jax.experimental import pallas as pl
from jax.experimental.pallas import tpu as pltpu
from jax.sharding import PartitionSpec as P


HEADS = 12
HS = 128
SPATIAL = 4
STEPS = 2
AXES = ("groups", "frame")


def coords(index):
    return index // 4, (index // 2) % 2, index % 2


def quarter_of(plane, y):
    return (plane % 2) * 2 + y


def moved(array, target):
    devices = lax.axis_size("frame")
    pairs = []
    for x in range(lax.axis_size("groups")):
        for index in range(devices):
            place = target(x, *coords(index))
            if place is not None:
                to_x, to_plane, to_y, to_c = place
                pairs.append((x * devices + index, to_x * devices + to_plane * 4 + to_y * 2 + to_c))
    return lax.ppermute(array, AXES, pairs)


def here():
    x = lax.axis_index("groups")
    index = lax.axis_index("frame")
    plane = index // 4
    rest = index - plane * 4
    y = rest // 2
    return x, index, plane, y, rest - y * 2


def flipped(value, bits):
    out = value
    bit = 1
    while bit <= bits:
        if bits & bit:
            out = out + bit - 2 * bit * ((value // bit) % 2)
        bit *= 2
    return out


def joined_bits(one, other):
    return one + other - 2 * one * other


def columns(quarter, width):
    return pl.ds(pl.multiple_of(quarter * width, 128), width)


def pack_kernel(
    w_query, w_key, w_value, list_hbm, slot_hbm, count_hbm, scale_hbm, gain_hbm, mem_ref,
    own_ref, beside_ref, even_ref, odd_ref, extra_ref, *refs,
):
    near_count = SPATIAL
    memory_refs = refs[:near_count]
    (
        list_ref, slot_ref, count_ref, scale_ref, gain, rows, stored, extra, row_sem, out_sem, scalar_sem, mem_sem, give_sem,
    ) = refs[near_count:]
    x, index, plane, y, c = here()
    devices = lax.axis_size("frame")
    frames, entries = list_ref.shape
    width = own_ref.shape[1] // 3
    scalars = [
        pltpu.make_async_copy(source, target, scalar_sem.at[number])
        for number, (source, target) in enumerate(
            (
                (list_hbm, list_ref),
                (slot_hbm, slot_ref),
                (count_hbm, count_ref),
                (scale_hbm, scale_ref),
                (gain_hbm, gain),
            )
        )
    ]
    for copy in scalars[:2]:
        copy.start()
    reads = []
    for number, weight in enumerate((w_query, w_key, w_value)):
        reads.append(pltpu.make_async_copy(weight, rows.at[number], row_sem.at[number]))
        reads[-1].start()
    for copy in scalars[2:]:
        copy.start()
    for copy in scalars[:2]:
        copy.wait()
    picks = []
    for frame in range(frames):
        for entry in range(entries):
            number = frame * entries + entry
            row = slot_ref[list_ref[frame, entry]]
            picks.append(pltpu.make_async_copy(mem_ref.at[row, 0], stored.at[number], mem_sem.at[number]))
            picks[-1].start()
    across = joined_bits(joined_bits(x, y), c)
    low = plane % 2
    quarters = (low * 2 + across, (1 - low) * 2 + across, low * 2 + 1 - y, quarter_of(plane, y))
    gives = []
    for number, read in enumerate(reads):
        read.wait()
        for place, (quarter, out) in enumerate(zip(quarters, (even_ref, odd_ref, beside_ref, own_ref))):
            gives.append(
                pltpu.make_async_copy(
                    rows.at[number, :, columns(quarter, width)],
                    out.at[:, pl.ds(number * width, width)],
                    out_sem.at[number, place],
                )
            )
            gives[-1].start()
    for copy in scalars[2:]:
        copy.wait()
    row = (1, extra.shape[1])
    extra[0:1, :] = gain[...].reshape(row)
    for number in range(STEPS):
        extra[1 + number : 2 + number, :] = jnp.full(row, scale_ref[number], jnp.float32)
    live = lax.broadcasted_iota(jnp.int32, row, 1) % entries < count_ref[(plane // 2) * 2 + 1 - c]
    extra[1 + STEPS : 2 + STEPS, :] = jnp.where(live, 1.0, 0.0)
    gives.append(pltpu.make_async_copy(extra, extra_ref, scalar_sem.at[5]))
    gives[-1].start()
    for pick in picks:
        pick.wait()
    bits = devices.bit_length() - 1
    for away in range(devices):
        to_plane, to_y, to_c = coords(flipped(index, away))
        to_frame = (to_plane // 2) * 2 + to_c
        place = 0
        for bit in range(2, bits):
            place = place * 2 + (away >> bit & 1)
        gives.append(
            pltpu.make_async_copy(
                stored.at[pl.ds(to_frame * entries, entries), :, columns(quarter_of(to_plane, to_y), width)],
                memory_refs[away % SPATIAL].at[place],
                give_sem.at[away],
            )
        )
        gives[-1].start()
    for give in gives:
        give.wait()


def pack(w_query, w_key, w_value, intersection, slot_of, counts, step_scale, norm_gain, mem_cache):
    devices = lax.axis_size("frame")
    shard_rows, features = w_query.shape
    frames, entries = intersection.shape
    piece = jax.ShapeDtypeStruct((shard_rows, 3 * (features // SPATIAL)), w_query.dtype)
    small = jax.ShapeDtypeStruct((2 + STEPS, features), jnp.float32)
    memory = jax.ShapeDtypeStruct((devices // SPATIAL, entries, 2, features // SPATIAL), mem_cache.dtype)
    out_shape = (piece,) * 4 + (small,) + (memory,) * SPATIAL
    anywhere = pl.BlockSpec(memory_space=pl.ANY)
    held = pl.BlockSpec(memory_space=pltpu.HBM)
    outs = pl.pallas_call(
        pack_kernel,
        out_shape=out_shape,
        in_specs=[held] * 9,
        out_specs=(anywhere,) * len(out_shape),
        scratch_shapes=[
            pltpu.SMEM(intersection.shape, intersection.dtype),
            pltpu.SMEM(slot_of.shape, slot_of.dtype),
            pltpu.SMEM(counts.shape, counts.dtype),
            pltpu.SMEM(step_scale.shape, step_scale.dtype),
            pltpu.VMEM(norm_gain.shape, norm_gain.dtype),
            pltpu.VMEM((3, shard_rows, features), w_query.dtype),
            pltpu.VMEM((frames * entries, 2, features), mem_cache.dtype),
            pltpu.VMEM(small.shape, small.dtype),
            pltpu.SemaphoreType.DMA((3,)),
            pltpu.SemaphoreType.DMA((3, 4)),
            pltpu.SemaphoreType.DMA((6,)),
            pltpu.SemaphoreType.DMA((frames * entries,)),
            pltpu.SemaphoreType.DMA((devices,)),
        ],
        name="pack",
    )(w_query, w_key, w_value, intersection, slot_of, counts, step_scale, norm_gain, mem_cache)
    return outs[:4], outs[4], outs[5:]


def all_pieces(own, beside, even, odd):
    late = late_plane(lax.axis_size("frame"))

    def direct(bits):
        sent = even if bits % 2 == 0 else odd
        return moved(sent, lambda x, p, y, c: (x, p ^ bits, y ^ x ^ c, c))

    near = moved(beside, lambda x, p, y, c: (x, p, 1 - y, c))
    pieces = [("own", own, [(0, 0, False)]), ("near", near, [(0, 1, False)])]
    early = list(range(1, late))
    for name, bits_list in (("early", early), ("late", [late])):
        if not bits_list:
            continue
        arrays = [direct(bits) for bits in bits_list]
        if len(arrays) > 1:
            arrays = [jnp.concatenate(arrays)]
        pieces.append((name, arrays[0], [(bits, 0, True) for bits in bits_list]))
        crossed = moved(arrays[0], lambda x, p, y, c: (1 - x, p, y, c))
        pieces.append((f"cross_{name}", crossed, [(bits, 1, True) for bits in bits_list]))
    found = [(array, tuple(place + (0,) for place in places)) for _, array, places in pieces]
    for name, array, places in pieces:
        swapped = moved(array, lambda x, p, y, c: (x, p, y, 1 - c))
        found.append((swapped, tuple(place + (1,) for place in places)))
    return found


def all_memory(parts):
    devices = lax.axis_size("frame")
    near = [parts[0]] + [hop(part, place) for place, part in enumerate(parts) if place]
    held = jnp.stack(near)
    for bit in range(2, devices.bit_length() - 1):
        half = held.shape[1] // 2
        arrived = hop(held[:, half:], 1 << bit)
        held = jnp.concatenate([held[:, :half], arrived])
    keys, values = held[:, 0, :, 0, :], held[:, 0, :, 1, :]
    return keys.reshape(-1, keys.shape[-1]), values.reshape(-1, values.shape[-1])


def hop(array, bits):
    return lax.ppermute(array, "frame", [(i, i ^ bits) for i in range(lax.axis_size("frame"))])


def all_tokens(latent):
    def swapped(array):
        return moved(array, lambda x, p, y, c: (x, p, y, 1 - c))

    far = moved(latent, lambda x, p, y, c: (x, p ^ 1, y, c))
    near = moved(latent, lambda x, p, y, c: (x, p, 1 - y, c))
    far_near = moved(far, lambda x, p, y, c: (x, p, 1 - y, c))
    home = (latent, near, swapped(latent), swapped(near))
    return home + (far, far_near, swapped(far), swapped(far_near))


def late_plane(devices):
    return devices // 4 - 1


def piece_start(place, shard_rows, plane_number):
    x, _, _, y, c = here()
    _, y_bits, with_x, c_bits = place
    from_y, from_c = flipped(y, y_bits), flipped(c, c_bits)
    if with_x:
        from_y = joined_bits(joined_bits(from_y, x), from_c)
    return pl.multiple_of((plane_number * 4 + from_y * 2 + from_c) * shard_rows, 16)


def gather_pieces(piece_refs, places, first_plane, weights):
    for ref, shards in zip(piece_refs, places):
        rows = ref.shape[0] // len(shards)
        for number, place in enumerate(shards):
            start = piece_start(place, rows, place[0] - first_plane)
            weights[pl.ds(start, rows), :] = ref[number * rows : (number + 1) * rows, :]


def store_normed(current, rows, inverse, gain_ref, normed):
    _, _, plane, _, _ = here()
    planes = lax.axis_size("frame") // 4
    span = current.shape[1] // planes
    for bits in range(planes):
        spot = columns(flipped(plane, bits), span)
        widened = current[rows, spot].astype(jnp.float32)
        normed[rows, bits * span : (bits + 1) * span] = (widened * inverse * gain_ref[0:1, spot]).astype(normed.dtype)


BLOCK = 32
ATTENTION_BLOCKS = 1


def prepare_kernel(extra_ref, *refs):
    token_refs, (extra, current, normed) = refs[:8], refs[8:]
    _, _, plane, y, c = here()
    rows = token_refs[0].shape[0]
    extra[...] = extra_ref[...]
    bases = [at_y * 2 * rows + core * rows for core in (0, 1) for at_y in (y, 1 - y)]

    def fill(refs):
        @pl.loop(0, rows // BLOCK)
        def _(number):
            for ref, base in zip(refs, bases):
                tokens = ref[pl.ds(pl.multiple_of(number * BLOCK, BLOCK), BLOCK), :]
                spot = pl.ds(pl.multiple_of(base + number * BLOCK, BLOCK), BLOCK)
                current[spot, :] = tokens
                widened = tokens.astype(jnp.float32)
                inverse = lax.rsqrt(jnp.mean(widened * widened, axis=-1, keepdims=True) + 1e-06)
                store_normed(current, spot, inverse, extra, normed)

    pl.when(plane % 2 == c)(lambda: fill(token_refs[:4]))
    pl.when(plane % 2 != c)(lambda: fill(token_refs[4:]))


def project_kernel(places, *refs):
    normed = refs[0]
    piece_refs = refs[1 : 1 + len(places)]
    out, weights = refs[1 + len(places) :]
    gather_pieces(piece_refs, places, 0, weights)
    out[...] = jnp.dot(normed[:, : weights.shape[0]], weights[...], preferred_element_type=jnp.float32)


def assemble_kernel(places, *refs):
    gather_pieces(refs[:-1], places, 0, refs[-1])


def attend_heads(projected, key_ref, value_ref, extra_ref, attended, head_count):
    width = projected.shape[1] // 3
    head_size = width // head_count
    scale_dot = 1.0 / math.sqrt(head_size)
    mem_rows = key_ref.shape[0]
    live = extra_ref[3:4, :mem_rows] > 0.5
    contract_last = (((1,), (1,)), ((), ()))
    frame_rows = projected.shape[0]
    half = frame_rows // ATTENTION_BLOCKS
    for head in range(head_count):
        span = slice(head * head_size, (head + 1) * head_size)
        keys = projected[:, width + head * head_size : width + (head + 1) * head_size]
        values = projected[:, 2 * width + head * head_size : 2 * width + (head + 1) * head_size]
        for start in range(0, frame_rows, half):
            queries = projected[start : start + half, span]
            frame_scores = (
                lax.dot_general(queries, keys, contract_last, preferred_element_type=jnp.float32) * scale_dot
            )
            mem_scores = (
                lax.dot_general(queries, key_ref[:, span], contract_last, preferred_element_type=jnp.float32)
                * scale_dot
            )
            scores = jnp.concatenate([frame_scores, jnp.where(live, mem_scores, -1e30)], axis=1)
            weights = jnp.exp(scores - jnp.max(scores, axis=-1, keepdims=True))
            denominator = jnp.sum(weights, axis=-1, keepdims=True)
            rounded = weights.astype(jnp.bfloat16)
            blended = jnp.dot(
                rounded[:, :frame_rows], values, preferred_element_type=jnp.float32
            ) + jnp.dot(rounded[:, frame_rows:], value_ref[:, span], preferred_element_type=jnp.float32)
            attended[start : start + half, span] = (blended / denominator).astype(attended.dtype)


def step_kernel(places, first_plane, head_count, extra_ref, key_ref, value_ref, normed, part_ref, *refs):
    piece_refs = refs[: len(places)]
    attended, weights, projected = refs[len(places) :]
    gather_pieces(piece_refs, places, first_plane, weights)
    early = normed.shape[1] - weights.shape[0]
    projected[...] = (
        part_ref[...] + jnp.dot(normed[:, early:], weights[...], preferred_element_type=jnp.float32)
    ).astype(projected.dtype)
    attend_heads(projected, key_ref, value_ref, extra_ref, attended, head_count)


def last_step_kernel(
    update_places, head_count, extra_ref, key_ref, value_ref, current_ref, weights, first_part, second_part, third_part,
    fourth_part, keep, first, second, current, normed, projected, attended,
):
    _, _, plane, y, c = here()
    width = first_part.shape[1]
    at_home = plane % 2 == c

    @pl.loop(0, current.shape[0] // BLOCK)
    def _(number):
        rows = pl.ds(pl.multiple_of(number * BLOCK, BLOCK), BLOCK)
        total = jnp.zeros((BLOCK, 1), jnp.float32)
        for part, (plane_bits, y_bits) in zip((first_part, second_part, third_part, fourth_part), update_places):
            spot = columns(quarter_of(flipped(plane, plane_bits), flipped(y, y_bits)), width)
            updated = (
                current_ref[rows, spot].astype(jnp.float32)
                + extra_ref[1:2, :width] * part[rows, :].astype(jnp.float32)
            ).astype(current.dtype)
            current[rows, spot] = updated
            widened = updated.astype(jnp.float32)
            total = total + jnp.sum(widened * widened, axis=-1, keepdims=True)
        inverse = lax.rsqrt(total / current.shape[1] + 1e-06)
        store_normed(current, rows, inverse, extra_ref, normed)

    projected[...] = jnp.dot(normed[...], weights[...], preferred_element_type=jnp.float32).astype(projected.dtype)
    attend_heads(projected, key_ref, value_ref, extra_ref, attended, head_count)
    spot = columns(quarter_of(plane, y), width)
    attended[...] = (
        current[:, spot].astype(jnp.float32) + extra_ref[2:3, :width] * attended[...].astype(jnp.float32)
    ).astype(attended.dtype)
    chip_rows = attended.shape[0] // 2

    def part(at_y):
        return attended[pl.ds(pl.multiple_of(at_y * chip_rows, chip_rows), chip_rows), :]

    keep[...] = part(y)
    second[...] = part(1 - y)

    @pl.when(at_home)
    def _():
        first[...] = part(1 - y)

    @pl.when(jnp.logical_not(at_home))
    def _():
        first[...] = part(y)


MIB = 1024 * 1024


def kernel_call(kernel, out_shape, operands, anywhere, scratch_shapes, limit, flops):
    vectors = pl.BlockSpec(memory_space=pltpu.VMEM)
    free = pl.BlockSpec(memory_space=pl.ANY)
    moved_bytes = sum(operand.size * operand.dtype.itemsize for operand in operands)
    return pl.pallas_call(
        kernel,
        out_shape=out_shape,
        in_specs=[free if number in anywhere else vectors for number in range(len(operands))],
        out_specs=jax.tree.map(lambda _: vectors, out_shape),
        scratch_shapes=scratch_shapes,
        compiler_params=pltpu.CompilerParams(vmem_limit_bytes=limit),
        cost_estimate=pl.CostEstimate(flops=flops, transcendentals=0, bytes_accessed=moved_bytes),
    )(*operands)


def prepare(extra, tokens):
    frame = jax.ShapeDtypeStruct((4 * tokens[0].shape[0], tokens[0].shape[1]), tokens[0].dtype)
    return kernel_call(
        prepare_kernel,
        (jax.ShapeDtypeStruct(extra.shape, extra.dtype), frame, frame),
        (extra, *tokens),
        (),
        [],
        8 * MIB,
        0,
    )


def project(normed, pieces):
    width = pieces[0][0].shape[1]
    depth = sum(array.shape[0] for array, _ in pieces)
    return kernel_call(
        functools.partial(project_kernel, tuple(place for _, place in pieces)),
        jax.ShapeDtypeStruct((normed.shape[0], width), jnp.float32),
        (normed, *[array for array, _ in pieces]),
        (),
        [pltpu.VMEM((depth, width), normed.dtype)],
        16 * MIB,
        2 * normed.shape[0] * depth * width,
    )


def assemble(pieces):
    width = pieces[0][0].shape[1]
    depth = sum(array.shape[0] for array, _ in pieces)
    return kernel_call(
        functools.partial(assemble_kernel, tuple(place for _, place in pieces)),
        jax.ShapeDtypeStruct((depth, width), pieces[0][0].dtype),
        [array for array, _ in pieces],
        (),
        [],
        8 * MIB,
        0,
    )


def step(extra, keys, values, normed, part, pieces):
    width = pieces[0][0].shape[1]
    depth = sum(array.shape[0] for array, _ in pieces)
    frame_rows = normed.shape[0]
    return kernel_call(
        functools.partial(step_kernel, tuple(place for _, place in pieces), pieces[0][1][0][0], HEADS // SPATIAL),
        jax.ShapeDtypeStruct((frame_rows, width // 3), normed.dtype),
        (extra, keys, values, normed, part, *[array for array, _ in pieces]),
        (),
        [pltpu.VMEM((depth, width), normed.dtype), pltpu.VMEM((frame_rows, width), normed.dtype)],
        16 * MIB,
        2 * frame_rows * width * (depth + frame_rows),
    )


def last_step(extra, keys, values, current, weights, updates):
    frame_rows, features = current.shape
    width = weights.shape[1] // 3
    share = jax.ShapeDtypeStruct((frame_rows // 2, width), current.dtype)
    return kernel_call(
        functools.partial(last_step_kernel, tuple(place for _, place in updates), HEADS // SPATIAL),
        (share,) * 3,
        (extra, keys, values, current, weights, *[array for array, _ in updates]),
        (),
        [
            pltpu.VMEM((frame_rows, features), current.dtype),
            pltpu.VMEM((frame_rows, features), current.dtype),
            pltpu.VMEM((frame_rows, 3 * width), current.dtype),
            pltpu.VMEM((frame_rows, width), current.dtype),
        ],
        16 * MIB,
        2 * frame_rows * 3 * width * (features + frame_rows),
    )


def join_kernel(keep, first, second, other_keep, other_first, other_second, out):
    _, _, plane, y, c = here()
    low = plane % 2
    rows, width = out.shape[0], keep.shape[1]

    def put(ref, start, plane_low, at_y):
        out[:, columns(plane_low * 2 + at_y, width)] = ref[start : start + rows, :]

    @pl.when(low == c)
    def _():
        put(keep, 0, low, y)
        put(first, 0, low, 1 - y)
        put(other_first, 0, 1 - low, y)
        put(other_second, 0, 1 - low, 1 - y)

    @pl.when(low != c)
    def _():
        put(other_keep, rows, low, y)
        put(other_first, rows, low, 1 - y)
        put(first, rows, 1 - low, y)
        put(second, rows, 1 - low, 1 - y)


def joined(keep, first, second):
    def at_home(p, c):
        return c == p % 2

    def swapped(array):
        return moved(array, lambda x, p, y, c: (x, p, y, 1 - c))

    first = moved(first, lambda x, p, y, c: (x, p, 1 - y, c) if at_home(p, c) else (x, p ^ 1, y, 1 - c))
    second = moved(second, lambda x, p, y, c: None if at_home(p, c) else (x, p ^ 1, 1 - y, 1 - c))
    others = (swapped(keep), swapped(first), swapped(second))
    rows, width = keep.shape
    return kernel_call(
        join_kernel,
        jax.ShapeDtypeStruct((rows // 2, width * SPATIAL), keep.dtype),
        (keep, first, second, *others),
        (),
        [],
        4 * MIB,
        0,
    )


def paired_planes(
    latent, norm_gain, w_query, w_key, w_value, mem_cache, intersection, counts, slot_of, step_scale
):
    late = late_plane(lax.axis_size("frame"))
    weights, extra, memory = pack(
        w_query, w_key, w_value, intersection, slot_of, counts, step_scale, norm_gain, mem_cache
    )
    extra = moved(extra, lambda x, p, y, c: (x, p, y, 1 - c))
    pieces = all_pieces(*weights)
    tokens = all_tokens(latent)
    keys, values = all_memory(memory)
    extra, current, normed = prepare(extra, tokens)
    part = project(normed, [piece for piece in pieces if piece[1][0][0] < late])
    attended = step(extra, keys, values, normed, part, [piece for piece in pieces if piece[1][0][0] == late])
    updates = [
        (attended, (0, 0)),
        (moved(attended, lambda x, p, y, c: (x, p ^ 1, 1 - y, c)), (1, 1)),
        (moved(attended, lambda x, p, y, c: (x, p ^ 1, y, c)), (1, 0)),
        (moved(attended, lambda x, p, y, c: (x, p, 1 - y, c)), (0, 1)),
    ]
    shares = last_step(extra, keys, values, current, assemble(pieces), updates)
    return joined(*shares)


def fits_paired_planes(latent, norm_gain, w_query, w_key, w_value, mem_cache, *_):
    devices = lax.axis_size("frame")
    planes = devices // SPATIAL
    return (
        lax.axis_size("groups") == 2
        and devices == planes * SPATIAL
        and planes >= 2
        and planes & (planes - 1) == 0
        and w_query.shape[0] % 16 == 0
        and mem_cache.shape[1] == 1
    )


def from_partner(array, axis, bit):
    return lax.ppermute(array, axis, [(i, i ^ 1 << bit) for i in range(lax.axis_size(axis))])


def in_order(mine, theirs, upper, axis_dim):
    low_first = jnp.concatenate([mine, theirs], axis=axis_dim)
    high_first = jnp.concatenate([theirs, mine], axis=axis_dim)
    return jnp.where(upper, high_first, low_first)


def attend(queries, frame_pair, mem_keys, mem_values, live_keys, head_count):
    tok_rows, feature_width = queries.shape
    head_size = feature_width // head_count
    scale_dot = 1.0 / math.sqrt(head_size)
    q_heads = queries.reshape(tok_rows, head_count, head_size)
    k_heads = frame_pair[0].reshape(-1, head_count, head_size)
    v_heads = frame_pair[1].reshape(-1, head_count, head_size)
    frame_scores = (
        jnp.einsum("thd,khd->htk", q_heads, k_heads, preferred_element_type=jnp.float32) * scale_dot
    )
    remote_scores = (
        jnp.einsum("thd,khd->htk", q_heads, mem_keys, preferred_element_type=jnp.float32)
        * scale_dot
    )
    remote_scores = jnp.where(live_keys[None, None, :], remote_scores, -1e30)
    largest = jnp.maximum(
        jnp.max(frame_scores, axis=-1, keepdims=True),
        jnp.max(remote_scores, axis=-1, keepdims=True),
    )
    frame_weights = jnp.exp(frame_scores - largest)
    remote_weights = jnp.exp(remote_scores - largest)
    denominator = jnp.sum(frame_weights, axis=-1) + jnp.sum(remote_weights, axis=-1)
    blended = jnp.einsum(
        "htk,khd->thd",
        frame_weights.astype(jnp.bfloat16),
        v_heads,
        preferred_element_type=jnp.float32,
    )
    blended = blended + jnp.einsum(
        "htk,khd->thd",
        remote_weights.astype(jnp.bfloat16),
        mem_values,
        preferred_element_type=jnp.float32,
    )
    blended = blended / jnp.transpose(denominator)[:, :, None]
    return blended.reshape(tok_rows, feature_width).astype(jnp.bfloat16)


def rms_normed(current, norm_gain):
    widened = current.astype(jnp.float32)
    inverse = lax.rsqrt(jnp.mean(widened * widened, axis=-1, keepdims=True) + 1e-06)
    return (widened, (widened * inverse * norm_gain).astype(jnp.bfloat16))


def separate_frames(
    latent, norm_gain, w_query, w_key, w_value, mem_cache, intersection, counts, slot_of, step_scale
):
    devices = lax.axis_size("frame")
    position = lax.axis_index("frame")
    frame_index = position // SPATIAL
    doublings = SPATIAL.bit_length() - 1
    target_frame = jnp.arange(devices, dtype=jnp.int32) // SPATIAL
    current = latent
    feature_width = latent.shape[1]
    share_width = feature_width // SPATIAL
    head_share = HEADS // SPATIAL

    def column_pieces(weight):
        row_count = weight.shape[0]
        split_cols = jnp.transpose(weight.reshape(row_count, SPATIAL, share_width), (1, 0, 2))
        return jnp.tile(split_cols, (devices // SPATIAL, 1, 1))

    own_query, own_key, own_value = (
        lax.all_to_all(column_pieces(w_query), "frame", split_axis=0, concat_axis=1, tiled=True),
        lax.all_to_all(column_pieces(w_key), "frame", split_axis=0, concat_axis=1, tiled=True),
        lax.all_to_all(column_pieces(w_value), "frame", split_axis=0, concat_axis=1, tiled=True),
    )
    own_query, own_key, own_value = (own_query[0], own_key[0], own_value[0])
    listed = mem_cache[slot_of[intersection[target_frame]]]
    list_len = listed.shape[1]
    local_mem = listed.shape[2]
    grouped = listed.reshape(
        devices // SPATIAL, SPATIAL, list_len, local_mem, 2, SPATIAL, share_width
    )
    diagonal_part = jnp.diagonal(grouped, axis1=1, axis2=5)
    outgoing = jnp.moveaxis(diagonal_part, -1, 1).reshape(
        devices, list_len, local_mem, 2, share_width
    )
    fetched = lax.all_to_all(outgoing, "frame", split_axis=0, concat_axis=2, tiled=True)[0]
    mem_len = fetched.shape[1]
    mem_keys = fetched[:, :, 0, :].reshape(list_len * mem_len, head_share, HS)
    mem_values = fetched[:, :, 1, :].reshape(list_len * mem_len, head_share, HS)
    live_keys = jnp.arange(list_len * mem_len, dtype=jnp.int32) // mem_len < counts[frame_index]
    tok_rows = latent.shape[0]
    for step_index in range(STEPS):
        widened, normed = rms_normed(current, norm_gain)
        gathered = normed
        for bit_index in range(doublings):
            partner = from_partner(gathered, "frame", bit_index)
            gathered = in_order(gathered, partner, position >> bit_index & 1 == 1, 0)
        queries = jnp.dot(gathered, own_query, preferred_element_type=jnp.float32).astype(
            jnp.bfloat16
        )
        keys_frame = jnp.dot(gathered, own_key, preferred_element_type=jnp.float32).astype(
            jnp.bfloat16
        )
        values_frame = jnp.dot(gathered, own_value, preferred_element_type=jnp.float32).astype(
            jnp.bfloat16
        )
        frame_pair = jnp.stack([keys_frame, values_frame])
        attended = attend(queries, frame_pair, mem_keys, mem_values, live_keys, head_share)
        blocks = attended.reshape(SPATIAL, tok_rows, share_width)[:, None]
        for bit_index in range(doublings):
            upper = position >> bit_index & 1 == 1
            dest_count = blocks.shape[0]
            paired = blocks.reshape((dest_count // 2, 2) + blocks.shape[1:])
            kept = jnp.where(upper, paired[:, 1], paired[:, 0])
            sent = jnp.where(upper, paired[:, 0], paired[:, 1])
            arrived = from_partner(sent, "frame", bit_index)
            blocks = in_order(kept, arrived, upper, 1)
        joined = jnp.transpose(blocks[0], (1, 0, 2)).reshape(tok_rows, feature_width)
        current = (widened + step_scale[step_index] * joined.astype(jnp.float32)).astype(
            jnp.bfloat16
        )
    return current


def per_device(*arguments):
    return (paired_planes if fits_paired_planes(*arguments) else separate_frames)(*arguments)


def solution(mesh):
    placed = (
        P(("groups", "frame"), None),
        P(),
        P("frame", None),
        P("frame", None),
        P("frame", None),
        P("groups", "frame", None, None),
        P("groups", None),
        P("groups"),
        P("groups"),
        P(),
    )
    return jax.shard_map(
        per_device,
        mesh=mesh,
        in_specs=placed,
        out_specs=P(("groups", "frame"), None),
        check_vma=False,
    )
```

```python
import functools
import math

import jax
import jax.numpy as jnp
from jax import lax
from jax.experimental import pallas as pl
from jax.experimental.pallas import tpu as pltpu
from jax.sharding import PartitionSpec as P


HEADS = 12
HS = 128
SPATIAL = 4
STEPS = 2
AXES = ("groups", "frame")


def coords(index):
    return index // 4, (index // 2) % 2, index % 2


def quarter_of(plane, y):
    return (plane % 2) * 2 + y


def moved(array, target):
    devices = lax.axis_size("frame")
    pairs = []
    for x in range(lax.axis_size("groups")):
        for index in range(devices):
            place = target(x, *coords(index))
            if place is not None:
                to_x, to_plane, to_y, to_c = place
                pairs.append((x * devices + index, to_x * devices + to_plane * 4 + to_y * 2 + to_c))
    return lax.ppermute(array, AXES, pairs)


def here():
    x = lax.axis_index("groups")
    index = lax.axis_index("frame")
    plane = index // 4
    rest = index - plane * 4
    y = rest // 2
    return x, index, plane, y, rest - y * 2


def flipped(value, bits):
    out = value
    bit = 1
    while bit <= bits:
        if bits & bit:
            out = out + bit - 2 * bit * ((value // bit) % 2)
        bit *= 2
    return out


def joined_bits(one, other):
    return one + other - 2 * one * other


def columns(quarter, width):
    return pl.ds(pl.multiple_of(quarter * width, 128), width)


def pack_kernel(
    w_query, w_key, w_value, list_hbm, slot_hbm, count_hbm, scale_hbm, gain_hbm, mem_ref,
    own_ref, beside_ref, even_ref, odd_ref, extra_ref, *refs,
):
    near_count = SPATIAL
    memory_refs = refs[:near_count]
    (
        list_ref, slot_ref, count_ref, scale_ref, gain, rows, stored, extra, row_sem, out_sem, scalar_sem, mem_sem, give_sem,
    ) = refs[near_count:]
    x, index, plane, y, c = here()
    devices = lax.axis_size("frame")
    frames, entries = list_ref.shape
    width = own_ref.shape[1] // 3
    scalars = [
        pltpu.make_async_copy(source, target, scalar_sem.at[number])
        for number, (source, target) in enumerate(
            (
                (list_hbm, list_ref),
                (slot_hbm, slot_ref),
                (count_hbm, count_ref),
                (scale_hbm, scale_ref),
                (gain_hbm, gain),
            )
        )
    ]
    for copy in scalars[:2]:
        copy.start()
    reads = []
    for number, weight in enumerate((w_query, w_key, w_value)):
        reads.append(pltpu.make_async_copy(weight, rows.at[number], row_sem.at[number]))
        reads[-1].start()
    for copy in scalars[2:]:
        copy.start()
    for copy in scalars[:2]:
        copy.wait()
    picks = []
    for frame in range(frames):
        for entry in range(entries):
            number = frame * entries + entry
            row = slot_ref[list_ref[frame, entry]]
            picks.append(pltpu.make_async_copy(mem_ref.at[row, 0], stored.at[number], mem_sem.at[number]))
            picks[-1].start()
    across = joined_bits(joined_bits(x, y), c)
    low = plane % 2
    quarters = (low * 2 + across, (1 - low) * 2 + across, low * 2 + 1 - y, quarter_of(plane, y))
    gives = []
    for number, read in enumerate(reads):
        read.wait()
        for place, (quarter, out) in enumerate(zip(quarters, (even_ref, odd_ref, beside_ref, own_ref))):
            gives.append(
                pltpu.make_async_copy(
                    rows.at[number, :, columns(quarter, width)],
                    out.at[:, pl.ds(number * width, width)],
                    out_sem.at[number, place],
                )
            )
            gives[-1].start()
    for copy in scalars[2:]:
        copy.wait()
    row = (1, extra.shape[1])
    extra[0:1, :] = gain[...].reshape(row)
    for number in range(STEPS):
        extra[1 + number : 2 + number, :] = jnp.full(row, scale_ref[number], jnp.float32)
    live = lax.broadcasted_iota(jnp.int32, row, 1) % entries < count_ref[(plane // 2) * 2 + 1 - c]
    extra[1 + STEPS : 2 + STEPS, :] = jnp.where(live, 1.0, 0.0)
    gives.append(pltpu.make_async_copy(extra, extra_ref, scalar_sem.at[5]))
    gives[-1].start()
    for pick in picks:
        pick.wait()
    bits = devices.bit_length() - 1
    for away in range(devices):
        to_plane, to_y, to_c = coords(flipped(index, away))
        to_frame = (to_plane // 2) * 2 + to_c
        place = 0
        for bit in range(2, bits):
            place = place * 2 + (away >> bit & 1)
        gives.append(
            pltpu.make_async_copy(
                stored.at[pl.ds(to_frame * entries, entries), :, columns(quarter_of(to_plane, to_y), width)],
                memory_refs[away % SPATIAL].at[place],
                give_sem.at[away],
            )
        )
        gives[-1].start()
    for give in gives:
        give.wait()


def pack(w_query, w_key, w_value, intersection, slot_of, counts, step_scale, norm_gain, mem_cache):
    devices = lax.axis_size("frame")
    shard_rows, features = w_query.shape
    frames, entries = intersection.shape
    piece = jax.ShapeDtypeStruct((shard_rows, 3 * (features // SPATIAL)), w_query.dtype)
    small = jax.ShapeDtypeStruct((2 + STEPS, features), jnp.float32)
    memory = jax.ShapeDtypeStruct((devices // SPATIAL, entries, 2, features // SPATIAL), mem_cache.dtype)
    out_shape = (piece,) * 4 + (small,) + (memory,) * SPATIAL
    anywhere = pl.BlockSpec(memory_space=pl.ANY)
    held = pl.BlockSpec(memory_space=pltpu.HBM)
    outs = pl.pallas_call(
        pack_kernel,
        out_shape=out_shape,
        in_specs=[held] * 9,
        out_specs=(anywhere,) * len(out_shape),
        scratch_shapes=[
            pltpu.SMEM(intersection.shape, intersection.dtype),
            pltpu.SMEM(slot_of.shape, slot_of.dtype),
            pltpu.SMEM(counts.shape, counts.dtype),
            pltpu.SMEM(step_scale.shape, step_scale.dtype),
            pltpu.VMEM(norm_gain.shape, norm_gain.dtype),
            pltpu.VMEM((3, shard_rows, features), w_query.dtype),
            pltpu.VMEM((frames * entries, 2, features), mem_cache.dtype),
            pltpu.VMEM(small.shape, small.dtype),
            pltpu.SemaphoreType.DMA((3,)),
            pltpu.SemaphoreType.DMA((3, 4)),
            pltpu.SemaphoreType.DMA((6,)),
            pltpu.SemaphoreType.DMA((frames * entries,)),
            pltpu.SemaphoreType.DMA((devices,)),
        ],
        name="pack",
    )(w_query, w_key, w_value, intersection, slot_of, counts, step_scale, norm_gain, mem_cache)
    return outs[:4], outs[4], outs[5:]


def all_pieces(own, beside, even, odd):
    late = late_plane(lax.axis_size("frame"))

    def direct(bits):
        sent = even if bits % 2 == 0 else odd
        return moved(sent, lambda x, p, y, c: (x, p ^ bits, y ^ x ^ c, c))

    near = moved(beside, lambda x, p, y, c: (x, p, 1 - y, c))
    pieces = [("own", own, [(0, 0, False)]), ("near", near, [(0, 1, False)])]
    early = list(range(1, late))
    for name, bits_list in (("early", early), ("late", [late])):
        if not bits_list:
            continue
        arrays = [direct(bits) for bits in bits_list]
        if len(arrays) > 1:
            arrays = [jnp.concatenate(arrays)]
        pieces.append((name, arrays[0], [(bits, 0, True) for bits in bits_list]))
        crossed = moved(arrays[0], lambda x, p, y, c: (1 - x, p, y, c))
        pieces.append((f"cross_{name}", crossed, [(bits, 1, True) for bits in bits_list]))
    found = [(array, tuple(place + (0,) for place in places)) for _, array, places in pieces]
    for name, array, places in pieces:
        swapped = moved(array, lambda x, p, y, c: (x, p, y, 1 - c))
        found.append((swapped, tuple(place + (1,) for place in places)))
    return found


def all_memory(parts):
    devices = lax.axis_size("frame")
    near = [parts[0]] + [hop(part, place) for place, part in enumerate(parts) if place]
    held = jnp.stack(near)
    for bit in range(2, devices.bit_length() - 1):
        half = held.shape[1] // 2
        arrived = hop(held[:, half:], 1 << bit)
        held = jnp.concatenate([held[:, :half], arrived])
    keys, values = held[:, 0, :, 0, :], held[:, 0, :, 1, :]
    return keys.reshape(-1, keys.shape[-1]), values.reshape(-1, values.shape[-1])


def hop(array, bits):
    return lax.ppermute(array, "frame", [(i, i ^ bits) for i in range(lax.axis_size("frame"))])


def all_tokens(latent):
    def swapped(array):
        return moved(array, lambda x, p, y, c: (x, p, y, 1 - c))

    far = moved(latent, lambda x, p, y, c: (x, p ^ 1, y, c))
    near = moved(latent, lambda x, p, y, c: (x, p, 1 - y, c))
    far_near = moved(far, lambda x, p, y, c: (x, p, 1 - y, c))
    home = (latent, near, swapped(latent), swapped(near))
    return home + (far, far_near, swapped(far), swapped(far_near))


def late_plane(devices):
    return devices // 4 - 1


def piece_start(place, shard_rows, plane_number):
    x, _, _, y, c = here()
    _, y_bits, with_x, c_bits = place
    from_y, from_c = flipped(y, y_bits), flipped(c, c_bits)
    if with_x:
        from_y = joined_bits(joined_bits(from_y, x), from_c)
    return pl.multiple_of((plane_number * 4 + from_y * 2 + from_c) * shard_rows, 16)


def gather_pieces(piece_refs, places, first_plane, weights):
    for ref, shards in zip(piece_refs, places):
        rows = ref.shape[0] // len(shards)
        for number, place in enumerate(shards):
            start = piece_start(place, rows, place[0] - first_plane)
            weights[pl.ds(start, rows), :] = ref[number * rows : (number + 1) * rows, :]


def store_normed(current, rows, inverse, gain_ref, normed):
    _, _, plane, _, _ = here()
    planes = lax.axis_size("frame") // 4
    span = current.shape[1] // planes
    for bits in range(planes):
        spot = columns(flipped(plane, bits), span)
        widened = current[rows, spot].astype(jnp.float32)
        normed[rows, bits * span : (bits + 1) * span] = (widened * inverse * gain_ref[0:1, spot]).astype(normed.dtype)


BLOCK = 32
ATTENTION_BLOCKS = 1


def prepare_kernel(extra_ref, *refs):
    token_refs, (extra, current, normed) = refs[:8], refs[8:]
    _, _, plane, y, c = here()
    rows = token_refs[0].shape[0]
    extra[...] = extra_ref[...]
    bases = [at_y * 2 * rows + core * rows for core in (0, 1) for at_y in (y, 1 - y)]

    def fill(refs):
        @pl.loop(0, rows // BLOCK)
        def _(number):
            for ref, base in zip(refs, bases):
                tokens = ref[pl.ds(pl.multiple_of(number * BLOCK, BLOCK), BLOCK), :]
                spot = pl.ds(pl.multiple_of(base + number * BLOCK, BLOCK), BLOCK)
                current[spot, :] = tokens
                widened = tokens.astype(jnp.float32)
                inverse = lax.rsqrt(jnp.mean(widened * widened, axis=-1, keepdims=True) + 1e-06)
                store_normed(current, spot, inverse, extra, normed)

    pl.when(plane % 2 == c)(lambda: fill(token_refs[:4]))
    pl.when(plane % 2 != c)(lambda: fill(token_refs[4:]))


def project_kernel(places, *refs):
    normed = refs[0]
    piece_refs = refs[1 : 1 + len(places)]
    out, weights = refs[1 + len(places) :]
    gather_pieces(piece_refs, places, 0, weights)
    out[...] = jnp.dot(normed[:, : weights.shape[0]], weights[...], preferred_element_type=jnp.float32)


def assemble_kernel(places, *refs):
    gather_pieces(refs[:-1], places, 0, refs[-1])


def attend_heads(projected, key_ref, value_ref, extra_ref, attended, head_count):
    width = projected.shape[1] // 3
    head_size = width // head_count
    scale_dot = 1.0 / math.sqrt(head_size)
    mem_rows = key_ref.shape[0]
    live = extra_ref[3:4, :mem_rows] > 0.5
    contract_last = (((1,), (1,)), ((), ()))
    frame_rows = projected.shape[0]
    half = frame_rows // ATTENTION_BLOCKS
    for head in range(head_count):
        span = slice(head * head_size, (head + 1) * head_size)
        keys = projected[:, width + head * head_size : width + (head + 1) * head_size]
        values = projected[:, 2 * width + head * head_size : 2 * width + (head + 1) * head_size]
        for start in range(0, frame_rows, half):
            queries = projected[start : start + half, span]
            frame_scores = (
                lax.dot_general(queries, keys, contract_last, preferred_element_type=jnp.float32) * scale_dot
            )
            mem_scores = (
                lax.dot_general(queries, key_ref[:, span], contract_last, preferred_element_type=jnp.float32)
                * scale_dot
            )
            scores = jnp.concatenate([frame_scores, jnp.where(live, mem_scores, -1e30)], axis=1)
            weights = jnp.exp(scores - jnp.max(scores, axis=-1, keepdims=True))
            denominator = jnp.sum(weights, axis=-1, keepdims=True)
            rounded = weights.astype(jnp.bfloat16)
            blended = jnp.dot(
                rounded[:, :frame_rows], values, preferred_element_type=jnp.float32
            ) + jnp.dot(rounded[:, frame_rows:], value_ref[:, span], preferred_element_type=jnp.float32)
            attended[start : start + half, span] = (blended / denominator).astype(attended.dtype)


def step_kernel(places, first_plane, head_count, extra_ref, key_ref, value_ref, normed, part_ref, *refs):
    piece_refs = refs[: len(places)]
    attended, weights, projected = refs[len(places) :]
    gather_pieces(piece_refs, places, first_plane, weights)
    early = normed.shape[1] - weights.shape[0]
    projected[...] = (
        part_ref[...] + jnp.dot(normed[:, early:], weights[...], preferred_element_type=jnp.float32)
    ).astype(projected.dtype)
    attend_heads(projected, key_ref, value_ref, extra_ref, attended, head_count)


def last_step_kernel(
    update_places, head_count, extra_ref, key_ref, value_ref, current_ref, weights, first_part, second_part, third_part,
    fourth_part, keep, first, second, third, fourth, current, normed, projected, attended,
):
    _, _, plane, y, c = here()
    width = first_part.shape[1]
    at_home = plane % 2 == c

    @pl.loop(0, current.shape[0] // BLOCK)
    def _(number):
        rows = pl.ds(pl.multiple_of(number * BLOCK, BLOCK), BLOCK)
        total = jnp.zeros((BLOCK, 1), jnp.float32)
        for part, (plane_bits, y_bits) in zip((first_part, second_part, third_part, fourth_part), update_places):
            spot = columns(quarter_of(flipped(plane, plane_bits), flipped(y, y_bits)), width)
            updated = (
                current_ref[rows, spot].astype(jnp.float32)
                + extra_ref[1:2, :width] * part[rows, :].astype(jnp.float32)
            ).astype(current.dtype)
            current[rows, spot] = updated
            widened = updated.astype(jnp.float32)
            total = total + jnp.sum(widened * widened, axis=-1, keepdims=True)
        inverse = lax.rsqrt(total / current.shape[1] + 1e-06)
        store_normed(current, rows, inverse, extra_ref, normed)

    projected[...] = jnp.dot(normed[...], weights[...], preferred_element_type=jnp.float32).astype(projected.dtype)
    attend_heads(projected, key_ref, value_ref, extra_ref, attended, head_count)
    spot = columns(quarter_of(plane, y), width)
    attended[...] = (
        current[:, spot].astype(jnp.float32) + extra_ref[2:3, :width] * attended[...].astype(jnp.float32)
    ).astype(attended.dtype)
    chip_rows = attended.shape[0] // 2
    rows = chip_rows // 2
    here_rows, there_rows = y * chip_rows, (1 - y) * chip_rows

    def part(start):
        return attended[pl.ds(pl.multiple_of(start, rows), rows), :]

    keep[...] = part(here_rows)
    fourth[...] = part(there_rows + rows)

    @pl.when(at_home)
    def _():
        first[...] = part(there_rows)
        second[...] = part(there_rows + rows)
        third[...] = part(here_rows + rows)

    @pl.when(jnp.logical_not(at_home))
    def _():
        first[...] = part(here_rows + rows)
        second[...] = part(here_rows)
        third[...] = part(there_rows)


MIB = 1024 * 1024


def kernel_call(kernel, out_shape, operands, anywhere, scratch_shapes, limit, flops):
    vectors = pl.BlockSpec(memory_space=pltpu.VMEM)
    free = pl.BlockSpec(memory_space=pl.ANY)
    moved_bytes = sum(operand.size * operand.dtype.itemsize for operand in operands)
    return pl.pallas_call(
        kernel,
        out_shape=out_shape,
        in_specs=[free if number in anywhere else vectors for number in range(len(operands))],
        out_specs=jax.tree.map(lambda _: vectors, out_shape),
        scratch_shapes=scratch_shapes,
        compiler_params=pltpu.CompilerParams(vmem_limit_bytes=limit),
        cost_estimate=pl.CostEstimate(flops=flops, transcendentals=0, bytes_accessed=moved_bytes),
    )(*operands)


def prepare(extra, tokens):
    frame = jax.ShapeDtypeStruct((4 * tokens[0].shape[0], tokens[0].shape[1]), tokens[0].dtype)
    return kernel_call(
        prepare_kernel,
        (jax.ShapeDtypeStruct(extra.shape, extra.dtype), frame, frame),
        (extra, *tokens),
        (),
        [],
        8 * MIB,
        0,
    )


def project(normed, pieces):
    width = pieces[0][0].shape[1]
    depth = sum(array.shape[0] for array, _ in pieces)
    return kernel_call(
        functools.partial(project_kernel, tuple(place for _, place in pieces)),
        jax.ShapeDtypeStruct((normed.shape[0], width), jnp.float32),
        (normed, *[array for array, _ in pieces]),
        (),
        [pltpu.VMEM((depth, width), normed.dtype)],
        16 * MIB,
        2 * normed.shape[0] * depth * width,
    )


def assemble(pieces):
    width = pieces[0][0].shape[1]
    depth = sum(array.shape[0] for array, _ in pieces)
    return kernel_call(
        functools.partial(assemble_kernel, tuple(place for _, place in pieces)),
        jax.ShapeDtypeStruct((depth, width), pieces[0][0].dtype),
        [array for array, _ in pieces],
        (),
        [],
        8 * MIB,
        0,
    )


def step(extra, keys, values, normed, part, pieces):
    width = pieces[0][0].shape[1]
    depth = sum(array.shape[0] for array, _ in pieces)
    frame_rows = normed.shape[0]
    return kernel_call(
        functools.partial(step_kernel, tuple(place for _, place in pieces), pieces[0][1][0][0], HEADS // SPATIAL),
        jax.ShapeDtypeStruct((frame_rows, width // 3), normed.dtype),
        (extra, keys, values, normed, part, *[array for array, _ in pieces]),
        (),
        [pltpu.VMEM((depth, width), normed.dtype), pltpu.VMEM((frame_rows, width), normed.dtype)],
        16 * MIB,
        2 * frame_rows * width * (depth + frame_rows),
    )


def last_step(extra, keys, values, current, weights, updates):
    frame_rows, features = current.shape
    width = weights.shape[1] // 3
    share = jax.ShapeDtypeStruct((frame_rows // 4, width), current.dtype)
    return kernel_call(
        functools.partial(last_step_kernel, tuple(place for _, place in updates), HEADS // SPATIAL),
        (share,) * 5,
        (extra, keys, values, current, weights, *[array for array, _ in updates]),
        (),
        [
            pltpu.VMEM((frame_rows, features), current.dtype),
            pltpu.VMEM((frame_rows, features), current.dtype),
            pltpu.VMEM((frame_rows, 3 * width), current.dtype),
            pltpu.VMEM((frame_rows, width), current.dtype),
        ],
        16 * MIB,
        2 * frame_rows * 3 * width * (features + frame_rows),
    )


def join_kernel(keep, first, second, third, fourth, out):
    _, _, plane, y, c = here()
    low = plane % 2
    width = keep.shape[1]

    def put(ref, plane_low, at_y):
        out[:, columns(plane_low * 2 + at_y, width)] = ref[...]

    @pl.when(low == c)
    def _():
        put(keep, low, y)
        put(first, low, 1 - y)
        put(second, 1 - low, y)
        put(third, 1 - low, 1 - y)

    @pl.when(low != c)
    def _():
        put(first, 1 - low, y)
        put(second, low, 1 - y)
        put(third, low, y)
        put(fourth, 1 - low, 1 - y)


def joined(keep, first, second, third, fourth):
    def at_home(p, c):
        return c == p % 2

    first = moved(first, lambda x, p, y, c: (x, p, 1 - y, c) if at_home(p, c) else (x, p ^ 1, y, 1 - c))
    second = moved(second, lambda x, p, y, c: (x, p, 1 - y, 1 - c) if at_home(p, c) else (x, p ^ 1, y, c))
    third = moved(third, lambda x, p, y, c: (x, p, y, 1 - c) if at_home(p, c) else (x, p ^ 1, 1 - y, c))
    fourth = moved(fourth, lambda x, p, y, c: None if at_home(p, c) else (x, p ^ 1, 1 - y, 1 - c))
    rows, width = keep.shape
    return kernel_call(
        join_kernel,
        jax.ShapeDtypeStruct((rows, width * SPATIAL), keep.dtype),
        (keep, first, second, third, fourth),
        (),
        [],
        4 * MIB,
        0,
    )


def paired_planes(
    latent, norm_gain, w_query, w_key, w_value, mem_cache, intersection, counts, slot_of, step_scale
):
    late = late_plane(lax.axis_size("frame"))
    weights, extra, memory = pack(
        w_query, w_key, w_value, intersection, slot_of, counts, step_scale, norm_gain, mem_cache
    )
    extra = moved(extra, lambda x, p, y, c: (x, p, y, 1 - c))
    pieces = all_pieces(*weights)
    tokens = all_tokens(latent)
    keys, values = all_memory(memory)
    extra, current, normed = prepare(extra, tokens)
    part = project(normed, [piece for piece in pieces if piece[1][0][0] < late])
    attended = step(extra, keys, values, normed, part, [piece for piece in pieces if piece[1][0][0] == late])
    updates = [
        (attended, (0, 0)),
        (moved(attended, lambda x, p, y, c: (x, p ^ 1, 1 - y, c)), (1, 1)),
        (moved(attended, lambda x, p, y, c: (x, p ^ 1, y, c)), (1, 0)),
        (moved(attended, lambda x, p, y, c: (x, p, 1 - y, c)), (0, 1)),
    ]
    shares = last_step(extra, keys, values, current, assemble(pieces), updates)
    return joined(*shares)


def fits_paired_planes(latent, norm_gain, w_query, w_key, w_value, mem_cache, *_):
    devices = lax.axis_size("frame")
    planes = devices // SPATIAL
    return (
        lax.axis_size("groups") == 2
        and devices == planes * SPATIAL
        and planes >= 2
        and planes & (planes - 1) == 0
        and w_query.shape[0] % 16 == 0
        and mem_cache.shape[1] == 1
    )


def from_partner(array, axis, bit):
    return lax.ppermute(array, axis, [(i, i ^ 1 << bit) for i in range(lax.axis_size(axis))])


def in_order(mine, theirs, upper, axis_dim):
    low_first = jnp.concatenate([mine, theirs], axis=axis_dim)
    high_first = jnp.concatenate([theirs, mine], axis=axis_dim)
    return jnp.where(upper, high_first, low_first)


def attend(queries, frame_pair, mem_keys, mem_values, live_keys, head_count):
    tok_rows, feature_width = queries.shape
    head_size = feature_width // head_count
    scale_dot = 1.0 / math.sqrt(head_size)
    q_heads = queries.reshape(tok_rows, head_count, head_size)
    k_heads = frame_pair[0].reshape(-1, head_count, head_size)
    v_heads = frame_pair[1].reshape(-1, head_count, head_size)
    frame_scores = (
        jnp.einsum("thd,khd->htk", q_heads, k_heads, preferred_element_type=jnp.float32) * scale_dot
    )
    remote_scores = (
        jnp.einsum("thd,khd->htk", q_heads, mem_keys, preferred_element_type=jnp.float32)
        * scale_dot
    )
    remote_scores = jnp.where(live_keys[None, None, :], remote_scores, -1e30)
    largest = jnp.maximum(
        jnp.max(frame_scores, axis=-1, keepdims=True),
        jnp.max(remote_scores, axis=-1, keepdims=True),
    )
    frame_weights = jnp.exp(frame_scores - largest)
    remote_weights = jnp.exp(remote_scores - largest)
    denominator = jnp.sum(frame_weights, axis=-1) + jnp.sum(remote_weights, axis=-1)
    blended = jnp.einsum(
        "htk,khd->thd",
        frame_weights.astype(jnp.bfloat16),
        v_heads,
        preferred_element_type=jnp.float32,
    )
    blended = blended + jnp.einsum(
        "htk,khd->thd",
        remote_weights.astype(jnp.bfloat16),
        mem_values,
        preferred_element_type=jnp.float32,
    )
    blended = blended / jnp.transpose(denominator)[:, :, None]
    return blended.reshape(tok_rows, feature_width).astype(jnp.bfloat16)


def rms_normed(current, norm_gain):
    widened = current.astype(jnp.float32)
    inverse = lax.rsqrt(jnp.mean(widened * widened, axis=-1, keepdims=True) + 1e-06)
    return (widened, (widened * inverse * norm_gain).astype(jnp.bfloat16))


def separate_frames(
    latent, norm_gain, w_query, w_key, w_value, mem_cache, intersection, counts, slot_of, step_scale
):
    devices = lax.axis_size("frame")
    position = lax.axis_index("frame")
    frame_index = position // SPATIAL
    doublings = SPATIAL.bit_length() - 1
    target_frame = jnp.arange(devices, dtype=jnp.int32) // SPATIAL
    current = latent
    feature_width = latent.shape[1]
    share_width = feature_width // SPATIAL
    head_share = HEADS // SPATIAL

    def column_pieces(weight):
        row_count = weight.shape[0]
        split_cols = jnp.transpose(weight.reshape(row_count, SPATIAL, share_width), (1, 0, 2))
        return jnp.tile(split_cols, (devices // SPATIAL, 1, 1))

    own_query, own_key, own_value = (
        lax.all_to_all(column_pieces(w_query), "frame", split_axis=0, concat_axis=1, tiled=True),
        lax.all_to_all(column_pieces(w_key), "frame", split_axis=0, concat_axis=1, tiled=True),
        lax.all_to_all(column_pieces(w_value), "frame", split_axis=0, concat_axis=1, tiled=True),
    )
    own_query, own_key, own_value = (own_query[0], own_key[0], own_value[0])
    listed = mem_cache[slot_of[intersection[target_frame]]]
    list_len = listed.shape[1]
    local_mem = listed.shape[2]
    grouped = listed.reshape(
        devices // SPATIAL, SPATIAL, list_len, local_mem, 2, SPATIAL, share_width
    )
    diagonal_part = jnp.diagonal(grouped, axis1=1, axis2=5)
    outgoing = jnp.moveaxis(diagonal_part, -1, 1).reshape(
        devices, list_len, local_mem, 2, share_width
    )
    fetched = lax.all_to_all(outgoing, "frame", split_axis=0, concat_axis=2, tiled=True)[0]
    mem_len = fetched.shape[1]
    mem_keys = fetched[:, :, 0, :].reshape(list_len * mem_len, head_share, HS)
    mem_values = fetched[:, :, 1, :].reshape(list_len * mem_len, head_share, HS)
    live_keys = jnp.arange(list_len * mem_len, dtype=jnp.int32) // mem_len < counts[frame_index]
    tok_rows = latent.shape[0]
    for step_index in range(STEPS):
        widened, normed = rms_normed(current, norm_gain)
        gathered = normed
        for bit_index in range(doublings):
            partner = from_partner(gathered, "frame", bit_index)
            gathered = in_order(gathered, partner, position >> bit_index & 1 == 1, 0)
        queries = jnp.dot(gathered, own_query, preferred_element_type=jnp.float32).astype(
            jnp.bfloat16
        )
        keys_frame = jnp.dot(gathered, own_key, preferred_element_type=jnp.float32).astype(
            jnp.bfloat16
        )
        values_frame = jnp.dot(gathered, own_value, preferred_element_type=jnp.float32).astype(
            jnp.bfloat16
        )
        frame_pair = jnp.stack([keys_frame, values_frame])
        attended = attend(queries, frame_pair, mem_keys, mem_values, live_keys, head_share)
        blocks = attended.reshape(SPATIAL, tok_rows, share_width)[:, None]
        for bit_index in range(doublings):
            upper = position >> bit_index & 1 == 1
            dest_count = blocks.shape[0]
            paired = blocks.reshape((dest_count // 2, 2) + blocks.shape[1:])
            kept = jnp.where(upper, paired[:, 1], paired[:, 0])
            sent = jnp.where(upper, paired[:, 0], paired[:, 1])
            arrived = from_partner(sent, "frame", bit_index)
            blocks = in_order(kept, arrived, upper, 1)
        joined = jnp.transpose(blocks[0], (1, 0, 2)).reshape(tok_rows, feature_width)
        current = (widened + step_scale[step_index] * joined.astype(jnp.float32)).astype(
            jnp.bfloat16
        )
    return current


def per_device(*arguments):
    return (paired_planes if fits_paired_planes(*arguments) else separate_frames)(*arguments)


def solution(mesh):
    placed = (
        P(("groups", "frame"), None),
        P(),
        P("frame", None),
        P("frame", None),
        P("frame", None),
        P("groups", "frame", None, None),
        P("groups", None),
        P("groups"),
        P("groups"),
        P(),
    )
    return jax.shard_map(
        per_device,
        mesh=mesh,
        in_specs=placed,
        out_specs=P(("groups", "frame"), None),
        check_vma=False,
    )
```

```python
import functools
import math

import jax
import jax.numpy as jnp
from jax import lax
from jax.experimental import pallas as pl
from jax.experimental.pallas import tpu as pltpu
from jax.sharding import PartitionSpec as P


HEADS = 12
HS = 128
SPATIAL = 4
STEPS = 2
AXES = ("groups", "frame")


def coords(index):
    return index // 4, (index // 2) % 2, index % 2


def quarter_of(plane, y):
    return (plane % 2) * 2 + y


def moved(array, target):
    devices = lax.axis_size("frame")
    pairs = []
    for x in range(lax.axis_size("groups")):
        for index in range(devices):
            place = target(x, *coords(index))
            if place is not None:
                to_x, to_plane, to_y, to_c = place
                pairs.append((x * devices + index, to_x * devices + to_plane * 4 + to_y * 2 + to_c))
    return lax.ppermute(array, AXES, pairs)


def here():
    x = lax.axis_index("groups")
    index = lax.axis_index("frame")
    plane = index // 4
    rest = index - plane * 4
    y = rest // 2
    return x, index, plane, y, rest - y * 2


def flipped(value, bits):
    out = value
    bit = 1
    while bit <= bits:
        if bits & bit:
            out = out + bit - 2 * bit * ((value // bit) % 2)
        bit *= 2
    return out


def joined_bits(one, other):
    return one + other - 2 * one * other


def columns(quarter, width):
    return pl.ds(pl.multiple_of(quarter * width, 128), width)


def pack_weights_kernel(
    w_query, w_key, w_value, own_ref, beside_ref, even_ref, odd_ref, rows, row_sem, out_sem
):
    x, _, plane, y, c = here()
    width = own_ref.shape[1] // 3
    reads = []
    for number, weight in enumerate((w_query, w_key, w_value)):
        reads.append(pltpu.make_async_copy(weight, rows.at[number], row_sem.at[number]))
        reads[-1].start()
    across = joined_bits(joined_bits(x, y), c)
    low = plane % 2
    quarters = (low * 2 + across, (1 - low) * 2 + across, low * 2 + 1 - y, quarter_of(plane, y))
    gives = []
    for number, read in enumerate(reads):
        read.wait()
        for place, (quarter, out) in enumerate(zip(quarters, (even_ref, odd_ref, beside_ref, own_ref))):
            gives.append(
                pltpu.make_async_copy(
                    rows.at[number, :, columns(quarter, width)],
                    out.at[:, pl.ds(number * width, width)],
                    out_sem.at[number, place],
                )
            )
            gives[-1].start()
    for give in gives:
        give.wait()


def pack_weights(w_query, w_key, w_value):
    shard_rows, features = w_query.shape
    piece = jax.ShapeDtypeStruct((shard_rows, 3 * (features // SPATIAL)), w_query.dtype)
    anywhere = pl.BlockSpec(memory_space=pl.ANY)
    held = pl.BlockSpec(memory_space=pltpu.HBM)
    return pl.pallas_call(
        pack_weights_kernel,
        out_shape=(piece,) * 4,
        in_specs=[held] * 3,
        out_specs=(anywhere,) * 4,
        scratch_shapes=[
            pltpu.VMEM((3, shard_rows, features), w_query.dtype),
            pltpu.SemaphoreType.DMA((3,)),
            pltpu.SemaphoreType.DMA((3, 4)),
        ],
        name="pack_weights",
    )(w_query, w_key, w_value)


def pack_memory_kernel(list_hbm, slot_hbm, count_hbm, scale_hbm, gain_hbm, mem_ref, extra_ref, *refs):
    memory_refs = refs[:SPATIAL]
    list_ref, slot_ref, count_ref, scale_ref, gain, stored, extra, scalar_sem, mem_sem, give_sem = refs[SPATIAL:]
    _, index, plane, _, c = here()
    devices = lax.axis_size("frame")
    frames, entries = list_ref.shape
    width = memory_refs[0].shape[-1]
    sources = (list_hbm, slot_hbm, count_hbm, scale_hbm, gain_hbm)
    targets = (list_ref, slot_ref, count_ref, scale_ref, gain)
    scalars = [
        pltpu.make_async_copy(source, target, scalar_sem.at[number])
        for number, (source, target) in enumerate(zip(sources, targets))
    ]
    for copy in scalars:
        copy.start()
    for copy in scalars[:2]:
        copy.wait()
    picks = []
    for frame in range(frames):
        for entry in range(entries):
            number = frame * entries + entry
            row = slot_ref[list_ref[frame, entry]]
            picks.append(pltpu.make_async_copy(mem_ref.at[row, 0], stored.at[number], mem_sem.at[number]))
            picks[-1].start()
    for copy in scalars[2:]:
        copy.wait()
    row = (1, extra.shape[1])
    extra[0:1, :] = gain[...].reshape(row)
    for number in range(STEPS):
        extra[1 + number : 2 + number, :] = jnp.full(row, scale_ref[number], jnp.float32)
    live = lax.broadcasted_iota(jnp.int32, row, 1) % entries < count_ref[(plane // 2) * 2 + 1 - c]
    extra[1 + STEPS : 2 + STEPS, :] = jnp.where(live, 1.0, 0.0)
    gives = [pltpu.make_async_copy(extra, extra_ref, scalar_sem.at[5])]
    gives[-1].start()
    for pick in picks:
        pick.wait()
    for away in range(devices):
        to_plane, to_y, to_c = coords(flipped(index, away))
        to_frame = (to_plane // 2) * 2 + to_c
        place = 0
        for bit in range(2, devices.bit_length() - 1):
            place = place * 2 + (away >> bit & 1)
        gives.append(
            pltpu.make_async_copy(
                stored.at[pl.ds(to_frame * entries, entries), :, columns(quarter_of(to_plane, to_y), width)],
                memory_refs[away % SPATIAL].at[place],
                give_sem.at[away],
            )
        )
        gives[-1].start()
    for give in gives:
        give.wait()


def pack_memory(intersection, slot_of, counts, step_scale, norm_gain, mem_cache):
    devices = lax.axis_size("frame")
    features = mem_cache.shape[-1]
    frames, entries = intersection.shape
    small = jax.ShapeDtypeStruct((2 + STEPS, features), jnp.float32)
    memory = jax.ShapeDtypeStruct((devices // SPATIAL, entries, 2, features // SPATIAL), mem_cache.dtype)
    out_shape = (small,) + (memory,) * SPATIAL
    anywhere = pl.BlockSpec(memory_space=pl.ANY)
    held = pl.BlockSpec(memory_space=pltpu.HBM)
    outs = pl.pallas_call(
        pack_memory_kernel,
        out_shape=out_shape,
        in_specs=[held] * 6,
        out_specs=(anywhere,) * len(out_shape),
        scratch_shapes=[
            pltpu.SMEM(intersection.shape, intersection.dtype),
            pltpu.SMEM(slot_of.shape, slot_of.dtype),
            pltpu.SMEM(counts.shape, counts.dtype),
            pltpu.SMEM(step_scale.shape, step_scale.dtype),
            pltpu.VMEM(norm_gain.shape, norm_gain.dtype),
            pltpu.VMEM((frames * entries, 2, features), mem_cache.dtype),
            pltpu.VMEM(small.shape, small.dtype),
            pltpu.SemaphoreType.DMA((6,)),
            pltpu.SemaphoreType.DMA((frames * entries,)),
            pltpu.SemaphoreType.DMA((devices,)),
        ],
        name="pack_memory",
    )(intersection, slot_of, counts, step_scale, norm_gain, mem_cache)
    return outs[0], outs[1:]


def all_pieces(own, beside, even, odd):
    late = late_plane(lax.axis_size("frame"))

    def direct(bits):
        sent = even if bits % 2 == 0 else odd
        return moved(sent, lambda x, p, y, c: (x, p ^ bits, y ^ x ^ c, c))

    near = moved(beside, lambda x, p, y, c: (x, p, 1 - y, c))
    pieces = [("own", own, [(0, 0, False)]), ("near", near, [(0, 1, False)])]
    early = list(range(1, late))
    for name, bits_list in (("early", early), ("late", [late])):
        if not bits_list:
            continue
        arrays = [direct(bits) for bits in bits_list]
        if len(arrays) > 1:
            arrays = [jnp.concatenate(arrays)]
        pieces.append((name, arrays[0], [(bits, 0, True) for bits in bits_list]))
        crossed = moved(arrays[0], lambda x, p, y, c: (1 - x, p, y, c))
        pieces.append((f"cross_{name}", crossed, [(bits, 1, True) for bits in bits_list]))
    found = [(array, tuple(place + (0,) for place in places)) for _, array, places in pieces]
    for name, array, places in pieces:
        swapped = moved(array, lambda x, p, y, c: (x, p, y, 1 - c))
        found.append((swapped, tuple(place + (1,) for place in places)))
    return found


def all_memory(parts):
    devices = lax.axis_size("frame")
    near = [parts[0]] + [hop(part, place) for place, part in enumerate(parts) if place]
    held = jnp.stack(near)
    for bit in range(2, devices.bit_length() - 1):
        half = held.shape[1] // 2
        arrived = hop(held[:, half:], 1 << bit)
        held = jnp.concatenate([held[:, :half], arrived])
    keys, values = held[:, 0, :, 0, :], held[:, 0, :, 1, :]
    return keys.reshape(-1, keys.shape[-1]), values.reshape(-1, values.shape[-1])


def hop(array, bits):
    return lax.ppermute(array, "frame", [(i, i ^ bits) for i in range(lax.axis_size("frame"))])


def all_tokens(latent):
    def swapped(array):
        return moved(array, lambda x, p, y, c: (x, p, y, 1 - c))

    far = moved(latent, lambda x, p, y, c: (x, p ^ 1, y, c))
    near = moved(latent, lambda x, p, y, c: (x, p, 1 - y, c))
    far_near = moved(far, lambda x, p, y, c: (x, p, 1 - y, c))
    home = (latent, near, swapped(latent), swapped(near))
    return home + (far, far_near, swapped(far), swapped(far_near))


def late_plane(devices):
    return devices // 4 - 1


def piece_start(place, shard_rows, plane_number):
    x, _, _, y, c = here()
    _, y_bits, with_x, c_bits = place
    from_y, from_c = flipped(y, y_bits), flipped(c, c_bits)
    if with_x:
        from_y = joined_bits(joined_bits(from_y, x), from_c)
    return pl.multiple_of((plane_number * 4 + from_y * 2 + from_c) * shard_rows, 16)


def gather_pieces(piece_refs, places, first_plane, weights):
    for ref, shards in zip(piece_refs, places):
        rows = ref.shape[0] // len(shards)
        for number, place in enumerate(shards):
            start = piece_start(place, rows, place[0] - first_plane)
            weights[pl.ds(start, rows), :] = ref[number * rows : (number + 1) * rows, :]


def store_normed(current, rows, inverse, gain_ref, normed):
    _, _, plane, _, _ = here()
    planes = lax.axis_size("frame") // 4
    span = current.shape[1] // planes
    for bits in range(planes):
        spot = columns(flipped(plane, bits), span)
        widened = current[rows, spot].astype(jnp.float32)
        normed[rows, bits * span : (bits + 1) * span] = (widened * inverse * gain_ref[0:1, spot]).astype(normed.dtype)


BLOCK = 32
ATTENTION_BLOCKS = 1


def prepare_kernel(extra_ref, *refs):
    token_refs, (extra, current, normed) = refs[:8], refs[8:]
    _, _, plane, y, c = here()
    rows = token_refs[0].shape[0]
    extra[...] = extra_ref[...]
    bases = [at_y * 2 * rows + core * rows for core in (0, 1) for at_y in (y, 1 - y)]

    def fill(refs):
        @pl.loop(0, rows // BLOCK)
        def _(number):
            for ref, base in zip(refs, bases):
                tokens = ref[pl.ds(pl.multiple_of(number * BLOCK, BLOCK), BLOCK), :]
                spot = pl.ds(pl.multiple_of(base + number * BLOCK, BLOCK), BLOCK)
                current[spot, :] = tokens
                widened = tokens.astype(jnp.float32)
                inverse = lax.rsqrt(jnp.mean(widened * widened, axis=-1, keepdims=True) + 1e-06)
                store_normed(current, spot, inverse, extra, normed)

    pl.when(plane % 2 == c)(lambda: fill(token_refs[:4]))
    pl.when(plane % 2 != c)(lambda: fill(token_refs[4:]))


def project_kernel(places, *refs):
    normed = refs[0]
    piece_refs = refs[1 : 1 + len(places)]
    out, weights = refs[1 + len(places) :]
    gather_pieces(piece_refs, places, 0, weights)
    out[...] = jnp.dot(normed[:, : weights.shape[0]], weights[...], preferred_element_type=jnp.float32)


def assemble_kernel(places, *refs):
    gather_pieces(refs[:-1], places, 0, refs[-1])


def attend_heads(projected, key_ref, value_ref, extra_ref, attended, head_count):
    width = projected.shape[1] // 3
    head_size = width // head_count
    scale_dot = 1.0 / math.sqrt(head_size)
    mem_rows = key_ref.shape[0]
    live = extra_ref[3:4, :mem_rows] > 0.5
    contract_last = (((1,), (1,)), ((), ()))
    frame_rows = projected.shape[0]
    half = frame_rows // ATTENTION_BLOCKS
    for head in range(head_count):
        span = slice(head * head_size, (head + 1) * head_size)
        keys = projected[:, width + head * head_size : width + (head + 1) * head_size]
        values = projected[:, 2 * width + head * head_size : 2 * width + (head + 1) * head_size]
        for start in range(0, frame_rows, half):
            queries = projected[start : start + half, span]
            frame_scores = (
                lax.dot_general(queries, keys, contract_last, preferred_element_type=jnp.float32) * scale_dot
            )
            mem_scores = (
                lax.dot_general(queries, key_ref[:, span], contract_last, preferred_element_type=jnp.float32)
                * scale_dot
            )
            scores = jnp.concatenate([frame_scores, jnp.where(live, mem_scores, -1e30)], axis=1)
            weights = jnp.exp(scores - jnp.max(scores, axis=-1, keepdims=True))
            denominator = jnp.sum(weights, axis=-1, keepdims=True)
            rounded = weights.astype(jnp.bfloat16)
            blended = jnp.dot(
                rounded[:, :frame_rows], values, preferred_element_type=jnp.float32
            ) + jnp.dot(rounded[:, frame_rows:], value_ref[:, span], preferred_element_type=jnp.float32)
            attended[start : start + half, span] = (blended / denominator).astype(attended.dtype)


def step_kernel(places, first_plane, head_count, extra_ref, key_ref, value_ref, normed, part_ref, *refs):
    piece_refs = refs[: len(places)]
    attended, weights, projected = refs[len(places) :]
    gather_pieces(piece_refs, places, first_plane, weights)
    early = normed.shape[1] - weights.shape[0]
    projected[...] = (
        part_ref[...] + jnp.dot(normed[:, early:], weights[...], preferred_element_type=jnp.float32)
    ).astype(projected.dtype)
    attend_heads(projected, key_ref, value_ref, extra_ref, attended, head_count)


def last_step_kernel(
    update_places, head_count, extra_ref, key_ref, value_ref, current_ref, weights, first_part, second_part, third_part,
    fourth_part, keep, first, second, third, fourth, current, normed, projected, attended,
):
    _, _, plane, y, c = here()
    width = first_part.shape[1]
    at_home = plane % 2 == c

    @pl.loop(0, current.shape[0] // BLOCK)
    def _(number):
        rows = pl.ds(pl.multiple_of(number * BLOCK, BLOCK), BLOCK)
        total = jnp.zeros((BLOCK, 1), jnp.float32)
        for part, (plane_bits, y_bits) in zip((first_part, second_part, third_part, fourth_part), update_places):
            spot = columns(quarter_of(flipped(plane, plane_bits), flipped(y, y_bits)), width)
            updated = (
                current_ref[rows, spot].astype(jnp.float32)
                + extra_ref[1:2, :width] * part[rows, :].astype(jnp.float32)
            ).astype(current.dtype)
            current[rows, spot] = updated
            widened = updated.astype(jnp.float32)
            total = total + jnp.sum(widened * widened, axis=-1, keepdims=True)
        inverse = lax.rsqrt(total / current.shape[1] + 1e-06)
        store_normed(current, rows, inverse, extra_ref, normed)

    projected[...] = jnp.dot(normed[...], weights[...], preferred_element_type=jnp.float32).astype(projected.dtype)
    attend_heads(projected, key_ref, value_ref, extra_ref, attended, head_count)
    spot = columns(quarter_of(plane, y), width)
    attended[...] = (
        current[:, spot].astype(jnp.float32) + extra_ref[2:3, :width] * attended[...].astype(jnp.float32)
    ).astype(attended.dtype)
    chip_rows = attended.shape[0] // 2
    rows = chip_rows // 2
    here_rows, there_rows = y * chip_rows, (1 - y) * chip_rows

    def part(start):
        return attended[pl.ds(pl.multiple_of(start, rows), rows), :]

    keep[...] = part(here_rows)
    fourth[...] = part(there_rows + rows)

    @pl.when(at_home)
    def _():
        first[...] = part(there_rows)
        second[...] = part(there_rows + rows)
        third[...] = part(here_rows + rows)

    @pl.when(jnp.logical_not(at_home))
    def _():
        first[...] = part(here_rows + rows)
        second[...] = part(here_rows)
        third[...] = part(there_rows)


MIB = 1024 * 1024


def kernel_call(kernel, out_shape, operands, anywhere, scratch_shapes, limit, flops):
    vectors = pl.BlockSpec(memory_space=pltpu.VMEM)
    free = pl.BlockSpec(memory_space=pl.ANY)
    moved_bytes = sum(operand.size * operand.dtype.itemsize for operand in operands)
    return pl.pallas_call(
        kernel,
        out_shape=out_shape,
        in_specs=[free if number in anywhere else vectors for number in range(len(operands))],
        out_specs=jax.tree.map(lambda _: vectors, out_shape),
        scratch_shapes=scratch_shapes,
        compiler_params=pltpu.CompilerParams(vmem_limit_bytes=limit),
        cost_estimate=pl.CostEstimate(flops=flops, transcendentals=0, bytes_accessed=moved_bytes),
    )(*operands)


def prepare(extra, tokens):
    frame = jax.ShapeDtypeStruct((4 * tokens[0].shape[0], tokens[0].shape[1]), tokens[0].dtype)
    return kernel_call(
        prepare_kernel,
        (jax.ShapeDtypeStruct(extra.shape, extra.dtype), frame, frame),
        (extra, *tokens),
        (),
        [],
        8 * MIB,
        0,
    )


def project(normed, pieces):
    width = pieces[0][0].shape[1]
    depth = sum(array.shape[0] for array, _ in pieces)
    return kernel_call(
        functools.partial(project_kernel, tuple(place for _, place in pieces)),
        jax.ShapeDtypeStruct((normed.shape[0], width), jnp.float32),
        (normed, *[array for array, _ in pieces]),
        (),
        [pltpu.VMEM((depth, width), normed.dtype)],
        16 * MIB,
        2 * normed.shape[0] * depth * width,
    )


def assemble(pieces):
    width = pieces[0][0].shape[1]
    depth = sum(array.shape[0] for array, _ in pieces)
    return kernel_call(
        functools.partial(assemble_kernel, tuple(place for _, place in pieces)),
        jax.ShapeDtypeStruct((depth, width), pieces[0][0].dtype),
        [array for array, _ in pieces],
        (),
        [],
        8 * MIB,
        0,
    )


def step(extra, keys, values, normed, part, pieces):
    width = pieces[0][0].shape[1]
    depth = sum(array.shape[0] for array, _ in pieces)
    frame_rows = normed.shape[0]
    return kernel_call(
        functools.partial(step_kernel, tuple(place for _, place in pieces), pieces[0][1][0][0], HEADS // SPATIAL),
        jax.ShapeDtypeStruct((frame_rows, width // 3), normed.dtype),
        (extra, keys, values, normed, part, *[array for array, _ in pieces]),
        (),
        [pltpu.VMEM((depth, width), normed.dtype), pltpu.VMEM((frame_rows, width), normed.dtype)],
        16 * MIB,
        2 * frame_rows * width * (depth + frame_rows),
    )


def last_step(extra, keys, values, current, weights, updates):
    frame_rows, features = current.shape
    width = weights.shape[1] // 3
    share = jax.ShapeDtypeStruct((frame_rows // 4, width), current.dtype)
    return kernel_call(
        functools.partial(last_step_kernel, tuple(place for _, place in updates), HEADS // SPATIAL),
        (share,) * 5,
        (extra, keys, values, current, weights, *[array for array, _ in updates]),
        (),
        [
            pltpu.VMEM((frame_rows, features), current.dtype),
            pltpu.VMEM((frame_rows, features), current.dtype),
            pltpu.VMEM((frame_rows, 3 * width), current.dtype),
            pltpu.VMEM((frame_rows, width), current.dtype),
        ],
        16 * MIB,
        2 * frame_rows * 3 * width * (features + frame_rows),
    )


def join_kernel(keep, first, second, third, fourth, out):
    _, _, plane, y, c = here()
    low = plane % 2
    width = keep.shape[1]

    def put(ref, plane_low, at_y):
        out[:, columns(plane_low * 2 + at_y, width)] = ref[...]

    @pl.when(low == c)
    def _():
        put(keep, low, y)
        put(first, low, 1 - y)
        put(second, 1 - low, y)
        put(third, 1 - low, 1 - y)

    @pl.when(low != c)
    def _():
        put(first, 1 - low, y)
        put(second, low, 1 - y)
        put(third, low, y)
        put(fourth, 1 - low, 1 - y)


def joined(keep, first, second, third, fourth):
    def at_home(p, c):
        return c == p % 2

    first = moved(first, lambda x, p, y, c: (x, p, 1 - y, c) if at_home(p, c) else (x, p ^ 1, y, 1 - c))
    second = moved(second, lambda x, p, y, c: (x, p, 1 - y, 1 - c) if at_home(p, c) else (x, p ^ 1, y, c))
    third = moved(third, lambda x, p, y, c: (x, p, y, 1 - c) if at_home(p, c) else (x, p ^ 1, 1 - y, c))
    fourth = moved(fourth, lambda x, p, y, c: None if at_home(p, c) else (x, p ^ 1, 1 - y, 1 - c))
    rows, width = keep.shape
    return kernel_call(
        join_kernel,
        jax.ShapeDtypeStruct((rows, width * SPATIAL), keep.dtype),
        (keep, first, second, third, fourth),
        (),
        [],
        4 * MIB,
        0,
    )


def paired_planes(
    latent, norm_gain, w_query, w_key, w_value, mem_cache, intersection, counts, slot_of, step_scale
):
    late = late_plane(lax.axis_size("frame"))
    weights = pack_weights(w_query, w_key, w_value)
    extra, memory = pack_memory(intersection, slot_of, counts, step_scale, norm_gain, mem_cache)
    extra = moved(extra, lambda x, p, y, c: (x, p, y, 1 - c))
    pieces = all_pieces(*weights)
    tokens = all_tokens(latent)
    keys, values = all_memory(memory)
    extra, current, normed = prepare(extra, tokens)
    part = project(normed, [piece for piece in pieces if piece[1][0][0] < late])
    attended = step(extra, keys, values, normed, part, [piece for piece in pieces if piece[1][0][0] == late])
    updates = [
        (attended, (0, 0)),
        (moved(attended, lambda x, p, y, c: (x, p ^ 1, 1 - y, c)), (1, 1)),
        (moved(attended, lambda x, p, y, c: (x, p ^ 1, y, c)), (1, 0)),
        (moved(attended, lambda x, p, y, c: (x, p, 1 - y, c)), (0, 1)),
    ]
    shares = last_step(extra, keys, values, current, assemble(pieces), updates)
    return joined(*shares)


def fits_paired_planes(latent, norm_gain, w_query, w_key, w_value, mem_cache, *_):
    devices = lax.axis_size("frame")
    planes = devices // SPATIAL
    return (
        lax.axis_size("groups") == 2
        and devices == planes * SPATIAL
        and planes >= 2
        and planes & (planes - 1) == 0
        and w_query.shape[0] % 16 == 0
        and mem_cache.shape[1] == 1
    )


def from_partner(array, axis, bit):
    return lax.ppermute(array, axis, [(i, i ^ 1 << bit) for i in range(lax.axis_size(axis))])


def in_order(mine, theirs, upper, axis_dim):
    low_first = jnp.concatenate([mine, theirs], axis=axis_dim)
    high_first = jnp.concatenate([theirs, mine], axis=axis_dim)
    return jnp.where(upper, high_first, low_first)


def attend(queries, frame_pair, mem_keys, mem_values, live_keys, head_count):
    tok_rows, feature_width = queries.shape
    head_size = feature_width // head_count
    scale_dot = 1.0 / math.sqrt(head_size)
    q_heads = queries.reshape(tok_rows, head_count, head_size)
    k_heads = frame_pair[0].reshape(-1, head_count, head_size)
    v_heads = frame_pair[1].reshape(-1, head_count, head_size)
    frame_scores = (
        jnp.einsum("thd,khd->htk", q_heads, k_heads, preferred_element_type=jnp.float32) * scale_dot
    )
    remote_scores = (
        jnp.einsum("thd,khd->htk", q_heads, mem_keys, preferred_element_type=jnp.float32)
        * scale_dot
    )
    remote_scores = jnp.where(live_keys[None, None, :], remote_scores, -1e30)
    largest = jnp.maximum(
        jnp.max(frame_scores, axis=-1, keepdims=True),
        jnp.max(remote_scores, axis=-1, keepdims=True),
    )
    frame_weights = jnp.exp(frame_scores - largest)
    remote_weights = jnp.exp(remote_scores - largest)
    denominator = jnp.sum(frame_weights, axis=-1) + jnp.sum(remote_weights, axis=-1)
    blended = jnp.einsum(
        "htk,khd->thd",
        frame_weights.astype(jnp.bfloat16),
        v_heads,
        preferred_element_type=jnp.float32,
    )
    blended = blended + jnp.einsum(
        "htk,khd->thd",
        remote_weights.astype(jnp.bfloat16),
        mem_values,
        preferred_element_type=jnp.float32,
    )
    blended = blended / jnp.transpose(denominator)[:, :, None]
    return blended.reshape(tok_rows, feature_width).astype(jnp.bfloat16)


def rms_normed(current, norm_gain):
    widened = current.astype(jnp.float32)
    inverse = lax.rsqrt(jnp.mean(widened * widened, axis=-1, keepdims=True) + 1e-06)
    return (widened, (widened * inverse * norm_gain).astype(jnp.bfloat16))


def separate_frames(
    latent, norm_gain, w_query, w_key, w_value, mem_cache, intersection, counts, slot_of, step_scale
):
    devices = lax.axis_size("frame")
    position = lax.axis_index("frame")
    frame_index = position // SPATIAL
    doublings = SPATIAL.bit_length() - 1
    target_frame = jnp.arange(devices, dtype=jnp.int32) // SPATIAL
    current = latent
    feature_width = latent.shape[1]
    share_width = feature_width // SPATIAL
    head_share = HEADS // SPATIAL

    def column_pieces(weight):
        row_count = weight.shape[0]
        split_cols = jnp.transpose(weight.reshape(row_count, SPATIAL, share_width), (1, 0, 2))
        return jnp.tile(split_cols, (devices // SPATIAL, 1, 1))

    own_query, own_key, own_value = (
        lax.all_to_all(column_pieces(w_query), "frame", split_axis=0, concat_axis=1, tiled=True),
        lax.all_to_all(column_pieces(w_key), "frame", split_axis=0, concat_axis=1, tiled=True),
        lax.all_to_all(column_pieces(w_value), "frame", split_axis=0, concat_axis=1, tiled=True),
    )
    own_query, own_key, own_value = (own_query[0], own_key[0], own_value[0])
    listed = mem_cache[slot_of[intersection[target_frame]]]
    list_len = listed.shape[1]
    local_mem = listed.shape[2]
    grouped = listed.reshape(
        devices // SPATIAL, SPATIAL, list_len, local_mem, 2, SPATIAL, share_width
    )
    diagonal_part = jnp.diagonal(grouped, axis1=1, axis2=5)
    outgoing = jnp.moveaxis(diagonal_part, -1, 1).reshape(
        devices, list_len, local_mem, 2, share_width
    )
    fetched = lax.all_to_all(outgoing, "frame", split_axis=0, concat_axis=2, tiled=True)[0]
    mem_len = fetched.shape[1]
    mem_keys = fetched[:, :, 0, :].reshape(list_len * mem_len, head_share, HS)
    mem_values = fetched[:, :, 1, :].reshape(list_len * mem_len, head_share, HS)
    live_keys = jnp.arange(list_len * mem_len, dtype=jnp.int32) // mem_len < counts[frame_index]
    tok_rows = latent.shape[0]
    for step_index in range(STEPS):
        widened, normed = rms_normed(current, norm_gain)
        gathered = normed
        for bit_index in range(doublings):
            partner = from_partner(gathered, "frame", bit_index)
            gathered = in_order(gathered, partner, position >> bit_index & 1 == 1, 0)
        queries = jnp.dot(gathered, own_query, preferred_element_type=jnp.float32).astype(
            jnp.bfloat16
        )
        keys_frame = jnp.dot(gathered, own_key, preferred_element_type=jnp.float32).astype(
            jnp.bfloat16
        )
        values_frame = jnp.dot(gathered, own_value, preferred_element_type=jnp.float32).astype(
            jnp.bfloat16
        )
        frame_pair = jnp.stack([keys_frame, values_frame])
        attended = attend(queries, frame_pair, mem_keys, mem_values, live_keys, head_share)
        blocks = attended.reshape(SPATIAL, tok_rows, share_width)[:, None]
        for bit_index in range(doublings):
            upper = position >> bit_index & 1 == 1
            dest_count = blocks.shape[0]
            paired = blocks.reshape((dest_count // 2, 2) + blocks.shape[1:])
            kept = jnp.where(upper, paired[:, 1], paired[:, 0])
            sent = jnp.where(upper, paired[:, 0], paired[:, 1])
            arrived = from_partner(sent, "frame", bit_index)
            blocks = in_order(kept, arrived, upper, 1)
        joined = jnp.transpose(blocks[0], (1, 0, 2)).reshape(tok_rows, feature_width)
        current = (widened + step_scale[step_index] * joined.astype(jnp.float32)).astype(
            jnp.bfloat16
        )
    return current


def per_device(*arguments):
    return (paired_planes if fits_paired_planes(*arguments) else separate_frames)(*arguments)


def solution(mesh):
    placed = (
        P(("groups", "frame"), None),
        P(),
        P("frame", None),
        P("frame", None),
        P("frame", None),
        P("groups", "frame", None, None),
        P("groups", None),
        P("groups"),
        P("groups"),
        P(),
    )
    return jax.shard_map(
        per_device,
        mesh=mesh,
        in_specs=placed,
        out_specs=P(("groups", "frame"), None),
        check_vma=False,
    )
```
